32 devices in a mesh: fsdp: 16 (over z, y, core), seq: 2 (over x).
Axes of the slice: x: 2, y: 2, z: 4, core: 2. Of those that a mesh axis runs over, the one named last changes fastest.
Arguments:
- inputs: bfloat16 [16, 2048, 1024], P('fsdp', 'seq'), may hold values from -6 to 6
- cotangent: bfloat16 [16, 2048, 1024], P('fsdp', 'seq'), may hold values from -6 to 6
- lengths: int32 [16, 16], P('fsdp'), may hold values from 1 to 1024, 2048 in all within a row
- norm_gains: float32 [2, 1024], replicated, may hold values from 0.5 to 1.5
- norm_first: float32 [2, 1024], replicated, may hold values from -128 to 128
- norm_second: float32 [2, 1024], replicated, may hold values from 851.968 to 13762.56
- qk_gains: float32 [2, 64], replicated, may hold values from 0.5 to 1.5
- qk_first: float32 [2, 64], replicated, may hold values from -256 to 256
- qk_second: float32 [2, 64], replicated, may hold values from 3276.8 to 55705.6
- qkv_master: float32 [1024, 2048], P(('fsdp', 'seq')), may hold values from -0.1875 to 0.1875
- qkv_first: float32 [1024, 2048], P(('fsdp', 'seq')), may hold values from -128 to 128
- qkv_second: float32 [1024, 2048], P(('fsdp', 'seq')), may hold values from 851.968 to 13762.56
- out_master: float32 [1024, 1024], P(('fsdp', 'seq')), may hold values from -0.75 to 0.75
- out_first: float32 [1024, 1024], P(('fsdp', 'seq')), may hold values from -32 to 32
- out_second: float32 [1024, 1024], P(('fsdp', 'seq')), may hold values from 78.6432 to 1245.184
- gate_up_master: float32 [1024, 9216], P(('fsdp', 'seq')), may hold values from -0.1875 to 0.1875
- gate_up_first: float32 [1024, 9216], P(('fsdp', 'seq')), may hold values from -32 to 32
- gate_up_second: float32 [1024, 9216], P(('fsdp', 'seq')), may hold values from 78.6432 to 1245.184
- down_master: float32 [4608, 1024], P(('fsdp', 'seq')), may hold values from -0.09375 to 0.09375
- down_first: float32 [4608, 1024], P(('fsdp', 'seq')), may hold values from -64 to 64
- down_second: float32 [4608, 1024], P(('fsdp', 'seq')), may hold values from 311.296 to 4915.2
Outputs:
- outputs: bfloat16 [16, 2048, 1024], P('fsdp', 'seq')
- input_grad: float32 [16, 2048, 1024], P('fsdp', 'seq')
- new_norm_gains: float32 [2, 1024], replicated
- new_norm_first: float32 [2, 1024], replicated
- new_norm_second: float32 [2, 1024], replicated
- new_qk_gains: float32 [2, 64], replicated
- new_qk_first: float32 [2, 64], replicated
- new_qk_second: float32 [2, 64], replicated
- new_qkv: float32 [1024, 2048], P(('fsdp', 'seq'))
- new_qkv_first: float32 [1024, 2048], P(('fsdp', 'seq'))
- new_qkv_second: float32 [1024, 2048], P(('fsdp', 'seq'))
- new_out: float32 [1024, 1024], P(('fsdp', 'seq'))
- new_out_first: float32 [1024, 1024], P(('fsdp', 'seq'))
- new_out_second: float32 [1024, 1024], P(('fsdp', 'seq'))
- new_gate_up: float32 [1024, 9216], P(('fsdp', 'seq'))
- new_gate_up_first: float32 [1024, 9216], P(('fsdp', 'seq'))
- new_gate_up_second: float32 [1024, 9216], P(('fsdp', 'seq'))
- new_down: float32 [4608, 1024], P(('fsdp', 'seq'))
- new_down_first: float32 [4608, 1024], P(('fsdp', 'seq'))
- new_down_second: float32 [4608, 1024], P(('fsdp', 'seq'))
The draws below stay inside these ranges and needn't reach their ends.
Inputs may be any that keep to these rules, and one draw needn't show every extreme that they name: The 16 lengths of a row sum to 2048 and one of them is 1024.
All inputs are finite; a program needn't handle non-finite values.
Results may differ from the reference program's by a relative error of at most 0.018.
Values may be sent and summed in bfloat16 or wider, within the bound.
A program may use at most 256 MiB of HBM per device.

```python
import math
import jax
import jax.numpy as jnp
import numpy as np
from jax import lax

D = 1024
HQ = 16
KEY_VALUE_HEADS = 8
HEAD_SIZE = 64
FF = 4608
QUERY_FEATURES = 1024
KEY_FEATURES = 512
GROUP_WIDTH = 2
NDOC = 16
BLOCK_SPAN = 512
STEP = 10
SEQLEN = 2048
ROWS = 16
TOKENS = 32768


def levels(key, shape, pieces, least, largest):
    def one(axis_at, shards_of):
        steps = jax.random.uniform(jax.random.fold_in(jax.random.fold_in(key, 6), axis_at), (shards_of,), jnp.float32, least / len(pieces), largest / len(pieces))
        return jnp.repeat(jnp.exp(steps), shape[axis_at] // shards_of).reshape((-1,) + (1,) * (len(shape) - axis_at - 1))

    gain = one(*pieces[0])
    for cut in pieces[1:]:
        gain = gain * one(*cut)
    return gain


def profile(count, total, limit, lean):
    loads = [(1 << 20) // math.isqrt(standing ** lean) + 1 for standing in range(2, count + 1)]
    spare, given = total - limit - (count - 1), [1] * (count - 1)
    while spare > 0:
        candidates = [i for i in range(count - 1) if given[i] < limit]
        pool, budget = sum([loads[i] for i in candidates]), spare
        for i in candidates:
            extra = min(limit - given[i], max(1, budget * loads[i] // pool), spare)
            given[i] = given[i] + extra
            spare = spare - extra
    return np.array([limit] + given)


def uneven(key, number_of, total, limit, skew):
    if number_of == 2:
        one = jax.random.randint(key, (), max(1, total - limit), min(limit, total - 1) + 1)
        return jnp.stack([one, total - one])
    tallies = jnp.asarray(profile(number_of, total, limit, skew), jnp.int32)
    pairs = (number_of - 1) // 2
    donor, taker = tallies[1:1 + 2 * pairs:2], tallies[2:2 + 2 * pairs:2]
    slack = jnp.minimum(donor - 1, limit - taker)
    shifted = jax.random.randint(jax.random.fold_in(key, 1), (pairs,), 0, 1 << 20) % (slack + 1)
    tallies = tallies.at[1:1 + 2 * pairs:2].set(donor - shifted).at[2:2 + 2 * pairs:2].set(taker + shifted)
    return tallies[jax.random.permutation(jax.random.fold_in(key, 2), number_of)]


def scatter_about(stream_key, extent, width, reach, pieces=(), kind=jnp.bfloat16):
    gain = levels(stream_key, extent, pieces, -0.22, 0.18) if pieces else 1.0
    values = jax.random.normal(stream_key, extent, jnp.float32) * width * gain
    return jnp.minimum(jnp.maximum(values, -reach), reach).astype(kind)


def setup_inputs(seed: int = 0) -> dict:
    seeds = jax.random.split(jax.random.key(seed), 22)
    return {
        "inputs": scatter_about(seeds[0], (ROWS, SEQLEN, D), 1.0, 6.0, ((0, 16), (1, 2))),
        "cotangent": scatter_about(seeds[1], (ROWS, SEQLEN, D), 1.0, 6.0, ((0, 16), (1, 2))),
        "lengths": jax.vmap(lambda own: uneven(own, NDOC, SEQLEN, SEQLEN // 2, 2))(jax.random.split(seeds[2], ROWS)).reshape((ROWS, NDOC)).astype(jnp.int32),
        "norm_gains": jnp.clip(1.0 + 0.1 * jax.random.normal(seeds[3], (2, D), jnp.float32), 0.5, 1.5),
        "norm_first": scatter_about(seeds[4], (2, D), (0.11 * TOKENS ** 0.5), 128.0, (), jnp.float32),
        "norm_second": jnp.clip(jnp.exp(jax.random.uniform(seeds[5], (2, D), jnp.float32, math.log(851.968), math.log(13762.56))), 851.968, 13762.56),
        "qk_gains": jnp.clip(1.0 + 0.1 * jax.random.normal(seeds[6], (2, HEAD_SIZE), jnp.float32), 0.5, 1.5),
        "qk_first": scatter_about(seeds[7], (2, HEAD_SIZE), (0.22 * TOKENS ** 0.5), 256.0, (), jnp.float32),
        "qk_second": jnp.clip(jnp.exp(jax.random.uniform(seeds[8], (2, HEAD_SIZE), jnp.float32, math.log(3276.8), math.log(55705.6))), 3276.8, 55705.6),
        "qkv_master": scatter_about(seeds[9], (D, QUERY_FEATURES + 2 * KEY_FEATURES), D ** -0.5, 0.1875, ((0, 32),), jnp.float32),
        "qkv_first": scatter_about(seeds[10], (D, QUERY_FEATURES + 2 * KEY_FEATURES), (0.11 * TOKENS ** 0.5), 128.0, ((0, 32),), jnp.float32),
        "qkv_second": jnp.clip(jnp.exp(math.log(13762.56) - 2.7821581 * jax.random.uniform(seeds[11], (D, QUERY_FEATURES + 2 * KEY_FEATURES), jnp.float32) ** levels(seeds[11], (D, QUERY_FEATURES + 2 * KEY_FEATURES), ((0, 32),), -0.2, 0.2)), 851.968, 13762.56),
        "out_master": scatter_about(seeds[12], (QUERY_FEATURES, D), (QUERY_FEATURES // 16) ** -0.5, 0.75, ((0, 32),), jnp.float32),
        "out_first": scatter_about(seeds[13], (QUERY_FEATURES, D), (0.033 * TOKENS ** 0.5), 32.0, ((0, 32),), jnp.float32),
        "out_second": jnp.clip(jnp.exp(math.log(1245.184) - 2.7621173 * jax.random.uniform(seeds[14], (QUERY_FEATURES, D), jnp.float32) ** levels(seeds[14], (QUERY_FEATURES, D), ((0, 32),), -0.2, 0.2)), 78.6432, 1245.184),
        "gate_up_master": scatter_about(seeds[15], (D, 2 * FF), D ** -0.5, 0.1875, ((0, 32),), jnp.float32),
        "gate_up_first": scatter_about(seeds[16], (D, 2 * FF), (0.033 * TOKENS ** 0.5), 32.0, ((0, 32),), jnp.float32),
        "gate_up_second": jnp.clip(jnp.exp(math.log(1245.184) - 2.7621173 * jax.random.uniform(seeds[17], (D, 2 * FF), jnp.float32) ** levels(seeds[17], (D, 2 * FF), ((0, 32),), -0.2, 0.2)), 78.6432, 1245.184),
        "down_master": scatter_about(seeds[18], (FF, D), FF ** -0.5, 0.09375, ((0, 32),), jnp.float32),
        "down_first": scatter_about(seeds[19], (FF, D), (0.066 * TOKENS ** 0.5), 64.0, ((0, 32),), jnp.float32),
        "down_second": jnp.clip(jnp.exp(math.log(4915.2) - 2.7593436 * jax.random.uniform(seeds[20], (FF, D), jnp.float32) ** levels(seeds[20], (FF, D), ((0, 32),), -0.2, 0.2)), 311.296, 4915.2),
    }


NORM_EPS = 1e-05
ROPE_BASE = 1000000.0
BETA_ONE = 0.9
BETA_TWO = 0.95
ADAM_EPS = 1e-08
DECAY_RATE = 0.1
GAIN_RATE = 0.3
MASKED_FILL = -1e+30

@jax.custom_vjp
def low(v):
    return lax.optimization_barrier(v.astype(jnp.bfloat16)).astype(jnp.float32)

@jax.custom_vjp
def low_back(v):
    return v

def low_keep(v):
    return (low(v), None)

def low_pass(kept, grad):
    return (grad,)

def back_keep(v):
    return (v, None)

def back_low(kept, grad):
    return (low(grad),)
low.defvjp(low_keep, low_pass)
low_back.defvjp(back_keep, back_low)

def matmul(left_side, right_side):
    return jnp.dot(left_side, right_side, precision=lax.Precision.HIGHEST, preferred_element_type=jnp.float32)

def rms_norm(values_in, gain_row):
    scale_row = lax.rsqrt(lax.optimization_barrier(jnp.mean(values_in * values_in, axis=-1, keepdims=True)) + NORM_EPS)
    return values_in * scale_row * gain_row

def doc_layout(row_lengths, places):
    doc_ends = jnp.cumsum(row_lengths).astype(jnp.int32)
    passed = doc_ends[None, :] <= places[:, None]
    segment = lax.optimization_barrier(jnp.sum(passed.astype(jnp.int32), axis=1)).astype(jnp.int32)
    begins = lax.optimization_barrier(jnp.sum(jnp.where(passed, row_lengths[None, :], 0), axis=1)).astype(jnp.int32)
    return (segment, (places - begins).astype(jnp.int32))

def rotate(values_in, position):
    half_width = values_in.shape[-1] // 2
    index_row = jnp.arange(half_width, dtype=jnp.float32)
    frequency = jnp.exp(index_row * (-2.0 * math.log(ROPE_BASE) / values_in.shape[-1]))
    angles = position.astype(jnp.float32)[:, None] * frequency[None, :]
    cosine = jnp.cos(angles)[:, None, :]
    sine_row = jnp.sin(angles)[:, None, :]
    front_half = values_in[..., :half_width]
    back_half = values_in[..., half_width:]
    return jnp.concatenate([front_half * cosine - back_half * sine_row, back_half * cosine + front_half * sine_row], axis=-1)

def attend(query_matrix, keys_in, values_in, segment):
    row_count_total = query_matrix.shape[0]
    places = jnp.arange(row_count_total, dtype=jnp.int32)
    scale_factor = HEAD_SIZE ** (-0.5)

    def one_block(block_offset):
        query_block_rows = lax.dynamic_slice_in_dim(query_matrix, block_offset, BLOCK_SPAN, 0).reshape(BLOCK_SPAN, KEY_VALUE_HEADS, GROUP_WIDTH, HEAD_SIZE)
        block_segment = lax.dynamic_slice_in_dim(segment, block_offset, BLOCK_SPAN, 0)
        block_places = block_offset + jnp.arange(BLOCK_SPAN, dtype=jnp.int32)
        scores = jnp.einsum('qkgd,tkd->kgqt', query_block_rows, keys_in, precision=lax.Precision.HIGHEST) * scale_factor
        scores = low_back(scores)
        allowed = (block_segment[:, None] == segment[None, :]) & (places[None, :] <= block_places[:, None])
        scores = jnp.where(allowed, scores, MASKED_FILL)
        soft_weights = jax.nn.softmax(scores, axis=-1)
        mixed_rows = jnp.einsum('kgqt,tkd->qkgd', low(soft_weights), values_in, precision=lax.Precision.HIGHEST)
        return mixed_rows.reshape(BLOCK_SPAN, QUERY_FEATURES)
    starts = jnp.arange(row_count_total // BLOCK_SPAN, dtype=jnp.int32) * BLOCK_SPAN
    return lax.map(jax.checkpoint(one_block), starts).reshape(row_count_total, QUERY_FEATURES)

def block_forward(x_rows, segment, position, norm_gains, qk_gains, weight_qkv, weight_out, weight_gate_up, weight_down):
    row_count_total = x_rows.shape[0]
    normed_first = low(rms_norm(x_rows, norm_gains[0]))
    query_key_value_rows = low_back(matmul(normed_first, weight_qkv))
    query_raw = query_key_value_rows[:, :QUERY_FEATURES].reshape(row_count_total, HQ, HEAD_SIZE)
    unnormed_key = query_key_value_rows[:, QUERY_FEATURES:QUERY_FEATURES + KEY_FEATURES].reshape(row_count_total, KEY_VALUE_HEADS, HEAD_SIZE)
    unnormed_value = query_key_value_rows[:, QUERY_FEATURES + KEY_FEATURES:].reshape(row_count_total, KEY_VALUE_HEADS, HEAD_SIZE)
    query_matrix = low(rotate(rms_norm(query_raw, qk_gains[0]), position))
    keys_in = low(rotate(rms_norm(unnormed_key, qk_gains[1]), position))
    values_in = low(unnormed_value)
    attn_mix = low_back(low(attend(query_matrix, keys_in, values_in, segment)))
    attn_branch = low_back(matmul(attn_mix, weight_out))
    x_mid = x_rows + attn_branch
    normed_second = low(rms_norm(x_mid, norm_gains[1]))
    gate_up = low_back(matmul(normed_second, weight_gate_up))
    hidden = low(jax.nn.silu(gate_up[:, :FF]) * gate_up[:, FF:])
    return x_mid + low_back(matmul(hidden, weight_down))

def adam_update(master, first_moment, second_moment, gradient, rate, decay):
    first_moment = BETA_ONE * first_moment + (1.0 - BETA_ONE) * gradient
    second_moment = BETA_TWO * second_moment + (1.0 - BETA_TWO) * gradient * gradient
    corrected = first_moment / (1.0 - BETA_ONE ** STEP) / (jnp.sqrt(second_moment / (1.0 - BETA_TWO ** STEP)) + ADAM_EPS)
    return (master - rate * (corrected + decay * master), first_moment, second_moment)

def reference(inputs, cotangent, lengths, norm_gains, norm_first, norm_second, qk_gains, qk_first, qk_second, qkv_master, qkv_first, qkv_second, out_master, out_first, out_second, gate_up_master, gate_up_first, gate_up_second, down_master, down_first, down_second):
    low_qkv = qkv_master.astype(jnp.bfloat16).astype(jnp.float32)
    low_out = out_master.astype(jnp.bfloat16).astype(jnp.float32)
    low_gate_up = gate_up_master.astype(jnp.bfloat16).astype(jnp.float32)
    low_down = down_master.astype(jnp.bfloat16).astype(jnp.float32)
    places = jnp.arange(SEQLEN, dtype=jnp.int32)

    def one_row(summed, row_items):
        x_row, cot_row, length_row = row_items
        segment, position = doc_layout(length_row, places)

        def forward(x_rows, gains_norm, gains_qk, weight_qkv, weight_out, weight_gate_up, weight_down):
            return block_forward(x_rows, segment, position, gains_norm, gains_qk, weight_qkv, weight_out, weight_gate_up, weight_down)
        result, pullback = jax.vjp(forward, x_row.astype(jnp.float32), norm_gains, qk_gains, low_qkv, low_out, low_gate_up, low_down)
        gradients = pullback(cot_row.astype(jnp.float32))
        summed = tuple((earlier + latest for earlier, latest in zip(summed, gradients[1:])))
        return (summed, (result.astype(jnp.bfloat16), gradients[0]))
    zero_init = tuple((jnp.zeros(parameter.shape, jnp.float32) for parameter in (norm_gains, qk_gains, low_qkv, low_out, low_gate_up, low_down)))
    summed, (outputs, input_grad) = lax.scan(one_row, zero_init, (inputs, cotangent, lengths))
    norm_new = adam_update(norm_gains, norm_first, norm_second, summed[0], GAIN_RATE, 0.0)
    qk_new = adam_update(qk_gains, qk_first, qk_second, summed[1], GAIN_RATE, 0.0)
    qkv_new = adam_update(qkv_master, qkv_first, qkv_second, summed[2], D ** (-0.5), DECAY_RATE)
    out_new = adam_update(out_master, out_first, out_second, summed[3], (QUERY_FEATURES // 16) ** (-0.5), DECAY_RATE)
    gate_new = adam_update(gate_up_master, gate_up_first, gate_up_second, summed[4], D ** (-0.5), DECAY_RATE)
    down_new = adam_update(down_master, down_first, down_second, summed[5], FF ** (-0.5), DECAY_RATE)
    return (outputs, input_grad, norm_new[0], norm_new[1], norm_new[2], qk_new[0], qk_new[1], qk_new[2], qkv_new[0], qkv_new[1], qkv_new[2], out_new[0], out_new[1], out_new[2], gate_new[0], gate_new[1], gate_new[2], down_new[0], down_new[1], down_new[2])
```

```python
import functools
import math

import jax
import jax.numpy as jnp
from jax import lax
from jax.experimental import pallas as pl
from jax.experimental.pallas import tpu as pltpu
from jax.sharding import PartitionSpec as P

D = 1024
HQ = 16
KEY_VALUE_HEADS = 8
HEAD_SIZE = 64
FF = 4608
QUERY_FEATURES = 1024
KEY_FEATURES = 512
STEP = 10
LANES = 128

NORM_EPS = 1e-05
ROPE_BASE = 1000000.0
BETA_ONE = 0.9
BETA_TWO = 0.95
ADAM_EPS = 1e-08
DECAY_RATE = 0.1
GAIN_RATE = 0.3

F32 = jnp.float32
BF16 = jnp.bfloat16
QUERY_BLOCK = 256
KEY_BLOCK = 256
FF_BLOCK = 256


def dot(a, b):
    return lax.dot_general(a, b, (((1,), (0,)), ((), ())), preferred_element_type=F32)


def dot_cols(a, b):
    return lax.dot_general(a, b, (((1,), (1,)), ((), ())), preferred_element_type=F32)


def dot_rows(a, b):
    return lax.dot_general(a, b, (((0,), (0,)), ((), ())), preferred_element_type=F32)


def params(limit=56):
    return pltpu.CompilerParams(vmem_limit_bytes=limit << 20)


def head_mean(v):
    row = lax.broadcasted_iota(jnp.int32, (LANES, LANES), 0) // HEAD_SIZE
    col = lax.broadcasted_iota(jnp.int32, (LANES, LANES), 1) // HEAD_SIZE
    ones = jnp.where(row == col, 1.0 / HEAD_SIZE, 0.0).astype(BF16)
    high = v.astype(BF16)
    low = (v - high.astype(F32)).astype(BF16)
    return dot(high, ones) + dot(low, ones)


def swap_halves(v):
    lane = lax.broadcasted_iota(jnp.int32, v.shape, 1) % HEAD_SIZE
    return jnp.where(
        lane < HEAD_SIZE // 2,
        pltpu.roll(v, LANES - HEAD_SIZE // 2, 1),
        pltpu.roll(v, HEAD_SIZE // 2, 1),
    )


def prep_kernel(raw_ref, gain_ref, cos_ref, sin_ref, q_ref, kv_ref):
    cosine, sine = cos_ref[...], sin_ref[...]
    for group in range(12):
        part = slice(group * LANES, (group + 1) * LANES)
        u = raw_ref[:, part]
        gain = gain_ref[0:1] if group < 8 else gain_ref[1:2]
        n = u * lax.rsqrt(head_mean(u * u) + NORM_EPS) * gain
        out = n * cosine + swap_halves(n) * sine
        if group < 8:
            q_ref[:, part] = (out * HEAD_SIZE**-0.5).astype(BF16)
        else:
            kv_ref[:, slice((group - 8) * LANES, (group - 7) * LANES)] = out.astype(BF16)
    kv_ref[:, KEY_FEATURES:] = raw_ref[:, QUERY_FEATURES + KEY_FEATURES :].astype(BF16)


def prep(raw, gains, cosine, sine):
    rows = raw.shape[0]
    block = min(rows, 256)
    whole = lambda width: pl.BlockSpec((block, width), lambda i: (i, 0))
    return pl.pallas_call(
        prep_kernel,
        name="prep",
        grid=(rows // block,),
        in_specs=[whole(2048), pl.BlockSpec((8, LANES), lambda i: (0, 0)), whole(LANES), whole(LANES)],
        out_specs=[whole(QUERY_FEATURES), whole(2 * KEY_FEATURES)],
        out_shape=[
            jax.ShapeDtypeStruct((rows, QUERY_FEATURES), BF16),
            jax.ShapeDtypeStruct((rows, 2 * KEY_FEATURES), BF16),
        ],
        compiler_params=params(),
        cost_estimate=pl.CostEstimate(
            flops=rows * 2048 * 40, transcendentals=rows * 24, bytes_accessed=rows * 2048 * 6
        ),
    )(raw, gains, cosine, sine)


def prep_back_kernel(raw_ref, gain_ref, cos_ref, sin_ref, dq_ref, dkv_ref, out_ref, dg_ref):
    cosine, sine = cos_ref[...], sin_ref[...]
    sums = [jnp.zeros((1, LANES), F32), jnp.zeros((1, LANES), F32)]
    for group in range(12):
        part = slice(group * LANES, (group + 1) * LANES)
        u = raw_ref[:, part]
        which = 0 if group < 8 else 1
        gain = gain_ref[which : which + 1]
        if group < 8:
            d = dq_ref[:, part] * HEAD_SIZE**-0.5
        else:
            d = dkv_ref[:, slice((group - 8) * LANES, (group - 7) * LANES)]
        d = d * cosine - swap_halves(d) * sine
        r = lax.rsqrt(head_mean(u * u) + NORM_EPS)
        w = d * gain
        n = u * r
        out_ref[:, part] = (r * (w - n * head_mean(w * n))).astype(BF16)
        sums[which] += jnp.sum(d * n, axis=0, keepdims=True)
    out_ref[:, QUERY_FEATURES + KEY_FEATURES :] = dkv_ref[:, KEY_FEATURES:].astype(BF16)

    @pl.when(pl.program_id(0) == 0)
    def _():
        dg_ref[...] = jnp.zeros_like(dg_ref)

    dg_ref[0:1] += sums[0]
    dg_ref[1:2] += sums[1]


def prep_back(raw, gains, cosine, sine, dq, dkv):
    rows = raw.shape[0]
    block = min(rows, 256)
    whole = lambda width: pl.BlockSpec((block, width), lambda i: (i, 0))
    small = pl.BlockSpec((8, LANES), lambda i: (0, 0))
    return pl.pallas_call(
        prep_back_kernel,
        name="prep_back",
        grid=(rows // block,),
        in_specs=[
            whole(2048),
            small,
            whole(LANES),
            whole(LANES),
            whole(QUERY_FEATURES),
            whole(2 * KEY_FEATURES),
        ],
        out_specs=[whole(2048), small],
        out_shape=[
            jax.ShapeDtypeStruct((rows, 2048), BF16),
            jax.ShapeDtypeStruct((8, LANES), F32),
        ],
        compiler_params=params(),
        cost_estimate=pl.CostEstimate(
            flops=rows * 2048 * 60, transcendentals=rows * 24, bytes_accessed=rows * 2048 * 10
        ),
    )(raw, gains, cosine, sine, dq, dkv)


def twice(pair, odd):
    wide = pair.astype(F32)
    turned = pltpu.roll(wide, HEAD_SIZE, 1)
    lane = lax.broadcasted_iota(jnp.int32, wide.shape, 1)
    first = lane < HEAD_SIZE
    keep = first != (odd == 1)
    return jnp.where(keep, wide, turned).astype(BF16)


def stack_heads(pair):
    lane = lax.broadcasted_iota(jnp.int32, pair.shape, 1)
    zero = jnp.zeros_like(pair)
    return jnp.concatenate(
        [jnp.where(lane < HEAD_SIZE, pair, zero), jnp.where(lane < HEAD_SIZE, zero, pair)], axis=0
    )


def fill(head, others, own, lane_block, target):
    odd = lax.rem(head, 2)
    at = 0
    for source in (others, own):
        rows = source.shape[0]
        for start in range(0, rows, 256):
            target[at + start : at + start + 256, lane_block : lane_block + LANES] = twice(
                source[start : start + 256, :], odd
            )
        at += rows


def attend_kernel(
    low_ref,
    first_ref,
    q_ref,
    ko_ref,
    vo_ref,
    k_ref,
    v_ref,
    out_ref,
    lse_ref,
    keys,
    values,
):
    head, turn = pl.program_id(0), pl.program_id(1)
    block = q_ref.shape[0]
    tall = 2 * block

    @pl.when(turn == 0)
    def _():
        fill(head, ko_ref, k_ref, 0, keys)
        fill(head, vo_ref, v_ref, 0, values)
        values[:, LANES:] = jnp.ones((values.shape[0], LANES), BF16)

    queries = stack_heads(q_ref[...])
    place0 = low_ref[0] + turn * block
    place = place0 + lax.rem(lax.broadcasted_iota(jnp.int32, (tall, 1), 0), block)
    first = first_ref[:, 0:1]
    first = jnp.concatenate([first, first], axis=0)
    begin = low_ref[1 + turn] // KEY_BLOCK
    end = (place0 + block - 1) // KEY_BLOCK + 1

    def step(at, total):
        start = pl.multiple_of(at * KEY_BLOCK, KEY_BLOCK)
        scores = dot_cols(queries, keys[pl.ds(start, KEY_BLOCK), :])
        key_place = start + lax.broadcasted_iota(jnp.int32, (tall, KEY_BLOCK), 1)
        allowed = (key_place >= first) & (key_place <= place)
        powers = jnp.where(allowed, jnp.exp(scores), 0.0).astype(BF16)
        return total + dot(powers, values[pl.ds(start, KEY_BLOCK), :])

    total = lax.fori_loop(begin, end, step, jnp.zeros((tall, 2 * LANES), F32))
    mass = total[:, LANES:]
    mixed = total[:, :LANES] / mass
    lane = lax.broadcasted_iota(jnp.int32, (block, LANES), 1)
    out_ref[...] = jnp.where(lane < HEAD_SIZE, mixed[:block], mixed[block:]).astype(BF16)
    logs = jnp.log(mass)
    lse_ref[0] = jnp.transpose(logs)[0:8, :]


def attend(q, others, own, low, first):
    rows = q.shape[0]
    block = min(QUERY_BLOCK, rows)
    turns = rows // block
    total = others.shape[0] + rows
    pair = lambda size, off: pl.BlockSpec((size, LANES), lambda h, t, low: (0, off + h // 2))
    return pl.pallas_call(
        attend_kernel,
        name="attend",
        grid_spec=pltpu.PrefetchScalarGridSpec(
            num_scalar_prefetch=1,
            grid=(KEY_VALUE_HEADS, turns),
            in_specs=[
                pl.BlockSpec((block, LANES), lambda h, t, low: (t, 0)),
                pl.BlockSpec((block, LANES), lambda h, t, low: (t, h)),
                pair(others.shape[0], 0),
                pair(others.shape[0], 4),
                pair(rows, 0),
                pair(rows, 4),
            ],
            out_specs=[
                pl.BlockSpec((block, LANES), lambda h, t, low: (t, h)),
                pl.BlockSpec((1, 8, 2 * block), lambda h, t, low: (h, t, 0)),
            ],
            scratch_shapes=[pltpu.VMEM((total, LANES), BF16), pltpu.VMEM((total, 2 * LANES), BF16)],
        ),
        out_shape=[
            jax.ShapeDtypeStruct((rows, QUERY_FEATURES), BF16),
            jax.ShapeDtypeStruct((KEY_VALUE_HEADS, 8 * turns, 2 * block), F32),
        ],
        compiler_params=params(),
        cost_estimate=pl.CostEstimate(
            flops=rows * 1024 * 1024 * 8, transcendentals=rows * 1024 * 16, bytes_accessed=16 << 20
        ),
    )(low, first, q, others, others, own, own)


def attend_back_kernel(
    low_ref,
    first_ref,
    q_ref,
    do_ref,
    mixed_ref,
    lse_ref,
    ko_ref,
    vo_ref,
    k_ref,
    v_ref,
    dq_ref,
    dk_ref,
    dv_ref,
    keys,
    values,
    dkeys,
    dvalues,
):
    head, turn = pl.program_id(0), pl.program_id(1)
    block = q_ref.shape[0]
    tall = 2 * block

    @pl.when(turn == 0)
    def _():
        fill(head, ko_ref, k_ref, 0, keys)
        fill(head, vo_ref, v_ref, 0, values)
        dkeys[...] = jnp.zeros_like(dkeys)
        dvalues[...] = jnp.zeros_like(dvalues)

    queries = stack_heads(q_ref[...])
    rising = stack_heads(do_ref[...])
    across = jnp.transpose(do_ref[...].astype(F32) * mixed_ref[...].astype(F32))
    delta = jnp.concatenate(
        [
            jnp.sum(across[:HEAD_SIZE], axis=0, keepdims=True),
            jnp.sum(across[HEAD_SIZE:], axis=0, keepdims=True),
        ],
        axis=1,
    )
    logs = lse_ref[0][0:1]
    place0 = low_ref[0] + turn * block
    place = place0 + lax.rem(lax.broadcasted_iota(jnp.int32, (1, tall), 1), block)
    first = first_ref[0:1]
    first = jnp.concatenate([first, first], axis=1)
    begin = low_ref[1 + turn] // KEY_BLOCK
    end = (place0 + block - 1) // KEY_BLOCK + 1

    def step(at, dq):
        start = pl.multiple_of(at * KEY_BLOCK, KEY_BLOCK)
        span = pl.ds(start, KEY_BLOCK)
        key = keys[span, :]
        scores = dot_cols(key, queries)
        key_place = start + lax.broadcasted_iota(jnp.int32, (KEY_BLOCK, tall), 0)
        allowed = (key_place >= first) & (key_place <= place)
        probs = jnp.where(allowed, jnp.exp(scores - logs), 0.0)
        dprobs = dot_cols(values[span, :], rising)
        dscores = (probs * (dprobs - delta)).astype(BF16)
        dkeys[span, :] += dot(dscores, queries)
        dvalues[span, :] += dot(probs.astype(BF16), rising)
        return dq + dot_rows(dscores, key)

    dq = lax.fori_loop(begin, end, step, jnp.zeros((tall, LANES), F32))
    lane = lax.broadcasted_iota(jnp.int32, (block, LANES), 1)
    dq_ref[...] = jnp.where(lane < HEAD_SIZE, dq[:block], dq[block:])

    @pl.when(turn == pl.num_programs(1) - 1)
    def _():
        odd = lax.rem(head, 2)
        for source, target in ((dkeys, dk_ref), (dvalues, dv_ref)):
            for start in range(0, source.shape[0], 256):
                part = slice(start, start + 256)
                both = source[part, :]
                both = both + pltpu.roll(both, HEAD_SIZE, 1)
                lane = lax.broadcasted_iota(jnp.int32, both.shape, 1)
                mine = (lane < HEAD_SIZE) != (odd == 1)

                @pl.when(odd == 0)
                def _():
                    target[part, :] = both

                @pl.when(odd == 1)
                def _():
                    target[part, :] = jnp.where(mine, both, target[part, :])


def attend_back(q, d_mixed, mixed, lse, others, own, low, first_lane):
    rows = q.shape[0]
    block = min(QUERY_BLOCK, rows)
    turns = rows // block
    total = others.shape[0] + rows
    pair = lambda size, off: pl.BlockSpec((size, LANES), lambda h, t, low: (0, off + h // 2))
    tile = pl.BlockSpec((block, LANES), lambda h, t, low: (t, h))
    return pl.pallas_call(
        attend_back_kernel,
        name="attend_back",
        grid_spec=pltpu.PrefetchScalarGridSpec(
            num_scalar_prefetch=1,
            grid=(KEY_VALUE_HEADS, turns),
            in_specs=[
                pl.BlockSpec((8, block), lambda h, t, low: (0, t)),
                tile,
                tile,
                tile,
                pl.BlockSpec((1, 8, 2 * block), lambda h, t, low: (h, t, 0)),
                pair(others.shape[0], 0),
                pair(others.shape[0], 4),
                pair(rows, 0),
                pair(rows, 4),
            ],
            out_specs=[tile, pair(total, 0), pair(total, 0)],
            scratch_shapes=[
                pltpu.VMEM((total, LANES), BF16),
                pltpu.VMEM((total, LANES), BF16),
                pltpu.VMEM((total, LANES), F32),
                pltpu.VMEM((total, LANES), F32),
            ],
        ),
        out_shape=[
            jax.ShapeDtypeStruct((rows, QUERY_FEATURES), F32),
            jax.ShapeDtypeStruct((total, KEY_FEATURES), F32),
            jax.ShapeDtypeStruct((total, KEY_FEATURES), F32),
        ],
        compiler_params=params(),
        cost_estimate=pl.CostEstimate(
            flops=rows * 1024 * 1024 * 20, transcendentals=rows * 1024 * 16, bytes_accessed=40 << 20
        ),
    )(low, first_lane, q, d_mixed, mixed, lse, others, others, own, own)


def feed_kernel(
    a_ref, at_ref, g_ref, wg_ref, wu_ref, wd_ref, y_in, b_in, y_ref, b_ref, gg_ref, gu_ref, gd_ref
):
    @pl.when(pl.program_id(0) == 0)
    def _():
        y_ref[...] = y_in[...]
        b_ref[...] = b_in[...]

    a, g = a_ref[...], g_ref[...]
    wg, wu, wd = wg_ref[...], wu_ref[...], wd_ref[...]
    gate = dot(a, wg)
    up = dot(a, wu)
    d_hidden = dot_cols(g, wd)
    sigma = 1.0 / (1.0 + jnp.exp(-gate))
    swish = gate * sigma
    hidden = (swish * up).astype(BF16)
    d_gate = (d_hidden * up * sigma * (1.0 + gate * (1.0 - sigma))).astype(BF16)
    d_up = (d_hidden * swish).astype(BF16)
    y_ref[...] += dot(hidden, wd)
    b_ref[...] += dot_cols(d_gate, wg) + dot_cols(d_up, wu)
    at = at_ref[...]
    gg_ref[...] = dot(at, d_gate).astype(BF16)
    gu_ref[...] = dot(at, d_up).astype(BF16)
    gd_ref[...] = dot_rows(hidden, g).astype(BF16)


def feed(a, at, g, w_gate, w_up, w_down, y, b):
    rows, width = a.shape[0], w_gate.shape[1]
    turns = width // FF_BLOCK
    fixed = lambda s: pl.BlockSpec(s, lambda j: (0, 0))
    col = pl.BlockSpec((D, FF_BLOCK), lambda j: (0, j))
    row = pl.BlockSpec((FF_BLOCK, D), lambda j: (j, 0))
    return pl.pallas_call(
        feed_kernel,
        name="feed",
        grid=(turns,),
        in_specs=[
            fixed((rows, D)),
            fixed((D, rows)),
            fixed((rows, D)),
            col,
            col,
            row,
            fixed((rows, D)),
            fixed((rows, D)),
        ],
        out_specs=[fixed((rows, D)), fixed((rows, D)), col, col, row],
        out_shape=[
            jax.ShapeDtypeStruct((rows, D), F32),
            jax.ShapeDtypeStruct((rows, D), F32),
            jax.ShapeDtypeStruct((D, width), BF16),
            jax.ShapeDtypeStruct((D, width), BF16),
            jax.ShapeDtypeStruct((width, D), BF16),
        ],
        compiler_params=params(60),
        cost_estimate=pl.CostEstimate(
            flops=18 * rows * D * width, transcendentals=rows * width, bytes_accessed=12 * D * width
        ),
    )(a, at, g, w_gate, w_up, w_down, y, b)


def rms_scale(v):
    return lax.rsqrt(jnp.mean(v * v, axis=-1, keepdims=True) + NORM_EPS)


def rms_back(v, scale, gain_row, d_out):
    w = d_out * gain_row
    n = v * scale
    d_v = scale * (w - n * jnp.mean(w * n, axis=-1, keepdims=True))
    return d_v, jnp.sum(d_out * n, axis=0)


def adam_update(master, first_moment, second_moment, gradient, rate, decay):
    first_moment = BETA_ONE * first_moment + (1.0 - BETA_ONE) * gradient
    second_moment = BETA_TWO * second_moment + (1.0 - BETA_TWO) * gradient * gradient
    corrected = (
        first_moment
        / (1.0 - BETA_ONE**STEP)
        / (jnp.sqrt(second_moment / (1.0 - BETA_TWO**STEP)) + ADAM_EPS)
    )
    return (master - rate * (corrected + decay * master), first_moment, second_moment)


def rotation_tables(position):
    half = HEAD_SIZE // 2
    index_row = jnp.arange(half, dtype=F32)
    frequency = jnp.exp(index_row * (-2.0 * math.log(ROPE_BASE) / HEAD_SIZE))
    angles = position.astype(F32)[:, None] * frequency[None, :]
    cosine, sine = jnp.cos(angles), jnp.sin(angles)
    return (
        jnp.concatenate([cosine] * 4, axis=1),
        jnp.concatenate([-sine, sine, -sine, sine], axis=1),
    )


ALL = ("fsdp", "seq")


def gather(shard):
    return lax.all_gather(shard, ALL, axis=0, tiled=True)


def scatter(terms):
    return lax.psum_scatter(terms, ALL, scatter_dimension=0, tiled=True).astype(F32)


def per_device(
    inputs,
    cotangent,
    lengths,
    norm_gains,
    norm_first,
    norm_second,
    qk_gains,
    qk_first,
    qk_second,
    qkv_master,
    qkv_first,
    qkv_second,
    out_master,
    out_first,
    out_second,
    gate_up_master,
    gate_up_first,
    gate_up_second,
    down_master,
    down_first,
    down_second,
):
    seq_width = lax.axis_size("seq")
    turn_here = lax.axis_index("seq")
    rows = inputs.shape[1]
    block = min(QUERY_BLOCK, rows)
    w_qkv = gather(qkv_master.astype(BF16))
    w_out = gather(out_master.astype(BF16))
    w_down = gather(down_master.astype(BF16))
    w_gate = gather(gate_up_master[:, :FF].astype(BF16))
    w_up = gather(gate_up_master[:, FF:].astype(BF16))

    places = turn_here * rows + jnp.arange(rows, dtype=jnp.int32)
    row_lengths = lengths[0]
    doc_ends = jnp.cumsum(row_lengths)
    passed = doc_ends[None, :] <= places[:, None]
    begins = jnp.sum(jnp.where(passed, row_lengths[None, :], 0), axis=1)
    cosine, sine = rotation_tables(places - begins)
    if seq_width == 2:
        base = (turn_here - 1) * rows
    else:
        base = turn_here * 0
    first = (begins - base).astype(jnp.int32)
    low = jnp.concatenate([(turn_here * rows - base)[None], first[::block]]).astype(jnp.int32)
    first_wide = jnp.broadcast_to(first[:, None], (rows, LANES))
    first_lane = jnp.broadcast_to(first[None, :], (8, rows))

    x = inputs[0].astype(F32)
    scale_first = rms_scale(x)
    normed_first = (x * scale_first * norm_gains[0]).astype(BF16)
    raw = jnp.dot(normed_first, w_qkv, preferred_element_type=F32)
    gain_rows = jnp.pad(jnp.tile(qk_gains, (1, 2)), ((0, 6), (0, 0)))
    q, kv = prep(raw, gain_rows, cosine, sine)
    if seq_width == 2:
        others = lax.ppermute(kv, "seq", [(0, 1)])
        own = kv
    else:
        everyone = lax.all_gather(kv, "seq", axis=0, tiled=True)
        others, own = everyone, kv
    mixed, lse = attend(q, others, own, low, first_wide)
    x_mid = x + jnp.dot(mixed, w_out, preferred_element_type=F32)
    scale_second = rms_scale(x_mid)
    normed_second = (x_mid * scale_second * norm_gains[1]).astype(BF16)
    g = cotangent[0]
    out_sum, d_b, grad_gate, grad_up, grad_down = feed(
        normed_second, normed_second.T, g, w_gate, w_up, w_down, x_mid, jnp.zeros_like(x_mid)
    )
    outputs = out_sum.astype(BF16)
    gate_grad = scatter(grad_gate)
    up_grad = scatter(grad_up)
    down_grad = scatter(grad_down)
    d_norm, d_gain_second = rms_back(x_mid, scale_second, norm_gains[1], d_b)
    d_mid = g.astype(F32) + d_norm
    d_attn = d_mid.astype(BF16)
    d_mixed = dot_cols(d_attn, w_out).astype(BF16)
    out_grad = scatter(dot_rows(mixed, d_attn).astype(BF16))
    dq, dk, dv = attend_back(q, d_mixed, mixed, lse, others, own, low, first_lane)
    d_all = jnp.concatenate([dk, dv], axis=1)
    if seq_width == 2:
        back = lax.ppermute(d_all[:rows].astype(BF16), "seq", [(1, 0)])
        dkv = d_all[rows:] + back.astype(F32)
    else:
        dkv = lax.psum_scatter(
            d_all[: seq_width * rows].astype(BF16), "seq", scatter_dimension=0, tiled=True
        ).astype(F32)
    d_qkv, d_gain_qk = prep_back(raw, gain_rows, cosine, sine, dq, dkv)
    qkv_grad = scatter(dot_rows(normed_first, d_qkv).astype(BF16))
    d_a = dot_cols(d_qkv, w_qkv)
    d_x, d_gain_first = rms_back(x, scale_first, norm_gains[0], d_a)
    input_grad = (d_mid + d_x)[None]
    norm_terms = jnp.stack([d_gain_first, d_gain_second])
    qk_terms = d_gain_qk[:2, :HEAD_SIZE] + d_gain_qk[:2, HEAD_SIZE:]
    norm_grad, qk_grad = lax.psum((norm_terms, qk_terms), ALL)

    norm_new = adam_update(norm_gains, norm_first, norm_second, norm_grad, GAIN_RATE, 0.0)
    qk_new = adam_update(qk_gains, qk_first, qk_second, qk_grad, GAIN_RATE, 0.0)
    qkv_new = adam_update(qkv_master, qkv_first, qkv_second, qkv_grad, D**-0.5, DECAY_RATE)
    out_new = adam_update(
        out_master, out_first, out_second, out_grad, (QUERY_FEATURES // 16) ** -0.5, DECAY_RATE
    )
    gate_up_grad = jnp.concatenate([gate_grad, up_grad], axis=1)
    gate_new = adam_update(
        gate_up_master, gate_up_first, gate_up_second, gate_up_grad, D**-0.5, DECAY_RATE
    )
    down_new = adam_update(down_master, down_first, down_second, down_grad, FF**-0.5, DECAY_RATE)
    return (
        outputs[None],
        input_grad,
        *norm_new,
        *qk_new,
        *qkv_new,
        *out_new,
        *gate_new,
        *down_new,
    )


def solution(mesh):
    token = P("fsdp", "seq", None)
    weight = P(ALL, None)
    return jax.shard_map(
        per_device,
        mesh=mesh,
        in_specs=(token, token, P("fsdp", None)) + (P(),) * 6 + (weight,) * 12,
        out_specs=(token, token) + (P(),) * 6 + (weight,) * 12,
        check_vma=False,
    )
```

```python
import functools
import math

import jax
import jax.numpy as jnp
from jax import lax
from jax.experimental import pallas as pl
from jax.experimental.pallas import tpu as pltpu
from jax.sharding import PartitionSpec as P

D = 1024
HQ = 16
KEY_VALUE_HEADS = 8
HEAD_SIZE = 64
FF = 4608
QUERY_FEATURES = 1024
KEY_FEATURES = 512
STEP = 10
LANES = 128

NORM_EPS = 1e-05
ROPE_BASE = 1000000.0
BETA_ONE = 0.9
BETA_TWO = 0.95
ADAM_EPS = 1e-08
DECAY_RATE = 0.1
GAIN_RATE = 0.3

F32 = jnp.float32
BF16 = jnp.bfloat16
QUERY_BLOCK = 256
KEY_BLOCK = 256
FF_BLOCK = 256
PIECES = 4


def dot(a, b):
    return lax.dot_general(a, b, (((1,), (0,)), ((), ())), preferred_element_type=F32)


def dot_cols(a, b):
    return lax.dot_general(a, b, (((1,), (1,)), ((), ())), preferred_element_type=F32)


def dot_rows(a, b):
    return lax.dot_general(a, b, (((0,), (0,)), ((), ())), preferred_element_type=F32)


def params(limit=56):
    return pltpu.CompilerParams(vmem_limit_bytes=limit << 20)


def head_mean(v):
    row = lax.broadcasted_iota(jnp.int32, (LANES, LANES), 0) // HEAD_SIZE
    col = lax.broadcasted_iota(jnp.int32, (LANES, LANES), 1) // HEAD_SIZE
    ones = jnp.where(row == col, 1.0 / HEAD_SIZE, 0.0).astype(BF16)
    high = v.astype(BF16)
    low = (v - high.astype(F32)).astype(BF16)
    return dot(high, ones) + dot(low, ones)


def swap_halves(v):
    lane = lax.broadcasted_iota(jnp.int32, v.shape, 1) % HEAD_SIZE
    return jnp.where(
        lane < HEAD_SIZE // 2,
        pltpu.roll(v, LANES - HEAD_SIZE // 2, 1),
        pltpu.roll(v, HEAD_SIZE // 2, 1),
    )


def prep_kernel(raw_ref, gain_ref, cos_ref, sin_ref, q_ref, *kv_refs):
    cosine, sine = cos_ref[...], sin_ref[...]
    for group in range(12):
        part = slice(group * LANES, (group + 1) * LANES)
        u = raw_ref[:, part]
        gain = gain_ref[0:1] if group < 8 else gain_ref[1:2]
        n = u * lax.rsqrt(head_mean(u * u) + NORM_EPS) * gain
        out = n * cosine + swap_halves(n) * sine
        if group < 8:
            q_ref[:, part] = (out * HEAD_SIZE**-0.5).astype(BF16)
        else:
            kv_ref = kv_refs[group - 8]
            kv_ref[:, :LANES] = out.astype(BF16)
            value = raw_ref[:, slice((group + 4) * LANES, (group + 5) * LANES)]
            kv_ref[:, LANES:] = value.astype(BF16)


def prep(raw, gains, cosine, sine):
    rows = raw.shape[0]
    block = min(rows, 256)
    whole = lambda width: pl.BlockSpec((block, width), lambda i: (i, 0))
    return pl.pallas_call(
        prep_kernel,
        name="prep",
        grid=(rows // block,),
        in_specs=[whole(2048), pl.BlockSpec((8, LANES), lambda i: (0, 0)), whole(LANES), whole(LANES)],
        out_specs=[whole(QUERY_FEATURES)] + [whole(2 * LANES)] * PIECES,
        out_shape=[jax.ShapeDtypeStruct((rows, QUERY_FEATURES), BF16)]
        + [jax.ShapeDtypeStruct((rows, 2 * LANES), BF16)] * PIECES,
        compiler_params=params(),
        cost_estimate=pl.CostEstimate(
            flops=rows * 2048 * 40, transcendentals=rows * 24, bytes_accessed=rows * 2048 * 6
        ),
    )(raw, gains, cosine, sine)


def prep_back_kernel(raw_ref, gain_ref, cos_ref, sin_ref, *rest):
    dq_refs, own_refs, back_refs = (rest[PIECES * i : PIECES * (i + 1)] for i in range(3))
    out_ref, dg_ref = rest[3 * PIECES :]
    cosine, sine = cos_ref[...], sin_ref[...]
    sums = [jnp.zeros((1, LANES), F32), jnp.zeros((1, LANES), F32)]
    for group in range(12):
        part = slice(group * LANES, (group + 1) * LANES)
        u = raw_ref[:, part]
        which = 0 if group < 8 else 1
        gain = gain_ref[which : which + 1]
        if group < 8:
            half = slice(group % 2 * LANES, (group % 2 + 1) * LANES)
            d = dq_refs[group // 2][:, half] * HEAD_SIZE**-0.5
        else:
            own, back = own_refs[group - 8], back_refs[group - 8]
            d = own[:, :LANES] + back[:, :LANES].astype(F32)
            value = slice((group + 4) * LANES, (group + 5) * LANES)
            out_ref[:, value] = (own[:, LANES:] + back[:, LANES:].astype(F32)).astype(BF16)
        d = d * cosine - swap_halves(d) * sine
        r = lax.rsqrt(head_mean(u * u) + NORM_EPS)
        w = d * gain
        n = u * r
        out_ref[:, part] = (r * (w - n * head_mean(w * n))).astype(BF16)
        sums[which] += jnp.sum(d * n, axis=0, keepdims=True)

    @pl.when(pl.program_id(0) == 0)
    def _():
        dg_ref[...] = jnp.zeros_like(dg_ref)

    dg_ref[0:1] += sums[0]
    dg_ref[1:2] += sums[1]


def prep_back(raw, gains, cosine, sine, dq, own, back):
    rows = raw.shape[0]
    block = min(rows, 256)
    whole = lambda width: pl.BlockSpec((block, width), lambda i: (i, 0))
    small = pl.BlockSpec((8, LANES), lambda i: (0, 0))
    return pl.pallas_call(
        prep_back_kernel,
        name="prep_back",
        grid=(rows // block,),
        in_specs=[
            whole(2048),
            small,
            whole(LANES),
            whole(LANES),
        ]
        + [whole(2 * LANES)] * (3 * PIECES),
        out_specs=[whole(2048), small],
        out_shape=[
            jax.ShapeDtypeStruct((rows, 2048), BF16),
            jax.ShapeDtypeStruct((8, LANES), F32),
        ],
        compiler_params=params(),
        cost_estimate=pl.CostEstimate(
            flops=rows * 2048 * 60, transcendentals=rows * 24, bytes_accessed=rows * 2048 * 10
        ),
    )(raw, gains, cosine, sine, *dq, *own, *back)


def twice(pair, odd):
    wide = pair.astype(F32)
    turned = pltpu.roll(wide, HEAD_SIZE, 1)
    lane = lax.broadcasted_iota(jnp.int32, wide.shape, 1)
    first = lane < HEAD_SIZE
    keep = first != (odd == 1)
    return jnp.where(keep, wide, turned).astype(BF16)


def stack_heads(pair):
    lane = lax.broadcasted_iota(jnp.int32, pair.shape, 1)
    zero = jnp.zeros_like(pair)
    return jnp.concatenate(
        [jnp.where(lane < HEAD_SIZE, pair, zero), jnp.where(lane < HEAD_SIZE, zero, pair)], axis=0
    )


def fill(head, others, own, lane_block, target):
    odd = lax.rem(head, 2)
    at = 0
    for source in (others, own):
        rows = source.shape[0]
        for start in range(0, rows, 256):
            target[at + start : at + start + 256, lane_block : lane_block + LANES] = twice(
                source[start : start + 256, :], odd
            )
        at += rows


def attend_kernel(
    low_ref,
    first_ref,
    q_ref,
    ko_ref,
    vo_ref,
    k_ref,
    v_ref,
    out_ref,
    lse_ref,
    keys,
    values,
):
    head, turn = pl.program_id(0), pl.program_id(1)
    block = q_ref.shape[0]
    tall = 2 * block

    @pl.when(turn == 0)
    def _():
        fill(head, ko_ref, k_ref, 0, keys)
        fill(head, vo_ref, v_ref, 0, values)
        values[:, LANES:] = jnp.ones((values.shape[0], LANES), BF16)

    queries = stack_heads(q_ref[...])
    place0 = low_ref[0] + turn * block
    place = place0 + lax.rem(lax.broadcasted_iota(jnp.int32, (tall, 1), 0), block)
    first = first_ref[:, 0:1]
    first = jnp.concatenate([first, first], axis=0)
    begin = low_ref[1 + turn] // KEY_BLOCK
    end = (place0 + block - 1) // KEY_BLOCK + 1

    def step(at, total):
        start = pl.multiple_of(at * KEY_BLOCK, KEY_BLOCK)
        scores = dot_cols(queries, keys[pl.ds(start, KEY_BLOCK), :])
        key_place = start + lax.broadcasted_iota(jnp.int32, (tall, KEY_BLOCK), 1)
        allowed = (key_place >= first) & (key_place <= place)
        powers = jnp.where(allowed, jnp.exp(scores), 0.0).astype(BF16)
        return total + dot(powers, values[pl.ds(start, KEY_BLOCK), :])

    total = lax.fori_loop(begin, end, step, jnp.zeros((tall, 2 * LANES), F32))
    mass = total[:, LANES:]
    mixed = total[:, :LANES] / mass
    lane = lax.broadcasted_iota(jnp.int32, (block, LANES), 1)
    out_ref[...] = jnp.where(lane < HEAD_SIZE, mixed[:block], mixed[block:]).astype(BF16)
    logs = jnp.log(mass)
    lse_ref[0] = jnp.transpose(logs)[0:8, :]


def attend(piece, q, others, own, low, first):
    rows = q.shape[0]
    block = min(QUERY_BLOCK, rows)
    turns = rows // block
    total = others.shape[0] + rows
    pair = lambda size, off: pl.BlockSpec((size, LANES), lambda h, t, low: (0, off))
    return pl.pallas_call(
        attend_kernel,
        name="attend",
        grid_spec=pltpu.PrefetchScalarGridSpec(
            num_scalar_prefetch=1,
            grid=(2, turns),
            in_specs=[
                pl.BlockSpec((block, LANES), lambda h, t, low: (t, 0)),
                pl.BlockSpec((block, LANES), lambda h, t, low: (t, 2 * piece + h)),
                pair(others.shape[0], 0),
                pair(others.shape[0], 1),
                pair(rows, 0),
                pair(rows, 1),
            ],
            out_specs=[
                pl.BlockSpec((block, LANES), lambda h, t, low: (t, h)),
                pl.BlockSpec((1, 8, 2 * block), lambda h, t, low: (h, t, 0)),
            ],
            scratch_shapes=[pltpu.VMEM((total, LANES), BF16), pltpu.VMEM((total, 2 * LANES), BF16)],
        ),
        out_shape=[
            jax.ShapeDtypeStruct((rows, 2 * LANES), BF16),
            jax.ShapeDtypeStruct((2, 8 * turns, 2 * block), F32),
        ],
        compiler_params=params(),
        cost_estimate=pl.CostEstimate(
            flops=rows * 1024 * 1024 * 8, transcendentals=rows * 1024 * 4, bytes_accessed=4 << 20
        ),
    )(low, first, q, others, others, own, own)


def attend_back_kernel(
    low_ref,
    first_ref,
    q_ref,
    do_ref,
    mixed_ref,
    lse_ref,
    ko_ref,
    vo_ref,
    k_ref,
    v_ref,
    dq_ref,
    far_ref,
    near_ref,
    keys,
    values,
    dkeys,
    dvalues,
):
    head, turn = pl.program_id(0), pl.program_id(1)
    block = q_ref.shape[0]
    tall = 2 * block

    @pl.when(turn == 0)
    def _():
        fill(head, ko_ref, k_ref, 0, keys)
        fill(head, vo_ref, v_ref, 0, values)
        dkeys[...] = jnp.zeros_like(dkeys)
        dvalues[...] = jnp.zeros_like(dvalues)

    queries = stack_heads(q_ref[...])
    rising = stack_heads(do_ref[...])
    across = jnp.transpose(do_ref[...].astype(F32) * mixed_ref[...].astype(F32))
    delta = jnp.concatenate(
        [
            jnp.sum(across[:HEAD_SIZE], axis=0, keepdims=True),
            jnp.sum(across[HEAD_SIZE:], axis=0, keepdims=True),
        ],
        axis=1,
    )
    logs = lse_ref[0][0:1]
    place0 = low_ref[0] + turn * block
    place = place0 + lax.rem(lax.broadcasted_iota(jnp.int32, (1, tall), 1), block)
    first = first_ref[0:1]
    first = jnp.concatenate([first, first], axis=1)
    begin = low_ref[1 + turn] // KEY_BLOCK
    end = (place0 + block - 1) // KEY_BLOCK + 1

    def step(at, dq):
        start = pl.multiple_of(at * KEY_BLOCK, KEY_BLOCK)
        span = pl.ds(start, KEY_BLOCK)
        key = keys[span, :]
        scores = dot_cols(key, queries)
        key_place = start + lax.broadcasted_iota(jnp.int32, (KEY_BLOCK, tall), 0)
        allowed = (key_place >= first) & (key_place <= place)
        probs = jnp.where(allowed, jnp.exp(scores - logs), 0.0)
        dprobs = dot_cols(values[span, :], rising)
        dscores = (probs * (dprobs - delta)).astype(BF16)
        dkeys[span, :] += dot(dscores, queries)
        dvalues[span, :] += dot(probs.astype(BF16), rising)
        return dq + dot_rows(dscores, key)

    dq = lax.fori_loop(begin, end, step, jnp.zeros((tall, LANES), F32))
    lane = lax.broadcasted_iota(jnp.int32, (block, LANES), 1)
    dq_ref[...] = jnp.where(lane < HEAD_SIZE, dq[:block], dq[block:])

    @pl.when(turn == pl.num_programs(1) - 1)
    def _():
        odd = lax.rem(head, 2)
        far = far_ref.shape[0]
        for source, off in ((dkeys, 0), (dvalues, LANES)):
            for start in range(0, source.shape[0], 256):
                both = source[start : start + 256, :]
                both = both + pltpu.roll(both, HEAD_SIZE, 1)
                lane = lax.broadcasted_iota(jnp.int32, both.shape, 1)
                mine = (lane < HEAD_SIZE) != (odd == 1)
                target, to = (far_ref, start) if start < far else (near_ref, start - far)
                part = (slice(to, to + 256), slice(off, off + LANES))

                @pl.when(odd == 0)
                def _():
                    target[part] = both.astype(target.dtype)

                @pl.when(odd == 1)
                def _():
                    target[part] = jnp.where(mine, both, target[part].astype(F32)).astype(target.dtype)


def attend_back(piece, q, d_mixed, mixed, lse, others, own, low, first_lane):
    rows = q.shape[0]
    block = min(QUERY_BLOCK, rows)
    turns = rows // block
    total = others.shape[0] + rows
    pair = lambda size, off: pl.BlockSpec((size, LANES), lambda h, t, low: (0, off))
    whole = lambda size: pl.BlockSpec((size, 2 * LANES), lambda h, t, low: (0, 0))
    tile = pl.BlockSpec((block, LANES), lambda h, t, low: (t, h))
    tile_of_all = pl.BlockSpec((block, LANES), lambda h, t, low: (t, 2 * piece + h))
    return pl.pallas_call(
        attend_back_kernel,
        name="attend_back",
        grid_spec=pltpu.PrefetchScalarGridSpec(
            num_scalar_prefetch=1,
            grid=(2, turns),
            in_specs=[
                pl.BlockSpec((8, block), lambda h, t, low: (0, t)),
                tile_of_all,
                tile_of_all,
                tile,
                pl.BlockSpec((1, 8, 2 * block), lambda h, t, low: (h, t, 0)),
                pair(others.shape[0], 0),
                pair(others.shape[0], 1),
                pair(rows, 0),
                pair(rows, 1),
            ],
            out_specs=[tile, whole(others.shape[0]), whole(rows)],
            scratch_shapes=[
                pltpu.VMEM((total, LANES), BF16),
                pltpu.VMEM((total, LANES), BF16),
                pltpu.VMEM((total, LANES), F32),
                pltpu.VMEM((total, LANES), F32),
            ],
        ),
        out_shape=[
            jax.ShapeDtypeStruct((rows, 2 * LANES), F32),
            jax.ShapeDtypeStruct((others.shape[0], 2 * LANES), BF16),
            jax.ShapeDtypeStruct((rows, 2 * LANES), F32),
        ],
        compiler_params=params(),
        cost_estimate=pl.CostEstimate(
            flops=rows * 1024 * 1024 * 12, transcendentals=rows * 1024 * 4, bytes_accessed=10 << 20
        ),
    )(low, first_lane, q, d_mixed, mixed, lse, others, others, own, own)


def feed_kernel(
    a_ref,
    atg_ref,
    atu_ref,
    g_ref,
    wg_ref,
    wu_ref,
    wd_ref,
    y_in,
    y_ref,
    b_ref,
    gg_ref,
    ggs_ref,
    gu_ref,
    gus_ref,
    gd_ref,
):
    @pl.when(pl.program_id(0) == 0)
    def _():
        y_ref[...] = y_in[...]
        b_ref[...] = jnp.zeros_like(b_ref)

    a, g = a_ref[...], g_ref[...]
    wg, wu, wd = wg_ref[...], wu_ref[...], wd_ref[...]
    gate = dot(a, wg)
    up = dot(a, wu)
    d_hidden = dot_cols(g, wd)
    sigma = 1.0 / (1.0 + jnp.exp(-gate))
    swish = gate * sigma
    hidden = (swish * up).astype(BF16)
    d_gate = (d_hidden * up * sigma * (1.0 + gate * (1.0 - sigma))).astype(BF16)
    d_up = (d_hidden * swish).astype(BF16)
    y_ref[...] += dot(hidden, wd)
    b_ref[...] += dot_cols(d_gate, wg) + dot_cols(d_up, wu)
    half = atg_ref.shape[0] // 2
    gg_ref[...] = dot(atg_ref[:half], d_gate).astype(BF16)
    ggs_ref[...] = dot(atg_ref[half:], d_gate).astype(BF16)
    gu_ref[...] = dot(atu_ref[:half], d_up).astype(BF16)
    gus_ref[...] = dot(atu_ref[half:], d_up).astype(BF16)
    gd_ref[...] = dot_rows(hidden, g).astype(BF16)


def feed(a, at_gate, at_up, g, w_gate, w_up, w_down, y):
    rows, width = a.shape[0], w_gate.shape[1]
    turns = width // FF_BLOCK
    fixed = lambda s: pl.BlockSpec(s, lambda j: (0, 0))
    col = pl.BlockSpec((D, FF_BLOCK), lambda j: (0, j))
    half_col = pl.BlockSpec((D // 2, FF_BLOCK), lambda j: (0, j))
    row = pl.BlockSpec((FF_BLOCK, D), lambda j: (j, 0))
    return pl.pallas_call(
        feed_kernel,
        name="feed",
        grid=(turns,),
        in_specs=[
            fixed((rows, D)),
            fixed((D, rows)),
            fixed((D, rows)),
            fixed((rows, D)),
            col,
            col,
            row,
            fixed((rows, D)),
        ],
        out_specs=[fixed((rows, D)), fixed((rows, D))] + [half_col] * 4 + [row],
        out_shape=[
            jax.ShapeDtypeStruct((rows, D), F32),
            jax.ShapeDtypeStruct((rows, D), F32),
        ]
        + [jax.ShapeDtypeStruct((D // 2, width), BF16)] * 4
        + [jax.ShapeDtypeStruct((width, D), BF16)],
        compiler_params=params(60),
        cost_estimate=pl.CostEstimate(
            flops=18 * rows * D * width, transcendentals=rows * width, bytes_accessed=12 * D * width
        ),
    )(a, at_gate, at_up, g, w_gate, w_up, w_down, y)


def rms_scale(v):
    return lax.rsqrt(jnp.mean(v * v, axis=-1, keepdims=True) + NORM_EPS)


def rms_back(v, scale, gain_row, d_out):
    w = d_out * gain_row
    n = v * scale
    d_v = scale * (w - n * jnp.mean(w * n, axis=-1, keepdims=True))
    return d_v, jnp.sum(d_out * n, axis=0)


def adam_update(master, first_moment, second_moment, gradient, rate, decay):
    first_moment = BETA_ONE * first_moment + (1.0 - BETA_ONE) * gradient
    second_moment = BETA_TWO * second_moment + (1.0 - BETA_TWO) * gradient * gradient
    corrected = (
        first_moment
        / (1.0 - BETA_ONE**STEP)
        / (jnp.sqrt(second_moment / (1.0 - BETA_TWO**STEP)) + ADAM_EPS)
    )
    return (master - rate * (corrected + decay * master), first_moment, second_moment)


def rotation_tables(position):
    half = HEAD_SIZE // 2
    index_row = jnp.arange(half, dtype=F32)
    frequency = jnp.exp(index_row * (-2.0 * math.log(ROPE_BASE) / HEAD_SIZE))
    angles = position.astype(F32)[:, None] * frequency[None, :]
    cosine, sine = jnp.cos(angles), jnp.sin(angles)
    return (
        jnp.concatenate([cosine] * 4, axis=1),
        jnp.concatenate([-sine, sine, -sine, sine], axis=1),
    )


ALL = ("fsdp", "seq")


def gather(shard):
    return lax.all_gather(shard, ALL, axis=0, tiled=True)


def dims():
    rest = lax.axis_size("fsdp") // 8
    return {
        "z": ("fsdp", 2 * rest, 4),
        "y": ("fsdp", 2, rest),
        "c": ("fsdp", 1, 2),
        "x": ("seq", 1, lax.axis_size("seq")),
    }


def place_along(direction):
    axis, stride, size = dims()[direction]
    return lax.rem(lax.div(lax.axis_index(axis), stride), size)


def swap(value, direction, distance):
    axis, stride, _ = dims()[direction]
    pairs = [(i, i ^ (distance * stride)) for i in range(lax.axis_size(axis))]
    return lax.ppermute(value, axis, pairs)


def relative_rows(order, count):
    sizes = {k: v[2] for k, v in dims().items()}
    width = count
    for size in sizes.values():
        width //= size
    index = jnp.arange(count, dtype=jnp.int32)
    left = index // width
    place = {}
    for k in reversed(order):
        place[k] = jnp.bitwise_xor(left % sizes[k], place_along(k))
        left = left // sizes[k]
    block = jnp.zeros_like(index)
    for k in "zycx":
        block = block * sizes[k] + place[k]
    row = block * width + index % width
    return (row[:, None] == index[None, :]).astype(BF16)


def transpose_in_order(hot, value):
    return dot_cols(hot, value).astype(BF16)


MESH = pl.DeviceIdType.MESH
NAMES = "zycx"


def neighbour(direction, distance):
    axis, stride, _ = dims()[direction]
    here = place_along(direction)
    return {axis: lax.axis_index(axis) + (jnp.bitwise_xor(here, distance) - here) * stride}


def greet():
    barrier = pltpu.get_barrier_semaphore()
    count = 0
    for k in NAMES:
        for d in range(1, dims()[k][2]):
            pl.semaphore_signal(barrier, 1, device_id=neighbour(k, d), device_id_type=MESH)
            count += 1
    pl.semaphore_wait(barrier, count)


def part_view(full, at, columns):
    index = tuple(at[k] if k in at else slice(None) for k in NAMES)
    return full.at[index + (slice(None), columns)]


def gather_kernel(plan, *refs):
    count = 1 + max(p[0] for p in plan)
    shards, fulls = refs[:count], refs[count : 2 * count]
    local, send, recv = refs[2 * count :]
    here = {k: place_along(k) for k in NAMES}
    own = []
    for t in range(count):
        copy = pltpu.make_async_copy(shards[t], part_view(fulls[t], here, slice(None)), local.at[t])
        copy.start()
        own.append(copy)
    greet()
    posted = []

    def post(source, target, k, d):
        n = len(posted)
        copy = pltpu.make_async_remote_copy(
            source, target, send.at[n], recv.at[n], device_id=neighbour(k, d), device_id_type=MESH
        )
        copy.start()
        posted.append(copy)
        return copy

    coming = {}
    for when in range(len(plan) + 3):
        for step in range(4):
            p = when - step
            if not 0 <= p < len(plan):
                continue
            t, column, width, order = plan[p]
            columns = pl.ds(column, width)
            full = fulls[t]
            if step == 0:
                k = order[0]
                target = part_view(full, here, columns)
                coming[p, 0] = [
                    post(shards[t].at[:, columns], target, k, d) for d in range(1, dims()[k][2])
                ]
                continue
            if own[t] is not None:
                own[t].wait()
                own[t] = None
            for copy in coming[p, step - 1]:
                copy.wait_recv()
            at = {k: v for k, v in here.items() if k not in order[:step]}
            if step < 3:
                k = order[step]
                view = part_view(full, at, columns)
                coming[p, step] = [post(view, view, k, d) for d in range(1, dims()[k][2])]
                if step == 2:
                    coming[p, 3] = [post(view, view, "c", 1)]
            else:
                k = order[2]
                for d in range(1, dims()[k][2]):
                    view = part_view(full, {**at, k: jnp.bitwise_xor(here[k], d)}, columns)
                    coming[p, 3].append(post(view, view, "c", 1))
    for p in range(len(plan)):
        for copy in coming[p, 3]:
            copy.wait_recv()
    for copy in posted:
        copy.wait_send()


def plan_parts(arrays, cut):
    plan = []
    for t, shard in enumerate(arrays):
        pieces = max(1, shard.shape[1] // cut)
        width = shard.shape[1] // pieces
        for i in range(pieces):
            plan.append((t, i * width, width, "zxy" if len(plan) % 2 else "zyx"))
    return plan


def gather_all(shards, cut, number):
    plan = plan_parts(shards, cut)
    size = {k: dims()[k][2] for k in NAMES}
    total = sum(sum(size[k] - 1 for k in order) + size[order[2]] for _, _, _, order in plan)
    fulls = pl.pallas_call(
        functools.partial(gather_kernel, plan),
        name="gather_all",
        in_specs=[pl.BlockSpec(memory_space=pl.ANY)] * len(shards),
        out_specs=[pl.BlockSpec(memory_space=pl.ANY)] * len(shards),
        out_shape=[
            jax.ShapeDtypeStruct((*(size[k] for k in NAMES), *shard.shape), shard.dtype)
            for shard in shards
        ],
        scratch_shapes=[
            pltpu.SemaphoreType.DMA((len(shards),)),
            pltpu.SemaphoreType.DMA((total,)),
            pltpu.SemaphoreType.DMA((total,)),
        ],
        compiler_params=pltpu.CompilerParams(collective_id=number, has_side_effects=True),
    )(*shards)
    return [full.reshape(-1, full.shape[-1]) for full in fulls]


def after(values, earlier):
    return lax.optimization_barrier((values, earlier))[0]


def sum_everywhere(terms):
    for k, (_, _, size) in dims().items():
        d = 1
        while d < size:
            terms = terms + swap(terms, k, d)
            d *= 2
    return terms


def add_swapped(keep, send, direction):
    return (keep.astype(F32) + swap(send, direction, 1).astype(F32)).astype(BF16)


def add_along(terms, direction, last=False):
    size = dims()[direction][2]
    step = terms.shape[0] // size
    total = terms[:step].astype(F32)
    for d in range(1, size):
        total = total + swap(terms[d * step : (d + 1) * step], direction, d).astype(F32)
    return total if last else total.astype(BF16)


def own_part(terms, direction, last=False):
    at, here, size = NAMES.index(direction), place_along(direction), dims()[direction][2]
    total = lax.dynamic_slice_in_dim(terms, here, 1, at).astype(F32)
    for d in range(1, size):
        sent = lax.dynamic_slice_in_dim(terms, jnp.bitwise_xor(here, d), 1, at)
        total = total + swap(sent, direction, d).astype(F32)
    return total if last else total.astype(BF16)


def per_device(
    inputs,
    cotangent,
    lengths,
    norm_gains,
    norm_first,
    norm_second,
    qk_gains,
    qk_first,
    qk_second,
    qkv_master,
    qkv_first,
    qkv_second,
    out_master,
    out_first,
    out_second,
    gate_up_master,
    gate_up_first,
    gate_up_second,
    down_master,
    down_first,
    down_second,
):
    seq_width = lax.axis_size("seq")
    turn_here = lax.axis_index("seq")
    rows = inputs.shape[1]
    block = min(QUERY_BLOCK, rows)
    w_qkv, w_out = gather_all([qkv_master.astype(BF16), out_master.astype(BF16)], 512, 1)
    w_down = gather(after(down_master.astype(BF16), w_qkv))

    places = turn_here * rows + jnp.arange(rows, dtype=jnp.int32)
    row_lengths = lengths[0]
    doc_ends = jnp.cumsum(row_lengths)
    passed = doc_ends[None, :] <= places[:, None]
    begins = jnp.sum(jnp.where(passed, row_lengths[None, :], 0), axis=1)
    cosine, sine = rotation_tables(places - begins)
    if seq_width == 2:
        base = (turn_here - 1) * rows
    else:
        base = turn_here * 0
    first = (begins - base).astype(jnp.int32)
    low = jnp.concatenate([(turn_here * rows - base)[None], first[::block]]).astype(jnp.int32)
    first_wide = jnp.broadcast_to(first[:, None], (rows, LANES))
    first_lane = jnp.broadcast_to(first[None, :], (8, rows))

    x = inputs[0].astype(F32)
    scale_first = rms_scale(x)
    normed_first = (x * scale_first * norm_gains[0]).astype(BF16)
    raw = jnp.dot(normed_first, w_qkv, preferred_element_type=F32)
    gain_rows = jnp.pad(jnp.tile(qk_gains, (1, 2)), ((0, 6), (0, 0)))
    q, *own = prep(raw, gain_rows, cosine, sine)
    pieces = range(PIECES)
    if seq_width == 2:
        others = [lax.ppermute(p, "seq", [(0, 1)]) for p in own]
    else:
        others = [lax.all_gather(p, "seq", axis=0, tiled=True) for p in own]
    mixes, lses = zip(*[attend(p, q, others[p], own[p], low, first_wide) for p in pieces])
    mixed = jnp.concatenate(mixes, axis=1)
    x_mid = x + jnp.dot(mixed, w_out, preferred_element_type=F32)
    scale_second = rms_scale(x_mid)
    normed_second = (x_mid * scale_second * norm_gains[1]).astype(BF16)
    g = cotangent[0]
    w_gate, w_up = gather_all(
        after([gate_up_master[:, :FF].astype(BF16), gate_up_master[:, FF:].astype(BF16)], normed_second),
        1152,
        2,
    )
    hot_x, hot_y = relative_rows("cxyz", D), relative_rows("cyxz", D)
    out_sum, d_b, gate_keep, gate_send, up_keep, up_send, grad_down = feed(
        normed_second,
        transpose_in_order(hot_x, normed_second),
        transpose_in_order(hot_y, normed_second),
        g,
        w_gate,
        w_up,
        w_down,
        x_mid,
    )
    outputs = out_sum.astype(BF16)
    gate_1 = add_swapped(gate_keep, gate_send, "c")
    up_1 = add_swapped(up_keep, up_send, "c")
    sizes = [dims()[k][2] for k in NAMES]
    down_1 = own_part(grad_down.reshape(*sizes, FF // math.prod(sizes), D), "c")
    d_norm, d_gain_second = rms_back(x_mid, scale_second, norm_gains[1], d_b)
    d_mid = g.astype(F32) + d_norm
    d_attn = d_mid.astype(BF16)
    d_mixed = dot_cols(d_attn, w_out).astype(BF16)
    out_terms = transpose_in_order(hot_y, mixed)
    half = QUERY_FEATURES // 2
    out_1 = add_swapped(
        dot(out_terms[:half], d_attn).astype(BF16), dot(out_terms[half:], d_attn).astype(BF16), "c"
    )

    def back_piece(p, earlier):
        d = after(d_mixed, earlier)
        return attend_back(p, q, d, mixes[p], lses[p], others[p], own[p], low, first_lane)

    parts = [back_piece(0, (gate_1, up_1))]
    parts.append(back_piece(1, (out_1, down_1)))
    gate_2, up_2 = add_along(gate_1, "x"), add_along(up_1, "y")
    parts.append(back_piece(2, (gate_2, up_2)))
    gate_3, up_3 = add_along(gate_2, "y"), add_along(up_2, "x")
    down_2, out_2 = own_part(down_1, "x"), add_along(out_1, "y")
    parts.append(back_piece(3, (gate_3, up_3)))
    gate_grad, up_grad = add_along(gate_3, "z", True), add_along(up_3, "z", True)
    down_3, out_3 = own_part(down_2, "y"), add_along(out_2, "x")
    down_grad, out_grad = own_part(down_3, "z", True), add_along(out_3, "z", True)
    down_grad = down_grad.reshape(-1, D)
    dq, far, near = zip(*parts)
    if seq_width == 2:
        back = [lax.ppermute(p, "seq", [(1, 0)]) for p in far]
    else:
        back = [lax.psum_scatter(p, "seq", scatter_dimension=0, tiled=True) for p in far]
    d_qkv, d_gain_qk = prep_back(raw, gain_rows, cosine, sine, dq, near, back)
    first_terms = transpose_in_order(hot_x, normed_first)
    qkv_1 = add_swapped(
        dot(first_terms[: D // 2], d_qkv).astype(BF16), dot(first_terms[D // 2 :], d_qkv).astype(BF16), "c"
    )
    qkv_grad = add_along(add_along(add_along(qkv_1, "x"), "y"), "z", True)
    d_a = dot_cols(d_qkv, w_qkv)
    d_x, d_gain_first = rms_back(x, scale_first, norm_gains[0], d_a)
    input_grad = (d_mid + d_x)[None]
    gain_terms = jnp.pad(d_gain_qk[:2], ((0, 0), (0, D - LANES)))
    gain_terms = jnp.concatenate([d_gain_first[None], d_gain_second[None], gain_terms], axis=0)
    gain_sums = sum_everywhere(jnp.pad(gain_terms, ((0, 4), (0, 0))))
    norm_grad = gain_sums[:2]
    qk_grad = gain_sums[2:4, :HEAD_SIZE] + gain_sums[2:4, HEAD_SIZE:LANES]

    norm_new = adam_update(norm_gains, norm_first, norm_second, norm_grad, GAIN_RATE, 0.0)
    qk_new = adam_update(qk_gains, qk_first, qk_second, qk_grad, GAIN_RATE, 0.0)
    qkv_new = adam_update(qkv_master, qkv_first, qkv_second, qkv_grad, D**-0.5, DECAY_RATE)
    out_new = adam_update(
        out_master, out_first, out_second, out_grad, (QUERY_FEATURES // 16) ** -0.5, DECAY_RATE
    )
    gate_up_grad = jnp.concatenate([gate_grad, up_grad], axis=1)
    gate_new = adam_update(
        gate_up_master, gate_up_first, gate_up_second, gate_up_grad, D**-0.5, DECAY_RATE
    )
    down_new = adam_update(down_master, down_first, down_second, down_grad, FF**-0.5, DECAY_RATE)
    return (
        outputs[None],
        input_grad,
        *norm_new,
        *qk_new,
        *qkv_new,
        *out_new,
        *gate_new,
        *down_new,
    )


def solution(mesh):
    token = P("fsdp", "seq", None)
    weight = P(ALL, None)
    return jax.shard_map(
        per_device,
        mesh=mesh,
        in_specs=(token, token, P("fsdp", None)) + (P(),) * 6 + (weight,) * 12,
        out_specs=(token, token) + (P(),) * 6 + (weight,) * 12,
        check_vma=False,
    )
```

```python
import functools
import math

import jax
import jax.numpy as jnp
from jax import lax
from jax.experimental import pallas as pl
from jax.experimental.pallas import tpu as pltpu
from jax.sharding import PartitionSpec as P

D = 1024
HQ = 16
KEY_VALUE_HEADS = 8
HEAD_SIZE = 64
FF = 4608
QUERY_FEATURES = 1024
KEY_FEATURES = 512
STEP = 10
LANES = 128

NORM_EPS = 1e-05
ROPE_BASE = 1000000.0
BETA_ONE = 0.9
BETA_TWO = 0.95
ADAM_EPS = 1e-08
DECAY_RATE = 0.1
GAIN_RATE = 0.3

F32 = jnp.float32
BF16 = jnp.bfloat16
QUERY_BLOCK = 256
KEY_BLOCK = 256
FF_BLOCK = 256
PIECES = 4


def dot(a, b):
    return lax.dot_general(a, b, (((1,), (0,)), ((), ())), preferred_element_type=F32)


def dot_cols(a, b):
    return lax.dot_general(a, b, (((1,), (1,)), ((), ())), preferred_element_type=F32)


def dot_rows(a, b):
    return lax.dot_general(a, b, (((0,), (0,)), ((), ())), preferred_element_type=F32)


def params(limit=56):
    return pltpu.CompilerParams(vmem_limit_bytes=limit << 20)


def head_mean(v):
    row = lax.broadcasted_iota(jnp.int32, (LANES, LANES), 0) // HEAD_SIZE
    col = lax.broadcasted_iota(jnp.int32, (LANES, LANES), 1) // HEAD_SIZE
    ones = jnp.where(row == col, 1.0 / HEAD_SIZE, 0.0).astype(BF16)
    high = v.astype(BF16)
    low = (v - high.astype(F32)).astype(BF16)
    return dot(high, ones) + dot(low, ones)


def swap_halves(v):
    lane = lax.broadcasted_iota(jnp.int32, v.shape, 1) % HEAD_SIZE
    return jnp.where(
        lane < HEAD_SIZE // 2,
        pltpu.roll(v, LANES - HEAD_SIZE // 2, 1),
        pltpu.roll(v, HEAD_SIZE // 2, 1),
    )


def prep_kernel(raw_ref, gain_ref, cos_ref, sin_ref, q_ref, *kv_refs):
    cosine, sine = cos_ref[...], sin_ref[...]
    for group in range(12):
        part = slice(group * LANES, (group + 1) * LANES)
        u = raw_ref[:, part]
        gain = gain_ref[0:1] if group < 8 else gain_ref[1:2]
        n = u * lax.rsqrt(head_mean(u * u) + NORM_EPS) * gain
        out = n * cosine + swap_halves(n) * sine
        if group < 8:
            q_ref[:, part] = (out * HEAD_SIZE**-0.5).astype(BF16)
        else:
            kv_ref = kv_refs[group - 8]
            kv_ref[:, :LANES] = out.astype(BF16)
            value = raw_ref[:, slice((group + 4) * LANES, (group + 5) * LANES)]
            kv_ref[:, LANES:] = value.astype(BF16)


def prep(raw, gains, cosine, sine):
    rows = raw.shape[0]
    block = min(rows, 256)
    whole = lambda width: pl.BlockSpec((block, width), lambda i: (i, 0))
    return pl.pallas_call(
        prep_kernel,
        name="prep",
        grid=(rows // block,),
        in_specs=[whole(2048), pl.BlockSpec((8, LANES), lambda i: (0, 0)), whole(LANES), whole(LANES)],
        out_specs=[whole(QUERY_FEATURES)] + [whole(2 * LANES)] * PIECES,
        out_shape=[jax.ShapeDtypeStruct((rows, QUERY_FEATURES), BF16)]
        + [jax.ShapeDtypeStruct((rows, 2 * LANES), BF16)] * PIECES,
        compiler_params=params(),
        cost_estimate=pl.CostEstimate(
            flops=rows * 2048 * 40, transcendentals=rows * 24, bytes_accessed=rows * 2048 * 6
        ),
    )(raw, gains, cosine, sine)


def prep_back_kernel(raw_ref, gain_ref, cos_ref, sin_ref, *rest):
    dq_refs, own_refs, back_refs = (rest[PIECES * i : PIECES * (i + 1)] for i in range(3))
    out_ref, dg_ref = rest[3 * PIECES :]
    cosine, sine = cos_ref[...], sin_ref[...]
    sums = [jnp.zeros((1, LANES), F32), jnp.zeros((1, LANES), F32)]
    for group in range(12):
        part = slice(group * LANES, (group + 1) * LANES)
        u = raw_ref[:, part]
        which = 0 if group < 8 else 1
        gain = gain_ref[which : which + 1]
        if group < 8:
            half = slice(group % 2 * LANES, (group % 2 + 1) * LANES)
            d = dq_refs[group // 2][:, half] * HEAD_SIZE**-0.5
        else:
            own, back = own_refs[group - 8], back_refs[group - 8]
            d = own[:, :LANES] + back[:, :LANES].astype(F32)
            value = slice((group + 4) * LANES, (group + 5) * LANES)
            out_ref[:, value] = (own[:, LANES:] + back[:, LANES:].astype(F32)).astype(BF16)
        d = d * cosine - swap_halves(d) * sine
        r = lax.rsqrt(head_mean(u * u) + NORM_EPS)
        w = d * gain
        n = u * r
        out_ref[:, part] = (r * (w - n * head_mean(w * n))).astype(BF16)
        sums[which] += jnp.sum(d * n, axis=0, keepdims=True)

    @pl.when(pl.program_id(0) == 0)
    def _():
        dg_ref[...] = jnp.zeros_like(dg_ref)

    dg_ref[0:1] += sums[0]
    dg_ref[1:2] += sums[1]


def prep_back(raw, gains, cosine, sine, dq, own, back):
    rows = raw.shape[0]
    block = min(rows, 256)
    whole = lambda width: pl.BlockSpec((block, width), lambda i: (i, 0))
    small = pl.BlockSpec((8, LANES), lambda i: (0, 0))
    return pl.pallas_call(
        prep_back_kernel,
        name="prep_back",
        grid=(rows // block,),
        in_specs=[
            whole(2048),
            small,
            whole(LANES),
            whole(LANES),
        ]
        + [whole(2 * LANES)] * (3 * PIECES),
        out_specs=[whole(2048), small],
        out_shape=[
            jax.ShapeDtypeStruct((rows, 2048), BF16),
            jax.ShapeDtypeStruct((8, LANES), F32),
        ],
        compiler_params=params(),
        cost_estimate=pl.CostEstimate(
            flops=rows * 2048 * 60, transcendentals=rows * 24, bytes_accessed=rows * 2048 * 10
        ),
    )(raw, gains, cosine, sine, *dq, *own, *back)


def twice(pair, odd):
    wide = pair.astype(F32)
    turned = pltpu.roll(wide, HEAD_SIZE, 1)
    lane = lax.broadcasted_iota(jnp.int32, wide.shape, 1)
    first = lane < HEAD_SIZE
    keep = first != (odd == 1)
    return jnp.where(keep, wide, turned).astype(BF16)


def stack_heads(pair):
    lane = lax.broadcasted_iota(jnp.int32, pair.shape, 1)
    zero = jnp.zeros_like(pair)
    return jnp.concatenate(
        [jnp.where(lane < HEAD_SIZE, pair, zero), jnp.where(lane < HEAD_SIZE, zero, pair)], axis=0
    )


def fill(head, others, own, lane_block, target):
    odd = lax.rem(head, 2)
    at = 0
    for source in (others, own):
        rows = source.shape[0]
        for start in range(0, rows, 256):
            target[at + start : at + start + 256, lane_block : lane_block + LANES] = twice(
                source[start : start + 256, :], odd
            )
        at += rows


def attend_kernel(
    low_ref,
    first_ref,
    q_ref,
    ko_ref,
    vo_ref,
    k_ref,
    v_ref,
    out_ref,
    lse_ref,
    keys,
    values,
):
    head, turn = pl.program_id(0), pl.program_id(1)
    block = q_ref.shape[0]
    tall = 2 * block

    @pl.when(turn == 0)
    def _():
        fill(head, ko_ref, k_ref, 0, keys)
        fill(head, vo_ref, v_ref, 0, values)
        values[:, LANES:] = jnp.ones((values.shape[0], LANES), BF16)

    queries = stack_heads(q_ref[...])
    place0 = low_ref[0] + turn * block
    place = place0 + lax.rem(lax.broadcasted_iota(jnp.int32, (tall, 1), 0), block)
    first = first_ref[:, 0:1]
    first = jnp.concatenate([first, first], axis=0)
    begin = low_ref[1 + turn] // KEY_BLOCK
    end = (place0 + block - 1) // KEY_BLOCK + 1

    def step(at, total):
        start = pl.multiple_of(at * KEY_BLOCK, KEY_BLOCK)
        scores = dot_cols(queries, keys[pl.ds(start, KEY_BLOCK), :])
        key_place = start + lax.broadcasted_iota(jnp.int32, (tall, KEY_BLOCK), 1)
        allowed = (key_place >= first) & (key_place <= place)
        powers = jnp.where(allowed, jnp.exp(scores), 0.0).astype(BF16)
        return total + dot(powers, values[pl.ds(start, KEY_BLOCK), :])

    total = lax.fori_loop(begin, end, step, jnp.zeros((tall, 2 * LANES), F32))
    mass = total[:, LANES:]
    mixed = total[:, :LANES] / mass
    lane = lax.broadcasted_iota(jnp.int32, (block, LANES), 1)
    out_ref[...] = jnp.where(lane < HEAD_SIZE, mixed[:block], mixed[block:]).astype(BF16)
    logs = jnp.log(mass)
    lse_ref[0] = jnp.transpose(logs)[0:8, :]


def attend(piece, q, others, own, low, first):
    rows = q.shape[0]
    block = min(QUERY_BLOCK, rows)
    turns = rows // block
    total = others.shape[0] + rows
    pair = lambda size, off: pl.BlockSpec((size, LANES), lambda h, t, low: (0, off))
    return pl.pallas_call(
        attend_kernel,
        name="attend",
        grid_spec=pltpu.PrefetchScalarGridSpec(
            num_scalar_prefetch=1,
            grid=(2, turns),
            in_specs=[
                pl.BlockSpec((block, LANES), lambda h, t, low: (t, 0)),
                pl.BlockSpec((block, LANES), lambda h, t, low: (t, 2 * piece + h)),
                pair(others.shape[0], 0),
                pair(others.shape[0], 1),
                pair(rows, 0),
                pair(rows, 1),
            ],
            out_specs=[
                pl.BlockSpec((block, LANES), lambda h, t, low: (t, h)),
                pl.BlockSpec((1, 8, 2 * block), lambda h, t, low: (h, t, 0)),
            ],
            scratch_shapes=[pltpu.VMEM((total, LANES), BF16), pltpu.VMEM((total, 2 * LANES), BF16)],
        ),
        out_shape=[
            jax.ShapeDtypeStruct((rows, 2 * LANES), BF16),
            jax.ShapeDtypeStruct((2, 8 * turns, 2 * block), F32),
        ],
        compiler_params=params(),
        cost_estimate=pl.CostEstimate(
            flops=rows * 1024 * 1024 * 8, transcendentals=rows * 1024 * 4, bytes_accessed=4 << 20
        ),
    )(low, first, q, others, others, own, own)


def attend_back_kernel(
    low_ref,
    first_ref,
    q_ref,
    do_ref,
    mixed_ref,
    lse_ref,
    ko_ref,
    vo_ref,
    k_ref,
    v_ref,
    dq_ref,
    far_ref,
    near_ref,
    keys,
    values,
    dkeys,
    dvalues,
):
    head, turn = pl.program_id(0), pl.program_id(1)
    block = q_ref.shape[0]
    tall = 2 * block

    @pl.when(turn == 0)
    def _():
        fill(head, ko_ref, k_ref, 0, keys)
        fill(head, vo_ref, v_ref, 0, values)
        dkeys[...] = jnp.zeros_like(dkeys)
        dvalues[...] = jnp.zeros_like(dvalues)

    queries = stack_heads(q_ref[...])
    rising = stack_heads(do_ref[...])
    across = jnp.transpose(do_ref[...].astype(F32) * mixed_ref[...].astype(F32))
    delta = jnp.concatenate(
        [
            jnp.sum(across[:HEAD_SIZE], axis=0, keepdims=True),
            jnp.sum(across[HEAD_SIZE:], axis=0, keepdims=True),
        ],
        axis=1,
    )
    logs = lse_ref[0][0:1]
    place0 = low_ref[0] + turn * block
    place = place0 + lax.rem(lax.broadcasted_iota(jnp.int32, (1, tall), 1), block)
    first = first_ref[0:1]
    first = jnp.concatenate([first, first], axis=1)
    begin = low_ref[1 + turn] // KEY_BLOCK
    end = (place0 + block - 1) // KEY_BLOCK + 1

    def step(at, dq):
        start = pl.multiple_of(at * KEY_BLOCK, KEY_BLOCK)
        span = pl.ds(start, KEY_BLOCK)
        key = keys[span, :]
        scores = dot_cols(key, queries)
        key_place = start + lax.broadcasted_iota(jnp.int32, (KEY_BLOCK, tall), 0)
        allowed = (key_place >= first) & (key_place <= place)
        probs = jnp.where(allowed, jnp.exp(scores - logs), 0.0)
        dprobs = dot_cols(values[span, :], rising)
        dscores = (probs * (dprobs - delta)).astype(BF16)
        dkeys[span, :] += dot(dscores, queries)
        dvalues[span, :] += dot(probs.astype(BF16), rising)
        return dq + dot_rows(dscores, key)

    dq = lax.fori_loop(begin, end, step, jnp.zeros((tall, LANES), F32))
    lane = lax.broadcasted_iota(jnp.int32, (block, LANES), 1)
    dq_ref[...] = jnp.where(lane < HEAD_SIZE, dq[:block], dq[block:])

    @pl.when(turn == pl.num_programs(1) - 1)
    def _():
        odd = lax.rem(head, 2)
        far = far_ref.shape[0]
        for source, off in ((dkeys, 0), (dvalues, LANES)):
            for start in range(0, source.shape[0], 256):
                both = source[start : start + 256, :]
                both = both + pltpu.roll(both, HEAD_SIZE, 1)
                lane = lax.broadcasted_iota(jnp.int32, both.shape, 1)
                mine = (lane < HEAD_SIZE) != (odd == 1)
                target, to = (far_ref, start) if start < far else (near_ref, start - far)
                part = (slice(to, to + 256), slice(off, off + LANES))

                @pl.when(odd == 0)
                def _():
                    target[part] = both.astype(target.dtype)

                @pl.when(odd == 1)
                def _():
                    target[part] = jnp.where(mine, both, target[part].astype(F32)).astype(target.dtype)


def attend_back(piece, q, d_mixed, mixed, lse, others, own, low, first_lane):
    rows = q.shape[0]
    block = min(QUERY_BLOCK, rows)
    turns = rows // block
    total = others.shape[0] + rows
    pair = lambda size, off: pl.BlockSpec((size, LANES), lambda h, t, low: (0, off))
    whole = lambda size: pl.BlockSpec((size, 2 * LANES), lambda h, t, low: (0, 0))
    tile = pl.BlockSpec((block, LANES), lambda h, t, low: (t, h))
    tile_of_all = pl.BlockSpec((block, LANES), lambda h, t, low: (t, 2 * piece + h))
    return pl.pallas_call(
        attend_back_kernel,
        name="attend_back",
        grid_spec=pltpu.PrefetchScalarGridSpec(
            num_scalar_prefetch=1,
            grid=(2, turns),
            in_specs=[
                pl.BlockSpec((8, block), lambda h, t, low: (0, t)),
                tile_of_all,
                tile_of_all,
                tile,
                pl.BlockSpec((1, 8, 2 * block), lambda h, t, low: (h, t, 0)),
                pair(others.shape[0], 0),
                pair(others.shape[0], 1),
                pair(rows, 0),
                pair(rows, 1),
            ],
            out_specs=[tile, whole(others.shape[0]), whole(rows)],
            scratch_shapes=[
                pltpu.VMEM((total, LANES), BF16),
                pltpu.VMEM((total, LANES), BF16),
                pltpu.VMEM((total, LANES), F32),
                pltpu.VMEM((total, LANES), F32),
            ],
        ),
        out_shape=[
            jax.ShapeDtypeStruct((rows, 2 * LANES), F32),
            jax.ShapeDtypeStruct((others.shape[0], 2 * LANES), BF16),
            jax.ShapeDtypeStruct((rows, 2 * LANES), F32),
        ],
        compiler_params=params(),
        cost_estimate=pl.CostEstimate(
            flops=rows * 1024 * 1024 * 12, transcendentals=rows * 1024 * 4, bytes_accessed=10 << 20
        ),
    )(low, first_lane, q, d_mixed, mixed, lse, others, others, own, own)


def rms_scale(v):
    return lax.rsqrt(jnp.mean(v * v, axis=-1, keepdims=True) + NORM_EPS)


def rms_back(v, scale, gain_row, d_out):
    w = d_out * gain_row
    n = v * scale
    d_v = scale * (w - n * jnp.mean(w * n, axis=-1, keepdims=True))
    return d_v, jnp.sum(d_out * n, axis=0)


def adam_update(master, first_moment, second_moment, gradient, rate, decay):
    first_moment = BETA_ONE * first_moment + (1.0 - BETA_ONE) * gradient
    second_moment = BETA_TWO * second_moment + (1.0 - BETA_TWO) * gradient * gradient
    corrected = (
        first_moment
        / (1.0 - BETA_ONE**STEP)
        / (jnp.sqrt(second_moment / (1.0 - BETA_TWO**STEP)) + ADAM_EPS)
    )
    return (master - rate * (corrected + decay * master), first_moment, second_moment)


def rotation_tables(position):
    half = HEAD_SIZE // 2
    index_row = jnp.arange(half, dtype=F32)
    frequency = jnp.exp(index_row * (-2.0 * math.log(ROPE_BASE) / HEAD_SIZE))
    angles = position.astype(F32)[:, None] * frequency[None, :]
    cosine, sine = jnp.cos(angles), jnp.sin(angles)
    return (
        jnp.concatenate([cosine] * 4, axis=1),
        jnp.concatenate([-sine, sine, -sine, sine], axis=1),
    )


ALL = ("fsdp", "seq")


def gather(shard):
    return lax.all_gather(shard, ALL, axis=0, tiled=True)


def dims():
    rest = lax.axis_size("fsdp") // 8
    return {
        "z": ("fsdp", 2 * rest, 4),
        "y": ("fsdp", 2, rest),
        "c": ("fsdp", 1, 2),
        "x": ("seq", 1, lax.axis_size("seq")),
    }


def place_along(direction):
    axis, stride, size = dims()[direction]
    return lax.rem(lax.div(lax.axis_index(axis), stride), size)


def swap(value, direction, distance):
    axis, stride, _ = dims()[direction]
    pairs = [(i, i ^ (distance * stride)) for i in range(lax.axis_size(axis))]
    return lax.ppermute(value, axis, pairs)


def relative_rows(order, count):
    sizes = {k: v[2] for k, v in dims().items()}
    width = count
    for size in sizes.values():
        width //= size
    index = jnp.arange(count, dtype=jnp.int32)
    left = index // width
    place = {}
    for k in reversed(order):
        place[k] = jnp.bitwise_xor(left % sizes[k], place_along(k))
        left = left // sizes[k]
    block = jnp.zeros_like(index)
    for k in "zycx":
        block = block * sizes[k] + place[k]
    row = block * width + index % width
    return (row[:, None] == index[None, :]).astype(BF16)


def transpose_in_order(hot, value):
    return dot_cols(hot, value).astype(BF16)


MESH = pl.DeviceIdType.MESH
NAMES = "zycx"


def neighbour(direction, distance):
    axis, stride, _ = dims()[direction]
    here = place_along(direction)
    return {axis: lax.axis_index(axis) + (jnp.bitwise_xor(here, distance) - here) * stride}


def greet():
    barrier = pltpu.get_barrier_semaphore()
    count = 0
    for k in NAMES:
        for d in range(1, dims()[k][2]):
            pl.semaphore_signal(barrier, 1, device_id=neighbour(k, d), device_id_type=MESH)
            count += 1
    pl.semaphore_wait(barrier, count)


def part_view(full, at, columns):
    index = tuple(at[k] if k in at else slice(None) for k in NAMES)
    return full.at[index + (slice(None), columns)]


def gather_kernel(plan, *refs):
    count = 1 + max(p[0] for p in plan)
    shards, fulls = refs[:count], refs[count : 2 * count]
    local, send, recv = refs[2 * count :]
    here = {k: place_along(k) for k in NAMES}
    own = []
    for t in range(count):
        copy = pltpu.make_async_copy(shards[t], part_view(fulls[t], here, slice(None)), local.at[t])
        copy.start()
        own.append(copy)
    greet()
    posted = []

    def post(source, target, k, d):
        n = len(posted)
        copy = pltpu.make_async_remote_copy(
            source, target, send.at[n], recv.at[n], device_id=neighbour(k, d), device_id_type=MESH
        )
        copy.start()
        posted.append(copy)
        return copy

    coming = {}
    for when in range(len(plan) + 3):
        for step in range(4):
            p = when - step
            if not 0 <= p < len(plan):
                continue
            t, column, width, order = plan[p]
            columns = pl.ds(column, width)
            full = fulls[t]
            if step == 0:
                k = order[0]
                target = part_view(full, here, columns)
                coming[p, 0] = [
                    post(shards[t].at[:, columns], target, k, d) for d in range(1, dims()[k][2])
                ]
                continue
            if own[t] is not None:
                own[t].wait()
                own[t] = None
            for copy in coming[p, step - 1]:
                copy.wait_recv()
            at = {k: v for k, v in here.items() if k not in order[:step]}
            if step < 3:
                k = order[step]
                view = part_view(full, at, columns)
                coming[p, step] = [post(view, view, k, d) for d in range(1, dims()[k][2])]
                if step == 2:
                    coming[p, 3] = [post(view, view, "c", 1)]
            else:
                k = order[2]
                for d in range(1, dims()[k][2]):
                    view = part_view(full, {**at, k: jnp.bitwise_xor(here[k], d)}, columns)
                    coming[p, 3].append(post(view, view, "c", 1))
    for p in range(len(plan)):
        for copy in coming[p, 3]:
            copy.wait_recv()
    for copy in posted:
        copy.wait_send()


def plan_parts(arrays, cut):
    plan = []
    for t, shard in enumerate(arrays):
        pieces = max(1, shard.shape[1] // cut)
        width = shard.shape[1] // pieces
        for i in range(pieces):
            plan.append((t, i * width, width, "zxy" if len(plan) % 2 else "zyx"))
    return plan


def gather_all(shards, cut, number):
    plan = plan_parts(shards, cut)
    size = {k: dims()[k][2] for k in NAMES}
    total = sum(sum(size[k] - 1 for k in order) + size[order[2]] for _, _, _, order in plan)
    fulls = pl.pallas_call(
        functools.partial(gather_kernel, plan),
        name="gather_all",
        in_specs=[pl.BlockSpec(memory_space=pl.ANY)] * len(shards),
        out_specs=[pl.BlockSpec(memory_space=pl.ANY)] * len(shards),
        out_shape=[
            jax.ShapeDtypeStruct((*(size[k] for k in NAMES), *shard.shape), shard.dtype)
            for shard in shards
        ],
        scratch_shapes=[
            pltpu.SemaphoreType.DMA((len(shards),)),
            pltpu.SemaphoreType.DMA((total,)),
            pltpu.SemaphoreType.DMA((total,)),
        ],
        compiler_params=pltpu.CompilerParams(collective_id=number, has_side_effects=True),
    )(*shards)
    return [full.reshape(-1, full.shape[-1]) for full in fulls]


def after(values, earlier):
    return lax.optimization_barrier((values, earlier))[0]


def sum_everywhere(terms):
    for k, (_, _, size) in dims().items():
        d = 1
        while d < size:
            terms = terms + swap(terms, k, d)
            d *= 2
    return terms


FEED_LEAD = 4


def feed_kernel(
    shard_ref,
    a_ref,
    at_ref,
    g_ref,
    start_ref,
    wd_ref,
    full_ref,
    y_ref,
    b_ref,
    gd_ref,
    sum_ref,
    weights,
    terms,
    total_1,
    total_2,
    total_3,
    got_c,
    got_1,
    got_2,
    got_z,
    load_sem,
    start_sem,
    own_sem,
    out_send,
    out_recv,
    in_send,
    in_recv,
):
    step = pl.program_id(0)
    width = weights.shape[-1]
    parts = shard_ref.shape[2] // width
    size = {k: v[2] for k, v in dims().items()}
    here = {k: place_along(k) for k in NAMES}
    shard_rows = shard_ref.shape[1]
    orders = ("xy", "yx")

    def columns(p):
        return pl.ds(pl.multiple_of(p * width, width), width)

    def view(which, at, p):
        index = tuple(at[k] if k in at else slice(None) for k in NAMES)
        return full_ref.at[(which,) + index + (slice(None), columns(p))]

    def remote(source, target, sems, p, n, k, d):
        send, recv = sems
        return pltpu.make_async_remote_copy(
            source,
            target,
            send.at[p, n],
            recv.at[p, n],
            device_id=neighbour(k, d),
            device_id_type=MESH,
        )

    def gather_copies(p, stage):
        sems = (out_send, out_recv)
        copies = []
        if stage == 0:
            for d in range(1, size["z"]):
                copies.append(
                    remote(shard_ref.at[:, :, columns(p)], view(slice(None), here, p), sems, p, d - 1, "z", d)
                )
            return copies
        slot = size["z"] - 1
        if stage == 3:
            slot += 2 * (size["x"] + size["y"] - 2)
            at = view(slice(None), {"c": here["c"]}, p)
            return [remote(at, at, sems, p, slot, "c", 1)]
        for which, order in enumerate(orders):
            for s in (1, 2):
                k = order[s - 1]
                gone = "z" + order[: s - 1]
                at = view(which, {q: v for q, v in here.items() if q not in gone}, p)
                for d in range(1, size[k]):
                    if s == stage:
                        copies.append(remote(at, at, sems, p, slot, k, d))
                    slot += 1
        return copies

    def scatter_copies(p, stage):
        sems = (in_send, in_recv)
        if stage == 0:
            return [remote(terms.at[lax.rem(p, 2), :, 1], got_c.at[p], sems, p, 0, "c", 1)]
        copies = []
        slot = 1
        for which, order in enumerate(orders):
            for s in (1, 2):
                k = order[s - 1]
                for d in range(1, size[k]):
                    if s == 1:
                        source = total_1.at[0, d] if k == "x" else total_1.at[1, :, d]
                    else:
                        source = total_2[which].at[d]
                    target = (got_1, got_2)[s - 1][which].at[p, d - 1]
                    if s == stage:
                        copies.append(remote(source, target, sems, p, slot, k, d))
                    slot += 1
        if stage == 3:
            for d in range(1, size["z"]):
                copies.append(remote(total_3.at[:, d], got_z.at[p, d - 1], sems, p, slot + d - 1, "z", d))
        return copies

    def own_copy():
        return pltpu.make_async_copy(shard_ref, full_ref.at[(slice(None),) + tuple(here[k] for k in NAMES)], own_sem)

    def load_copy(p):
        return pltpu.make_async_copy(
            full_ref.at[:, :, :, :, :, :, columns(p)], weights.at[lax.rem(p, 2)], load_sem.at[lax.rem(p, 2)]
        )

    def on(offset, run):
        p = step - offset

        @pl.when((p >= 0) & (p < parts))
        def _():
            run(p)

    @pl.when(step == 0)
    def _():
        own_copy().start()
        pltpu.make_async_copy(start_ref, y_ref, start_sem).start()
        greet()

        def begin(p, _):
            for copy in gather_copies(p, 0):
                copy.start()
            return 0

        lax.fori_loop(0, parts, begin, 0)
        own_copy().wait()
        pltpu.make_async_copy(start_ref, y_ref, start_sem).wait()
        b_ref[...] = jnp.zeros_like(b_ref)

    def pass_on(stage):
        def run(p):
            for copy in gather_copies(p, stage - 1):
                copy.wait_recv()
            for copy in gather_copies(p, stage):
                copy.start()

        return run

    def arrived(p):
        for copy in gather_copies(p, 3):
            copy.wait_recv()
        load_copy(p).start()

    on(3, arrived)
    on(2, pass_on(3))
    on(1, pass_on(2))
    on(0, pass_on(1))

    def finish(p):
        for copy in scatter_copies(p, 3):
            copy.wait()
        total = total_3[:, 0].astype(F32)
        for d in range(1, size["z"]):
            total = total + got_z[p, d - 1].astype(F32)
        sum_ref[:, :, columns(p)] = total

    def third(p):
        for copy in scatter_copies(p, 2):
            copy.wait()
        for which, order in enumerate(orders):
            total = total_2[which][0].astype(F32)
            for d in range(1, size[order[1]]):
                total = total + got_2[which][p, d - 1].astype(F32)
            total_3[which] = total.astype(BF16)
        for copy in scatter_copies(p, 3):
            copy.start()

    def second(p):
        for copy in scatter_copies(p, 1):
            copy.wait()
        for which, order in enumerate(orders):
            kept = total_1[0, 0] if order[0] == "x" else total_1[1, :, 0]
            total = kept.astype(F32)
            for d in range(1, size[order[0]]):
                total = total + got_1[which][p, d - 1].astype(F32)
            total_2[which][...] = total.astype(BF16)
        for copy in scatter_copies(p, 2):
            copy.start()

    def first(p):
        for copy in scatter_copies(p, 0):
            copy.wait()
        total = terms[lax.rem(p, 2), :, 0].astype(F32) + got_c[p].astype(F32)
        total_1[...] = total.astype(BF16)
        for copy in scatter_copies(p, 1):
            copy.start()

    on(FEED_LEAD + 4, finish)
    on(FEED_LEAD + 3, third)
    on(FEED_LEAD + 2, second)
    on(FEED_LEAD + 1, first)

    def compute(p):
        load_copy(p).wait()
        slot = lax.rem(p, 2)
        rows = D
        a, g, wd = a_ref[...], g_ref[...], wd_ref[...]
        wg = weights[slot, 0].reshape(rows, width)
        wu = weights[slot, 1].reshape(rows, width)
        gate = dot(a, wg)
        up = dot(a, wu)
        d_hidden = dot_cols(g, wd)
        sigma = 1.0 / (1.0 + jnp.exp(-gate))
        swish = gate * sigma
        hidden = (swish * up).astype(BF16)
        d_gate = (d_hidden * up * sigma * (1.0 + gate * (1.0 - sigma))).astype(BF16)
        d_up = (d_hidden * swish).astype(BF16)
        y_ref[...] += dot(hidden, wd)
        b_ref[...] += dot_cols(d_gate, wg) + dot_cols(d_up, wu)
        at = at_ref[...]
        shape = (2,) + total_1.shape[1:]
        terms[slot, 0] = dot(at, d_gate).astype(BF16).reshape(shape)
        terms[slot, 1] = dot(at, d_up).astype(BF16).reshape(shape)
        gd_ref[...] = dot_rows(hidden, g).astype(BF16)
        for copy in scatter_copies(p, 0):
            copy.start()

    on(FEED_LEAD, compute)

    @pl.when(step == pl.num_programs(0) - 1)
    def _():
        def end(p, _):
            for stage in range(4):
                for copy in gather_copies(p, stage):
                    copy.wait_send()
            return 0

        lax.fori_loop(0, parts, end, 0)


def feed(shards, a, at, g, w_down, start, number):
    rows = a.shape[0]
    size = {k: v[2] for k, v in dims().items()}
    _, shard_rows, width = shards.shape
    parts = width // FF_BLOCK
    x, y, z = size["x"], size["y"], size["z"]
    last = (z, shard_rows, FF_BLOCK)
    whole = pl.BlockSpec(memory_space=pltpu.VMEM)
    anywhere = pl.BlockSpec(memory_space=pl.ANY)
    row = pl.BlockSpec((FF_BLOCK, D), lambda t: (jnp.clip(t - FEED_LEAD, 0, parts - 1), 0))
    out_count = z - 1 + 2 * (x + y - 2) + 1
    in_count = 1 + 2 * (x + y - 2) + z - 1
    sems = pltpu.SemaphoreType.DMA
    _, y_sum, b_sum, grad_down, sums = pl.pallas_call(
        feed_kernel,
        name="feed",
        grid=(parts + FEED_LEAD + 4,),
        in_specs=[anywhere, whole, whole, whole, anywhere, row],
        out_specs=[anywhere, whole, whole, row, whole],
        out_shape=[
            jax.ShapeDtypeStruct((2, *(size[k] for k in NAMES), shard_rows, width), BF16),
            jax.ShapeDtypeStruct((rows, D), F32),
            jax.ShapeDtypeStruct((rows, D), F32),
            jax.ShapeDtypeStruct((width, D), BF16),
            jax.ShapeDtypeStruct((2, shard_rows, width), F32),
        ],
        scratch_shapes=[
            pltpu.VMEM((2, 2, *(size[k] for k in NAMES), shard_rows, FF_BLOCK), BF16),
            pltpu.VMEM((2, 2, 2, x, y, *last), BF16),
            pltpu.VMEM((2, x, y, *last), BF16),
            [pltpu.VMEM((y, *last), BF16), pltpu.VMEM((x, *last), BF16)],
            pltpu.VMEM((2, *last), BF16),
            pltpu.VMEM((parts, 2, x, y, *last), BF16),
            [pltpu.VMEM((parts, x - 1, y, *last), BF16), pltpu.VMEM((parts, y - 1, x, *last), BF16)],
            [pltpu.VMEM((parts, y - 1, *last), BF16), pltpu.VMEM((parts, x - 1, *last), BF16)],
            pltpu.VMEM((parts, z - 1, 2, shard_rows, FF_BLOCK), BF16),
            sems((2,)),
            sems,
            sems,
            sems((parts, out_count)),
            sems((parts, out_count)),
            sems((parts, in_count)),
            sems((parts, in_count)),
        ],
        compiler_params=pltpu.CompilerParams(
            collective_id=number, has_side_effects=True, vmem_limit_bytes=60 << 20
        ),
        cost_estimate=pl.CostEstimate(
            flops=18 * rows * D * width, transcendentals=rows * width, bytes_accessed=12 * D * width
        ),
    )(shards, a, at, g, start, w_down)
    return y_sum, b_sum, grad_down, sums


def add_swapped(keep, send, direction):
    return (keep.astype(F32) + swap(send, direction, 1).astype(F32)).astype(BF16)


def add_along(terms, direction, last=False):
    size = dims()[direction][2]
    step = terms.shape[0] // size
    total = terms[:step].astype(F32)
    for d in range(1, size):
        total = total + swap(terms[d * step : (d + 1) * step], direction, d).astype(F32)
    return total if last else total.astype(BF16)


def own_part(terms, direction, last=False):
    at, here, size = NAMES.index(direction), place_along(direction), dims()[direction][2]
    total = lax.dynamic_slice_in_dim(terms, here, 1, at).astype(F32)
    for d in range(1, size):
        sent = lax.dynamic_slice_in_dim(terms, jnp.bitwise_xor(here, d), 1, at)
        total = total + swap(sent, direction, d).astype(F32)
    return total if last else total.astype(BF16)


def per_device(
    inputs,
    cotangent,
    lengths,
    norm_gains,
    norm_first,
    norm_second,
    qk_gains,
    qk_first,
    qk_second,
    qkv_master,
    qkv_first,
    qkv_second,
    out_master,
    out_first,
    out_second,
    gate_up_master,
    gate_up_first,
    gate_up_second,
    down_master,
    down_first,
    down_second,
):
    seq_width = lax.axis_size("seq")
    turn_here = lax.axis_index("seq")
    rows = inputs.shape[1]
    block = min(QUERY_BLOCK, rows)
    w_qkv, w_out = gather_all([qkv_master.astype(BF16), out_master.astype(BF16)], 512, 1)
    w_down = gather(after(down_master.astype(BF16), w_qkv))

    places = turn_here * rows + jnp.arange(rows, dtype=jnp.int32)
    row_lengths = lengths[0]
    doc_ends = jnp.cumsum(row_lengths)
    passed = doc_ends[None, :] <= places[:, None]
    begins = jnp.sum(jnp.where(passed, row_lengths[None, :], 0), axis=1)
    cosine, sine = rotation_tables(places - begins)
    if seq_width == 2:
        base = (turn_here - 1) * rows
    else:
        base = turn_here * 0
    first = (begins - base).astype(jnp.int32)
    low = jnp.concatenate([(turn_here * rows - base)[None], first[::block]]).astype(jnp.int32)
    first_wide = jnp.broadcast_to(first[:, None], (rows, LANES))
    first_lane = jnp.broadcast_to(first[None, :], (8, rows))

    x = inputs[0].astype(F32)
    scale_first = rms_scale(x)
    normed_first = (x * scale_first * norm_gains[0]).astype(BF16)
    raw = jnp.dot(normed_first, w_qkv, preferred_element_type=F32)
    gain_rows = jnp.pad(jnp.tile(qk_gains, (1, 2)), ((0, 6), (0, 0)))
    q, *own = prep(raw, gain_rows, cosine, sine)
    pieces = range(PIECES)
    if seq_width == 2:
        others = [lax.ppermute(p, "seq", [(0, 1)]) for p in own]
    else:
        others = [lax.all_gather(p, "seq", axis=0, tiled=True) for p in own]
    mixes, lses = zip(*[attend(p, q, others[p], own[p], low, first_wide) for p in pieces])
    mixed = jnp.concatenate(mixes, axis=1)
    x_mid = x + jnp.dot(mixed, w_out, preferred_element_type=F32)
    scale_second = rms_scale(x_mid)
    normed_second = (x_mid * scale_second * norm_gains[1]).astype(BF16)
    g = cotangent[0]
    hot_x, hot_y = relative_rows("cxyz", D), relative_rows("cyxz", D)
    shards = jnp.stack([gate_up_master[:, :FF], gate_up_master[:, FF:]]).astype(BF16)
    out_sum, d_b, grad_down, gate_up_sums = feed(
        after(shards, normed_second),
        normed_second,
        transpose_in_order(hot_x, normed_second),
        g,
        w_down,
        x_mid,
        2,
    )
    outputs = out_sum.astype(BF16)
    sizes = [dims()[k][2] for k in NAMES]
    down_1 = own_part(grad_down.reshape(*sizes, FF // math.prod(sizes), D), "c")
    d_norm, d_gain_second = rms_back(x_mid, scale_second, norm_gains[1], d_b)
    d_mid = g.astype(F32) + d_norm
    d_attn = d_mid.astype(BF16)
    d_mixed = dot_cols(d_attn, w_out).astype(BF16)
    out_terms = transpose_in_order(hot_y, mixed)
    half = QUERY_FEATURES // 2
    out_1 = add_swapped(
        dot(out_terms[:half], d_attn).astype(BF16), dot(out_terms[half:], d_attn).astype(BF16), "c"
    )

    def back_piece(p, earlier):
        d = after(d_mixed, earlier)
        return attend_back(p, q, d, mixes[p], lses[p], others[p], own[p], low, first_lane)

    parts = [back_piece(0, (out_1, down_1))]
    down_2, out_2 = own_part(down_1, "x"), add_along(out_1, "y")
    parts.append(back_piece(1, out_2))
    out_3 = add_along(out_2, "x")
    parts.append(back_piece(2, (down_2, out_3)))
    down_3, out_grad = own_part(down_2, "y"), add_along(out_3, "z", True)
    parts.append(back_piece(3, (down_3, out_grad)))
    down_grad = own_part(down_3, "z", True).reshape(-1, D)
    dq, far, near = zip(*parts)
    if seq_width == 2:
        back = [lax.ppermute(p, "seq", [(1, 0)]) for p in far]
    else:
        back = [lax.psum_scatter(p, "seq", scatter_dimension=0, tiled=True) for p in far]
    d_qkv, d_gain_qk = prep_back(raw, gain_rows, cosine, sine, dq, near, back)
    first_terms = transpose_in_order(hot_x, normed_first)
    qkv_1 = add_swapped(
        dot(first_terms[: D // 2], d_qkv).astype(BF16), dot(first_terms[D // 2 :], d_qkv).astype(BF16), "c"
    )
    qkv_grad = add_along(add_along(add_along(qkv_1, "x"), "y"), "z", True)
    d_a = dot_cols(d_qkv, w_qkv)
    d_x, d_gain_first = rms_back(x, scale_first, norm_gains[0], d_a)
    input_grad = (d_mid + d_x)[None]
    gain_terms = jnp.pad(d_gain_qk[:2], ((0, 0), (0, D - LANES)))
    gain_terms = jnp.concatenate([d_gain_first[None], d_gain_second[None], gain_terms], axis=0)
    gain_sums = sum_everywhere(jnp.pad(gain_terms, ((0, 4), (0, 0))))
    norm_grad = gain_sums[:2]
    qk_grad = gain_sums[2:4, :HEAD_SIZE] + gain_sums[2:4, HEAD_SIZE:LANES]

    norm_new = adam_update(norm_gains, norm_first, norm_second, norm_grad, GAIN_RATE, 0.0)
    qk_new = adam_update(qk_gains, qk_first, qk_second, qk_grad, GAIN_RATE, 0.0)
    qkv_new = adam_update(qkv_master, qkv_first, qkv_second, qkv_grad, D**-0.5, DECAY_RATE)
    out_new = adam_update(
        out_master, out_first, out_second, out_grad, (QUERY_FEATURES // 16) ** -0.5, DECAY_RATE
    )
    gate_up_grad = jnp.concatenate([gate_up_sums[0], gate_up_sums[1]], axis=1)
    gate_new = adam_update(
        gate_up_master, gate_up_first, gate_up_second, gate_up_grad, D**-0.5, DECAY_RATE
    )
    down_new = adam_update(down_master, down_first, down_second, down_grad, FF**-0.5, DECAY_RATE)
    return (
        outputs[None],
        input_grad,
        *norm_new,
        *qk_new,
        *qkv_new,
        *out_new,
        *gate_new,
        *down_new,
    )


def solution(mesh):
    token = P("fsdp", "seq", None)
    weight = P(ALL, None)
    return jax.shard_map(
        per_device,
        mesh=mesh,
        in_specs=(token, token, P("fsdp", None)) + (P(),) * 6 + (weight,) * 12,
        out_specs=(token, token) + (P(),) * 6 + (weight,) * 12,
        check_vma=False,
    )
```

```python
import functools
import math

import jax
import jax.numpy as jnp
from jax import lax
from jax.experimental import pallas as pl
from jax.experimental.pallas import tpu as pltpu
from jax.sharding import PartitionSpec as P

D = 1024
HQ = 16
KEY_VALUE_HEADS = 8
HEAD_SIZE = 64
FF = 4608
QUERY_FEATURES = 1024
KEY_FEATURES = 512
STEP = 10
LANES = 128

NORM_EPS = 1e-05
ROPE_BASE = 1000000.0
BETA_ONE = 0.9
BETA_TWO = 0.95
ADAM_EPS = 1e-08
DECAY_RATE = 0.1
GAIN_RATE = 0.3

F32 = jnp.float32
BF16 = jnp.bfloat16
QUERY_BLOCK = 128
KEY_BLOCK = 256
FF_BLOCK = 256
PIECES = 4


def dot(a, b):
    return lax.dot_general(a, b, (((1,), (0,)), ((), ())), preferred_element_type=F32)


def dot_cols(a, b):
    return lax.dot_general(a, b, (((1,), (1,)), ((), ())), preferred_element_type=F32)


def dot_rows(a, b):
    return lax.dot_general(a, b, (((0,), (0,)), ((), ())), preferred_element_type=F32)


def params(limit=56):
    return pltpu.CompilerParams(vmem_limit_bytes=limit << 20)


def head_mean(v):
    row = lax.broadcasted_iota(jnp.int32, (LANES, LANES), 0) // HEAD_SIZE
    col = lax.broadcasted_iota(jnp.int32, (LANES, LANES), 1) // HEAD_SIZE
    ones = jnp.where(row == col, 1.0 / HEAD_SIZE, 0.0).astype(BF16)
    high = v.astype(BF16)
    low = (v - high.astype(F32)).astype(BF16)
    return dot(high, ones) + dot(low, ones)


def swap_halves(v):
    lane = lax.broadcasted_iota(jnp.int32, v.shape, 1) % HEAD_SIZE
    return jnp.where(
        lane < HEAD_SIZE // 2,
        pltpu.roll(v, LANES - HEAD_SIZE // 2, 1),
        pltpu.roll(v, HEAD_SIZE // 2, 1),
    )


def prep_kernel(raw_ref, gain_ref, cos_ref, sin_ref, q_ref, *kv_refs):
    cosine, sine = cos_ref[...], sin_ref[...]
    for group in range(12):
        part = slice(group * LANES, (group + 1) * LANES)
        u = raw_ref[:, part]
        gain = gain_ref[0:1] if group < 8 else gain_ref[1:2]
        n = u * lax.rsqrt(head_mean(u * u) + NORM_EPS) * gain
        out = n * cosine + swap_halves(n) * sine
        if group < 8:
            q_ref[:, part] = (out * HEAD_SIZE**-0.5).astype(BF16)
        else:
            kv_ref = kv_refs[group - 8]
            kv_ref[:, :LANES] = out.astype(BF16)
            value = raw_ref[:, slice((group + 4) * LANES, (group + 5) * LANES)]
            kv_ref[:, LANES:] = value.astype(BF16)


def prep(raw, gains, cosine, sine):
    rows = raw.shape[0]
    block = min(rows, 256)
    whole = lambda width: pl.BlockSpec((block, width), lambda i: (i, 0))
    return pl.pallas_call(
        prep_kernel,
        name="prep",
        grid=(rows // block,),
        in_specs=[whole(2048), pl.BlockSpec((8, LANES), lambda i: (0, 0)), whole(LANES), whole(LANES)],
        out_specs=[whole(QUERY_FEATURES)] + [whole(2 * LANES)] * PIECES,
        out_shape=[jax.ShapeDtypeStruct((rows, QUERY_FEATURES), BF16)]
        + [jax.ShapeDtypeStruct((rows, 2 * LANES), BF16)] * PIECES,
        compiler_params=params(),
        cost_estimate=pl.CostEstimate(
            flops=rows * 2048 * 40, transcendentals=rows * 24, bytes_accessed=rows * 2048 * 6
        ),
    )(raw, gains, cosine, sine)


def prep_back_kernel(raw_ref, gain_ref, cos_ref, sin_ref, *rest):
    dq_ref, own_refs, back_refs = rest[0], rest[1 : PIECES + 1], rest[PIECES + 1 : 2 * PIECES + 1]
    out_ref, dg_ref = rest[2 * PIECES + 1 :]
    cosine, sine = cos_ref[...], sin_ref[...]
    sums = [jnp.zeros((1, LANES), F32), jnp.zeros((1, LANES), F32)]
    for group in range(12):
        part = slice(group * LANES, (group + 1) * LANES)
        u = raw_ref[:, part]
        which = 0 if group < 8 else 1
        gain = gain_ref[which : which + 1]
        if group < 8:
            d = dq_ref[:, part] * HEAD_SIZE**-0.5
        else:
            own, back = own_refs[group - 8], back_refs[group - 8]
            d = own[:, :LANES] + back[:, :LANES].astype(F32)
            value = slice((group + 4) * LANES, (group + 5) * LANES)
            out_ref[:, value] = (own[:, LANES:] + back[:, LANES:].astype(F32)).astype(BF16)
        d = d * cosine - swap_halves(d) * sine
        r = lax.rsqrt(head_mean(u * u) + NORM_EPS)
        w = d * gain
        n = u * r
        out_ref[:, part] = (r * (w - n * head_mean(w * n))).astype(BF16)
        sums[which] += jnp.sum(d * n, axis=0, keepdims=True)

    @pl.when(pl.program_id(0) == 0)
    def _():
        dg_ref[...] = jnp.zeros_like(dg_ref)

    dg_ref[0:1] += sums[0]
    dg_ref[1:2] += sums[1]


def prep_back(raw, gains, cosine, sine, dq, own, back):
    rows = raw.shape[0]
    block = min(rows, 256)
    whole = lambda width: pl.BlockSpec((block, width), lambda i: (i, 0))
    small = pl.BlockSpec((8, LANES), lambda i: (0, 0))
    return pl.pallas_call(
        prep_back_kernel,
        name="prep_back",
        grid=(rows // block,),
        in_specs=[
            whole(2048),
            small,
            whole(LANES),
            whole(LANES),
            whole(QUERY_FEATURES),
        ]
        + [whole(2 * LANES)] * (2 * PIECES),
        out_specs=[whole(2048), small],
        out_shape=[
            jax.ShapeDtypeStruct((rows, 2048), BF16),
            jax.ShapeDtypeStruct((8, LANES), F32),
        ],
        compiler_params=params(),
        cost_estimate=pl.CostEstimate(
            flops=rows * 2048 * 60, transcendentals=rows * 24, bytes_accessed=rows * 2048 * 10
        ),
    )(raw, gains, cosine, sine, dq, *own, *back)


def stack_heads(rows):
    first, second = rows[:, :LANES].astype(F32), rows[:, LANES:].astype(F32)
    lane = lax.broadcasted_iota(jnp.int32, first.shape, 1)
    low = lane < HEAD_SIZE
    turn = lambda v: pltpu.roll(v, HEAD_SIZE, 1)
    heads = [
        jnp.where(low, first, 0.0),
        jnp.where(low, turn(first), 0.0),
        jnp.where(low, 0.0, turn(second)),
        jnp.where(low, 0.0, second),
    ]
    return jnp.concatenate(heads, axis=0).astype(BF16)


def unstack_heads(tall):
    n = tall.shape[0] // 4
    a, b, c, d = (tall[i * n : (i + 1) * n] for i in range(4))
    low = lax.broadcasted_iota(jnp.int32, a.shape, 1) < HEAD_SIZE
    turn = lambda v: pltpu.roll(v, HEAD_SIZE, 1)
    return jnp.concatenate([jnp.where(low, a, turn(b)), jnp.where(low, turn(c), d)], axis=1)


def key_range(low_ref, turn, block, start, rows):
    begin = low_ref[1 + turn] // KEY_BLOCK
    end = (low_ref[0] + turn * block + block - 1) // KEY_BLOCK + 1
    first, last = start // KEY_BLOCK, (start + rows) // KEY_BLOCK
    return jnp.clip(begin, first, last), jnp.clip(end, first, last)


def attend_kernel(low_ref, first_ref, q_ref, *rest):
    sources = (rest[:PIECES], rest[PIECES : 2 * PIECES])
    out_ref, lse_ref, queries, totals = rest[2 * PIECES :]
    turn = pl.program_id(0)
    block = q_ref.shape[0]
    for p in range(PIECES):
        queries[p] = stack_heads(q_ref[:, p * 2 * LANES : (p + 1) * 2 * LANES])
    totals[...] = jnp.zeros_like(totals)
    place = low_ref[0] + turn * block + lax.broadcasted_iota(jnp.int32, (block, KEY_BLOCK), 0)
    first = jnp.concatenate([first_ref[...]] * (KEY_BLOCK // LANES), axis=1)
    column = lax.broadcasted_iota(jnp.int32, (block, KEY_BLOCK), 1)
    ones = jnp.ones((KEY_BLOCK, LANES), BF16)
    start = 0
    for refs in sources:
        rows = refs[0].shape[0]

        def step(at, _):
            span = pl.ds(pl.multiple_of(at * KEY_BLOCK - start, KEY_BLOCK), KEY_BLOCK)
            key_place = at * KEY_BLOCK + column
            allowed = (key_place >= first) & (key_place <= place)
            for p in range(PIECES):
                scores = dot_cols(queries[p], refs[p][span, :LANES])
                scores = scores.reshape(4, block, KEY_BLOCK)
                powers = jnp.where(allowed[None], jnp.exp(scores), 0.0).astype(BF16)
                values = jnp.concatenate([refs[p][span, LANES:], ones], axis=1)
                totals[p] += dot(powers.reshape(4 * block, KEY_BLOCK), values)
            return 0

        begin, end = key_range(low_ref, turn, block, start, rows)
        lax.fori_loop(begin, end, step, 0)
        start += rows
    for p in range(PIECES):
        mass = totals[p, :, LANES:]
        mixed = totals[p, :, :LANES] / mass
        out_ref[:, p * 2 * LANES : (p + 1) * 2 * LANES] = unstack_heads(mixed).astype(BF16)
        lse_ref[:, p * 4 * block : (p + 1) * 4 * block] = jnp.transpose(jnp.log(mass))[0:8, :]


def attend(q, others, own, low, first):
    rows = q.shape[0]
    block = QUERY_BLOCK
    turns = rows // block
    whole = lambda size: pl.BlockSpec((size, 2 * LANES), lambda t, low: (0, 0))
    wide = pl.BlockSpec((block, QUERY_FEATURES), lambda t, low: (t, 0))
    return pl.pallas_call(
        attend_kernel,
        name="attend",
        grid_spec=pltpu.PrefetchScalarGridSpec(
            num_scalar_prefetch=1,
            grid=(turns,),
            in_specs=[pl.BlockSpec((block, LANES), lambda t, low: (t, 0)), wide]
            + [whole(others[0].shape[0])] * PIECES
            + [whole(rows)] * PIECES,
            out_specs=[wide, pl.BlockSpec((8, HQ * block), lambda t, low: (t, 0))],
            scratch_shapes=[
                pltpu.VMEM((PIECES, 4 * block, LANES), BF16),
                pltpu.VMEM((PIECES, 4 * block, 2 * LANES), F32),
            ],
        ),
        out_shape=[
            jax.ShapeDtypeStruct((rows, QUERY_FEATURES), BF16),
            jax.ShapeDtypeStruct((8 * turns, HQ * block), F32),
        ],
        compiler_params=params(),
        cost_estimate=pl.CostEstimate(
            flops=rows * 1024 * 1024 * 24, transcendentals=rows * 1024 * 16, bytes_accessed=16 << 20
        ),
    )(low, first, q, *others, *own)


def attend_back_kernel(start, low_ref, first_ref, q_ref, do_ref, mixed_ref, lse_ref, before_ref, *rest):
    refs, d_refs = rest[:PIECES], rest[PIECES : 2 * PIECES]
    dq_ref, queries, rising, deltas, dqs, dkvs = rest[2 * PIECES :]
    turn = pl.program_id(0)
    block = q_ref.shape[0]
    rows = refs[0].shape[0]
    tall = 4 * block

    @pl.when(turn == 0)
    def _():
        dkvs[...] = jnp.zeros_like(dkvs)

    begin, end = key_range(low_ref, turn, block, start, rows)

    @pl.when(end <= begin)
    def _():
        dq_ref[...] = before_ref[...]

    @pl.when(end > begin)
    def _():
        for p in range(PIECES):
            part = slice(p * 2 * LANES, (p + 1) * 2 * LANES)
            queries[p] = stack_heads(q_ref[:, part])
            rising[p] = stack_heads(do_ref[:, part])
            across = jnp.transpose(do_ref[:, part].astype(F32) * mixed_ref[:, part].astype(F32))
            deltas[p] = jnp.concatenate(
                [
                    jnp.broadcast_to(
                        jnp.sum(across[i * HEAD_SIZE : (i + 1) * HEAD_SIZE], axis=0, keepdims=True),
                        (8, block),
                    )
                    for i in range(4)
                ],
                axis=1,
            )
        dqs[...] = jnp.zeros_like(dqs)
        shape = (KEY_BLOCK, block)
        place = low_ref[0] + turn * block + lax.broadcasted_iota(jnp.int32, shape, 1)
        row = lax.broadcasted_iota(jnp.int32, shape, 0)
        first = first_ref[0:1]

        def step(at, _):
            span = pl.ds(pl.multiple_of(at * KEY_BLOCK - start, KEY_BLOCK), KEY_BLOCK)
            key_place = at * KEY_BLOCK + row
            allowed = (key_place >= first) & (key_place <= place)
            allowed = jnp.concatenate([allowed] * 4, axis=1)
            for p in range(PIECES):
                key, value = refs[p][span, :LANES], refs[p][span, LANES:]
                logs = lse_ref[0:1, p * tall : (p + 1) * tall]
                probs = jnp.where(allowed, jnp.exp(dot_cols(key, queries[p]) - logs), 0.0)
                dprobs = dot_cols(value, rising[p])
                dscores = (probs * (dprobs - deltas[p, 0:1])).astype(BF16)
                dkvs[p, span, :LANES] += dot(dscores, queries[p])
                dkvs[p, span, LANES:] += dot(probs.astype(BF16), rising[p])
                dqs[p] += dot_rows(dscores, key)
            return 0

        lax.fori_loop(begin, end, step, 0)
        for p in range(PIECES):
            part = slice(p * 2 * LANES, (p + 1) * 2 * LANES)
            dq_ref[:, part] = before_ref[:, part] + unstack_heads(dqs[p])

    @pl.when(turn == pl.num_programs(0) - 1)
    def _():
        for p in range(PIECES):
            d_refs[p][...] = dkvs[p].astype(d_refs[p].dtype)


def attend_back(start, q, d_mixed, mixed, lse, before, source, low, first_lane, kind):
    rows = q.shape[0]
    block = QUERY_BLOCK
    turns = rows // block
    count = source[0].shape[0]
    whole = pl.BlockSpec((count, 2 * LANES), lambda t, low: (0, 0))
    wide = pl.BlockSpec((block, QUERY_FEATURES), lambda t, low: (t, 0))
    *pieces, dq = pl.pallas_call(
        functools.partial(attend_back_kernel, start),
        name="attend_back",
        grid_spec=pltpu.PrefetchScalarGridSpec(
            num_scalar_prefetch=1,
            grid=(turns,),
            in_specs=[
                pl.BlockSpec((8, block), lambda t, low: (0, t)),
                wide,
                wide,
                wide,
                pl.BlockSpec((8, HQ * block), lambda t, low: (t, 0)),
                wide,
            ]
            + [whole] * PIECES,
            out_specs=[whole] * PIECES + [wide],
            scratch_shapes=[
                pltpu.VMEM((PIECES, 4 * block, LANES), BF16),
                pltpu.VMEM((PIECES, 4 * block, LANES), BF16),
                pltpu.VMEM((PIECES, 8, 4 * block), F32),
                pltpu.VMEM((PIECES, 4 * block, LANES), F32),
                pltpu.VMEM((PIECES, count, 2 * LANES), F32),
            ],
        ),
        out_shape=[jax.ShapeDtypeStruct((count, 2 * LANES), kind)] * PIECES
        + [jax.ShapeDtypeStruct((rows, QUERY_FEATURES), F32)],
        compiler_params=params(),
        cost_estimate=pl.CostEstimate(
            flops=rows * 1024 * 1024 * 24, transcendentals=rows * 1024 * 16, bytes_accessed=30 << 20
        ),
    )(low, first_lane, q, d_mixed, mixed, lse, before, *source)
    return dq, pieces


def rms_scale(v):
    return lax.rsqrt(jnp.mean(v * v, axis=-1, keepdims=True) + NORM_EPS)


def rms_back(v, scale, gain_row, d_out):
    w = d_out * gain_row
    n = v * scale
    d_v = scale * (w - n * jnp.mean(w * n, axis=-1, keepdims=True))
    return d_v, jnp.sum(d_out * n, axis=0)


def adam_update(master, first_moment, second_moment, gradient, rate, decay):
    first_moment = BETA_ONE * first_moment + (1.0 - BETA_ONE) * gradient
    second_moment = BETA_TWO * second_moment + (1.0 - BETA_TWO) * gradient * gradient
    corrected = (
        first_moment
        / (1.0 - BETA_ONE**STEP)
        / (jnp.sqrt(second_moment / (1.0 - BETA_TWO**STEP)) + ADAM_EPS)
    )
    return (master - rate * (corrected + decay * master), first_moment, second_moment)


def rotation_tables(position):
    half = HEAD_SIZE // 2
    index_row = jnp.arange(half, dtype=F32)
    frequency = jnp.exp(index_row * (-2.0 * math.log(ROPE_BASE) / HEAD_SIZE))
    angles = position.astype(F32)[:, None] * frequency[None, :]
    cosine, sine = jnp.cos(angles), jnp.sin(angles)
    return (
        jnp.concatenate([cosine] * 4, axis=1),
        jnp.concatenate([-sine, sine, -sine, sine], axis=1),
    )


ALL = ("fsdp", "seq")


def gather(shard):
    return lax.all_gather(shard, ALL, axis=0, tiled=True)


def dims():
    rest = lax.axis_size("fsdp") // 8
    return {
        "z": ("fsdp", 2 * rest, 4),
        "y": ("fsdp", 2, rest),
        "c": ("fsdp", 1, 2),
        "x": ("seq", 1, lax.axis_size("seq")),
    }


def place_along(direction):
    axis, stride, size = dims()[direction]
    return lax.rem(lax.div(lax.axis_index(axis), stride), size)


def swap(value, direction, distance):
    axis, stride, _ = dims()[direction]
    pairs = [(i, i ^ (distance * stride)) for i in range(lax.axis_size(axis))]
    return lax.ppermute(value, axis, pairs)


def relative_rows(order, count):
    sizes = {k: v[2] for k, v in dims().items()}
    width = count
    for size in sizes.values():
        width //= size
    index = jnp.arange(count, dtype=jnp.int32)
    left = index // width
    place = {}
    for k in reversed(order):
        place[k] = jnp.bitwise_xor(left % sizes[k], place_along(k))
        left = left // sizes[k]
    block = jnp.zeros_like(index)
    for k in "zycx":
        block = block * sizes[k] + place[k]
    row = block * width + index % width
    return (row[:, None] == index[None, :]).astype(BF16)


def transpose_in_order(hot, value):
    return dot_cols(hot, value).astype(BF16)


MESH = pl.DeviceIdType.MESH
NAMES = "zycx"


def neighbour(direction, distance):
    axis, stride, _ = dims()[direction]
    here = place_along(direction)
    return {axis: lax.axis_index(axis) + (jnp.bitwise_xor(here, distance) - here) * stride}


def greet():
    barrier = pltpu.get_barrier_semaphore()
    count = 0
    for k in NAMES:
        for d in range(1, dims()[k][2]):
            pl.semaphore_signal(barrier, 1, device_id=neighbour(k, d), device_id_type=MESH)
            count += 1
    pl.semaphore_wait(barrier, count)


def part_view(full, at, columns):
    index = tuple(at[k] if k in at else slice(None) for k in NAMES)
    return full.at[index + (slice(None), columns)]


def gather_kernel(plan, *refs):
    count = 1 + max(p[0] for p in plan)
    shards, fulls = refs[:count], refs[count : 2 * count]
    local, send, recv = refs[2 * count :]
    here = {k: place_along(k) for k in NAMES}
    own = []
    for t in range(count):
        copy = pltpu.make_async_copy(shards[t], part_view(fulls[t], here, slice(None)), local.at[t])
        copy.start()
        own.append(copy)
    greet()
    posted = []

    def post(source, target, k, d):
        n = len(posted)
        copy = pltpu.make_async_remote_copy(
            source, target, send.at[n], recv.at[n], device_id=neighbour(k, d), device_id_type=MESH
        )
        copy.start()
        posted.append(copy)
        return copy

    coming = {}
    for when in range(len(plan) + 3):
        for step in range(4):
            p = when - step
            if not 0 <= p < len(plan):
                continue
            t, column, width, order = plan[p]
            columns = pl.ds(column, width)
            full = fulls[t]
            if step == 0:
                k = order[0]
                target = part_view(full, here, columns)
                coming[p, 0] = [
                    post(shards[t].at[:, columns], target, k, d) for d in range(1, dims()[k][2])
                ]
                continue
            if own[t] is not None:
                own[t].wait()
                own[t] = None
            for copy in coming[p, step - 1]:
                copy.wait_recv()
            at = {k: v for k, v in here.items() if k not in order[:step]}
            if step < 3:
                k = order[step]
                view = part_view(full, at, columns)
                coming[p, step] = [post(view, view, k, d) for d in range(1, dims()[k][2])]
                if step == 2:
                    coming[p, 3] = [post(view, view, "c", 1)]
            else:
                k = order[2]
                for d in range(1, dims()[k][2]):
                    view = part_view(full, {**at, k: jnp.bitwise_xor(here[k], d)}, columns)
                    coming[p, 3].append(post(view, view, "c", 1))
    for p in range(len(plan)):
        for copy in coming[p, 3]:
            copy.wait_recv()
    for copy in posted:
        copy.wait_send()


def plan_parts(arrays, cut):
    plan = []
    for t, shard in enumerate(arrays):
        pieces = max(1, shard.shape[1] // cut)
        width = shard.shape[1] // pieces
        for i in range(pieces):
            plan.append((t, i * width, width, "zxy" if len(plan) % 2 else "zyx"))
    return plan


def gather_all(shards, cut, number):
    plan = plan_parts(shards, cut)
    size = {k: dims()[k][2] for k in NAMES}
    total = sum(sum(size[k] - 1 for k in order) + size[order[2]] for _, _, _, order in plan)
    fulls = pl.pallas_call(
        functools.partial(gather_kernel, plan),
        name="gather_all",
        in_specs=[pl.BlockSpec(memory_space=pl.ANY)] * len(shards),
        out_specs=[pl.BlockSpec(memory_space=pl.ANY)] * len(shards),
        out_shape=[
            jax.ShapeDtypeStruct((*(size[k] for k in NAMES), *shard.shape), shard.dtype)
            for shard in shards
        ],
        scratch_shapes=[
            pltpu.SemaphoreType.DMA((len(shards),)),
            pltpu.SemaphoreType.DMA((total,)),
            pltpu.SemaphoreType.DMA((total,)),
        ],
        compiler_params=pltpu.CompilerParams(collective_id=number, has_side_effects=True),
    )(*shards)
    return [full.reshape(-1, full.shape[-1]) for full in fulls]


def after(values, earlier):
    return lax.optimization_barrier((values, earlier))[0]


def sum_everywhere(terms):
    for k, (_, _, size) in dims().items():
        d = 1
        while d < size:
            terms = terms + swap(terms, k, d)
            d *= 2
    return terms


FIRST_PARTS = 3
FEED_LEAD = 4


def feed_kernel(
    shard_ref,
    a_ref,
    at_ref,
    g_ref,
    start_ref,
    wd_ref,
    full_ref,
    y_ref,
    b_ref,
    gd_ref,
    sum_ref,
    weights,
    terms,
    total_1,
    total_2,
    total_3,
    got_c,
    got_1,
    got_2,
    got_z,
    load_sem,
    start_sem,
    own_sem,
    out_send,
    out_recv,
    in_send,
    in_recv,
):
    step = pl.program_id(0)
    width = weights.shape[-1]
    parts = shard_ref.shape[2] // width
    size = {k: v[2] for k, v in dims().items()}
    here = {k: place_along(k) for k in NAMES}
    shard_rows = shard_ref.shape[1]
    orders = ("xy", "yx")

    def columns(p):
        return pl.ds(pl.multiple_of(p * width, width), width)

    def view(which, at, p):
        index = tuple(at[k] if k in at else slice(None) for k in NAMES)
        return full_ref.at[(which,) + index + (slice(None), columns(p))]

    def remote(source, target, sems, p, n, k, d):
        send, recv = sems
        return pltpu.make_async_remote_copy(
            source,
            target,
            send.at[p, n],
            recv.at[p, n],
            device_id=neighbour(k, d),
            device_id_type=MESH,
        )

    def gather_copies(p, stage):
        sems = (out_send, out_recv)
        copies = []
        if stage == 0:
            for d in range(1, size["z"]):
                copies.append(
                    remote(shard_ref.at[:, :, columns(p)], view(slice(None), here, p), sems, p, d - 1, "z", d)
                )
            return copies
        slot = size["z"] - 1
        if stage == 3:
            slot += 2 * (size["x"] + size["y"] - 2)
            at = view(slice(None), {"c": here["c"]}, p)
            return [remote(at, at, sems, p, slot, "c", 1)]
        for which, order in enumerate(orders):
            for s in (1, 2):
                k = order[s - 1]
                gone = "z" + order[: s - 1]
                at = view(which, {q: v for q, v in here.items() if q not in gone}, p)
                for d in range(1, size[k]):
                    if s == stage:
                        copies.append(remote(at, at, sems, p, slot, k, d))
                    slot += 1
        return copies

    def scatter_copies(p, stage):
        sems = (in_send, in_recv)
        if stage == 0:
            return [remote(terms.at[lax.rem(p, 2), :, 1], got_c.at[p], sems, p, 0, "c", 1)]
        copies = []
        slot = 1
        for which, order in enumerate(orders):
            for s in (1, 2):
                k = order[s - 1]
                for d in range(1, size[k]):
                    if s == 1:
                        source = total_1.at[0, d] if k == "x" else total_1.at[1, :, d]
                    else:
                        source = total_2[which].at[d]
                    target = (got_1, got_2)[s - 1][which].at[p, d - 1]
                    if s == stage:
                        copies.append(remote(source, target, sems, p, slot, k, d))
                    slot += 1
        if stage == 3:
            for d in range(1, size["z"]):
                copies.append(remote(total_3.at[:, d], got_z.at[p, d - 1], sems, p, slot + d - 1, "z", d))
        return copies

    def own_copy():
        return pltpu.make_async_copy(shard_ref, full_ref.at[(slice(None),) + tuple(here[k] for k in NAMES)], own_sem)

    def load_copy(p):
        return pltpu.make_async_copy(
            full_ref.at[:, :, :, :, :, :, columns(p)], weights.at[lax.rem(p, 2)], load_sem.at[lax.rem(p, 2)]
        )

    def on(offset, run):
        p = step - offset

        @pl.when((p >= 0) & (p < parts))
        def _():
            run(p)

    def begin(p):
        for copy in gather_copies(p, 0):
            copy.start()

    @pl.when(step == 0)
    def _():
        own_copy().start()
        pltpu.make_async_copy(start_ref, y_ref, start_sem).start()
        greet()

        for p in range(FIRST_PARTS):
            begin(jnp.int32(p))
        own_copy().wait()
        pltpu.make_async_copy(start_ref, y_ref, start_sem).wait()
        b_ref[...] = jnp.zeros_like(b_ref)

    def pass_on(stage):
        def run(p):
            for copy in gather_copies(p, stage - 1):
                copy.wait_recv()
            for copy in gather_copies(p, stage):
                copy.start()

        return run

    def arrived(p):
        for copy in gather_copies(p, 3):
            copy.wait_recv()
        load_copy(p).start()

    @pl.when((step > 0) & (step + FIRST_PARTS - 1 < parts))
    def _():
        begin(step + FIRST_PARTS - 1)

    on(3, arrived)
    on(2, pass_on(3))
    on(1, pass_on(2))
    on(0, pass_on(1))

    def finish(p):
        for copy in scatter_copies(p, 3):
            copy.wait()
        total = total_3[:, 0].astype(F32)
        for d in range(1, size["z"]):
            total = total + got_z[p, d - 1].astype(F32)
        sum_ref[:, :, columns(p)] = total

    def third(p):
        for copy in scatter_copies(p, 2):
            copy.wait()
        for which, order in enumerate(orders):
            total = total_2[which][0].astype(F32)
            for d in range(1, size[order[1]]):
                total = total + got_2[which][p, d - 1].astype(F32)
            total_3[which] = total.astype(BF16)
        for copy in scatter_copies(p, 3):
            copy.start()

    def second(p):
        for copy in scatter_copies(p, 1):
            copy.wait()
        for which, order in enumerate(orders):
            kept = total_1[0, 0] if order[0] == "x" else total_1[1, :, 0]
            total = kept.astype(F32)
            for d in range(1, size[order[0]]):
                total = total + got_1[which][p, d - 1].astype(F32)
            total_2[which][...] = total.astype(BF16)
        for copy in scatter_copies(p, 2):
            copy.start()

    def first(p):
        for copy in scatter_copies(p, 0):
            copy.wait()
        total = terms[lax.rem(p, 2), :, 0].astype(F32) + got_c[p].astype(F32)
        total_1[...] = total.astype(BF16)
        for copy in scatter_copies(p, 1):
            copy.start()

    on(FEED_LEAD + 4, finish)
    on(FEED_LEAD + 3, third)
    on(FEED_LEAD + 2, second)
    on(FEED_LEAD + 1, first)

    def compute(p):
        load_copy(p).wait()
        slot = lax.rem(p, 2)
        rows = D
        a, g, wd = a_ref[...], g_ref[...], wd_ref[...]
        wg = weights[slot, 0].reshape(rows, width)
        wu = weights[slot, 1].reshape(rows, width)
        gate = dot(a, wg)
        up = dot(a, wu)
        d_hidden = dot_cols(g, wd)
        sigma = 1.0 / (1.0 + jnp.exp(-gate))
        swish = gate * sigma
        hidden = (swish * up).astype(BF16)
        d_gate = (d_hidden * up * sigma * (1.0 + gate * (1.0 - sigma))).astype(BF16)
        d_up = (d_hidden * swish).astype(BF16)
        y_ref[...] += dot(hidden, wd)
        b_ref[...] += dot_cols(d_gate, wg) + dot_cols(d_up, wu)
        at = at_ref[...]
        shape = (2,) + total_1.shape[1:]
        terms[slot, 0] = dot(at, d_gate).astype(BF16).reshape(shape)
        terms[slot, 1] = dot(at, d_up).astype(BF16).reshape(shape)
        gd_ref[...] = dot_rows(hidden, g).astype(BF16)
        for copy in scatter_copies(p, 0):
            copy.start()

    on(FEED_LEAD, compute)

    @pl.when(step == pl.num_programs(0) - 1)
    def _():
        def end(p, _):
            for stage in range(4):
                for copy in gather_copies(p, stage):
                    copy.wait_send()
            return 0

        lax.fori_loop(0, parts, end, 0)


def feed(shards, a, at, g, w_down, start, number):
    rows = a.shape[0]
    size = {k: v[2] for k, v in dims().items()}
    _, shard_rows, width = shards.shape
    parts = width // FF_BLOCK
    x, y, z = size["x"], size["y"], size["z"]
    last = (z, shard_rows, FF_BLOCK)
    whole = pl.BlockSpec(memory_space=pltpu.VMEM)
    anywhere = pl.BlockSpec(memory_space=pl.ANY)
    row = pl.BlockSpec((FF_BLOCK, D), lambda t: (jnp.clip(t - FEED_LEAD, 0, parts - 1), 0))
    out_count = z - 1 + 2 * (x + y - 2) + 1
    in_count = 1 + 2 * (x + y - 2) + z - 1
    sems = pltpu.SemaphoreType.DMA
    _, y_sum, b_sum, grad_down, sums = pl.pallas_call(
        feed_kernel,
        name="feed",
        grid=(parts + FEED_LEAD + 4,),
        in_specs=[anywhere, whole, whole, whole, anywhere, row],
        out_specs=[anywhere, whole, whole, row, whole],
        out_shape=[
            jax.ShapeDtypeStruct((2, *(size[k] for k in NAMES), shard_rows, width), BF16),
            jax.ShapeDtypeStruct((rows, D), F32),
            jax.ShapeDtypeStruct((rows, D), F32),
            jax.ShapeDtypeStruct((width, D), BF16),
            jax.ShapeDtypeStruct((2, shard_rows, width), F32),
        ],
        scratch_shapes=[
            pltpu.VMEM((2, 2, *(size[k] for k in NAMES), shard_rows, FF_BLOCK), BF16),
            pltpu.VMEM((2, 2, 2, x, y, *last), BF16),
            pltpu.VMEM((2, x, y, *last), BF16),
            [pltpu.VMEM((y, *last), BF16), pltpu.VMEM((x, *last), BF16)],
            pltpu.VMEM((2, *last), BF16),
            pltpu.VMEM((parts, 2, x, y, *last), BF16),
            [pltpu.VMEM((parts, x - 1, y, *last), BF16), pltpu.VMEM((parts, y - 1, x, *last), BF16)],
            [pltpu.VMEM((parts, y - 1, *last), BF16), pltpu.VMEM((parts, x - 1, *last), BF16)],
            pltpu.VMEM((parts, z - 1, 2, shard_rows, FF_BLOCK), BF16),
            sems((2,)),
            sems,
            sems,
            sems((parts, out_count)),
            sems((parts, out_count)),
            sems((parts, in_count)),
            sems((parts, in_count)),
        ],
        compiler_params=pltpu.CompilerParams(
            collective_id=number, has_side_effects=True, vmem_limit_bytes=60 << 20
        ),
        cost_estimate=pl.CostEstimate(
            flops=18 * rows * D * width, transcendentals=rows * width, bytes_accessed=12 * D * width
        ),
    )(shards, a, at, g, start, w_down)
    return y_sum, b_sum, grad_down, sums


def add_swapped(keep, send, direction):
    return (keep.astype(F32) + swap(send, direction, 1).astype(F32)).astype(BF16)


def add_along(terms, direction, last=False):
    size = dims()[direction][2]
    step = terms.shape[0] // size
    total = terms[:step].astype(F32)
    for d in range(1, size):
        total = total + swap(terms[d * step : (d + 1) * step], direction, d).astype(F32)
    return total if last else total.astype(BF16)


def own_part(terms, direction, last=False):
    at, here, size = NAMES.index(direction), place_along(direction), dims()[direction][2]
    total = lax.dynamic_slice_in_dim(terms, here, 1, at).astype(F32)
    for d in range(1, size):
        sent = lax.dynamic_slice_in_dim(terms, jnp.bitwise_xor(here, d), 1, at)
        total = total + swap(sent, direction, d).astype(F32)
    return total if last else total.astype(BF16)


def per_device(
    inputs,
    cotangent,
    lengths,
    norm_gains,
    norm_first,
    norm_second,
    qk_gains,
    qk_first,
    qk_second,
    qkv_master,
    qkv_first,
    qkv_second,
    out_master,
    out_first,
    out_second,
    gate_up_master,
    gate_up_first,
    gate_up_second,
    down_master,
    down_first,
    down_second,
):
    seq_width = lax.axis_size("seq")
    turn_here = lax.axis_index("seq")
    rows = inputs.shape[1]
    block = QUERY_BLOCK
    w_qkv, w_out = gather_all([qkv_master.astype(BF16), out_master.astype(BF16)], 512, 1)

    places = turn_here * rows + jnp.arange(rows, dtype=jnp.int32)
    row_lengths = lengths[0]
    doc_ends = jnp.cumsum(row_lengths)
    passed = doc_ends[None, :] <= places[:, None]
    begins = jnp.sum(jnp.where(passed, row_lengths[None, :], 0), axis=1)
    cosine, sine = rotation_tables(places - begins)
    if seq_width == 2:
        base = (turn_here - 1) * rows
    else:
        base = turn_here * 0
    first = (begins - base).astype(jnp.int32)
    low = jnp.concatenate([(turn_here * rows - base)[None], first[::block]]).astype(jnp.int32)
    first_wide = jnp.broadcast_to(first[:, None], (rows, LANES))
    first_lane = jnp.broadcast_to(first[None, :], (8, rows))

    x = inputs[0].astype(F32)
    scale_first = rms_scale(x)
    normed_first = (x * scale_first * norm_gains[0]).astype(BF16)
    raw = jnp.dot(normed_first, w_qkv, preferred_element_type=F32)
    gain_rows = jnp.pad(jnp.tile(qk_gains, (1, 2)), ((0, 6), (0, 0)))
    q, *own = prep(raw, gain_rows, cosine, sine)
    if seq_width == 2:
        others = [lax.ppermute(p, "seq", [(0, 1)]) for p in own]
    else:
        others = [lax.all_gather(p, "seq", axis=0, tiled=True) for p in own]
    w_down = gather(after(down_master.astype(BF16), others[3]))
    mixed, lse = attend(q, others, own, low, first_wide)
    x_mid = x + jnp.dot(mixed, w_out, preferred_element_type=F32)
    scale_second = rms_scale(x_mid)
    normed_second = (x_mid * scale_second * norm_gains[1]).astype(BF16)
    g = cotangent[0]
    hot_x, hot_y = relative_rows("cxyz", D), relative_rows("cyxz", D)
    shards = jnp.stack([gate_up_master[:, :FF], gate_up_master[:, FF:]]).astype(BF16)
    out_sum, d_b, grad_down, gate_up_sums = feed(
        after(shards, normed_second),
        normed_second,
        transpose_in_order(hot_x, normed_second),
        g,
        w_down,
        x_mid,
        2,
    )
    outputs = out_sum.astype(BF16)
    down_grad = lax.psum_scatter(grad_down, ALL, scatter_dimension=0, tiled=True).astype(F32)
    d_norm, d_gain_second = rms_back(x_mid, scale_second, norm_gains[1], d_b)
    d_mid = g.astype(F32) + d_norm
    d_attn = d_mid.astype(BF16)
    d_mixed = dot_cols(d_attn, w_out).astype(BF16)
    out_terms = transpose_in_order(hot_y, mixed)
    half = QUERY_FEATURES // 2
    out_1 = add_swapped(
        dot(out_terms[:half], d_attn).astype(BF16), dot(out_terms[half:], d_attn).astype(BF16), "c"
    )

    zero = jnp.zeros((rows, QUERY_FEATURES), F32)
    dq, far = attend_back(0, q, d_mixed, mixed, lse, zero, others, low, first_lane, BF16)
    if seq_width == 2:
        back = [lax.ppermute(p, "seq", [(1, 0)]) for p in far]
    else:
        back = [lax.psum_scatter(p, "seq", scatter_dimension=0, tiled=True) for p in far]
    out_2 = add_along(out_1, "y")
    dq, near = attend_back(
        others[0].shape[0], q, after(d_mixed, out_2), mixed, lse, dq, own, low, first_lane, F32
    )
    out_grad = add_along(add_along(out_2, "x"), "z", True)
    d_qkv, d_gain_qk = prep_back(raw, gain_rows, cosine, sine, dq, near, back)
    first_terms = transpose_in_order(hot_x, normed_first)
    qkv_1 = add_swapped(
        dot(first_terms[: D // 2], d_qkv).astype(BF16), dot(first_terms[D // 2 :], d_qkv).astype(BF16), "c"
    )
    qkv_grad = add_along(add_along(add_along(qkv_1, "x"), "y"), "z", True)
    d_a = dot_cols(d_qkv, w_qkv)
    d_x, d_gain_first = rms_back(x, scale_first, norm_gains[0], d_a)
    input_grad = (d_mid + d_x)[None]
    gain_terms = jnp.pad(d_gain_qk[:2], ((0, 0), (0, D - LANES)))
    gain_terms = jnp.concatenate([d_gain_first[None], d_gain_second[None], gain_terms], axis=0)
    gain_sums = sum_everywhere(jnp.pad(gain_terms, ((0, 4), (0, 0))))
    norm_grad = gain_sums[:2]
    qk_grad = gain_sums[2:4, :HEAD_SIZE] + gain_sums[2:4, HEAD_SIZE:LANES]

    norm_new = adam_update(norm_gains, norm_first, norm_second, norm_grad, GAIN_RATE, 0.0)
    qk_new = adam_update(qk_gains, qk_first, qk_second, qk_grad, GAIN_RATE, 0.0)
    qkv_new = adam_update(qkv_master, qkv_first, qkv_second, qkv_grad, D**-0.5, DECAY_RATE)
    out_new = adam_update(
        out_master, out_first, out_second, out_grad, (QUERY_FEATURES // 16) ** -0.5, DECAY_RATE
    )
    gate_up_grad = jnp.concatenate([gate_up_sums[0], gate_up_sums[1]], axis=1)
    gate_new = adam_update(
        gate_up_master, gate_up_first, gate_up_second, gate_up_grad, D**-0.5, DECAY_RATE
    )
    down_new = adam_update(down_master, down_first, down_second, down_grad, FF**-0.5, DECAY_RATE)
    return (
        outputs[None],
        input_grad,
        *norm_new,
        *qk_new,
        *qkv_new,
        *out_new,
        *gate_new,
        *down_new,
    )


def solution(mesh):
    token = P("fsdp", "seq", None)
    weight = P(ALL, None)
    return jax.shard_map(
        per_device,
        mesh=mesh,
        in_specs=(token, token, P("fsdp", None)) + (P(),) * 6 + (weight,) * 12,
        out_specs=(token, token) + (P(),) * 6 + (weight,) * 12,
        check_vma=False,
    )
```

```python
import functools
import math

import jax
import jax.numpy as jnp
from jax import lax
from jax.experimental import pallas as pl
from jax.experimental.pallas import tpu as pltpu
from jax.sharding import PartitionSpec as P

D = 1024
HQ = 16
KEY_VALUE_HEADS = 8
HEAD_SIZE = 64
FF = 4608
QUERY_FEATURES = 1024
KEY_FEATURES = 512
STEP = 10
LANES = 128

NORM_EPS = 1e-05
ROPE_BASE = 1000000.0
BETA_ONE = 0.9
BETA_TWO = 0.95
ADAM_EPS = 1e-08
DECAY_RATE = 0.1
GAIN_RATE = 0.3

F32 = jnp.float32
BF16 = jnp.bfloat16
QUERY_BLOCK = 128
KEY_BLOCK = 256
FF_BLOCK = 256
PIECES = 4


def dot(a, b):
    return lax.dot_general(a, b, (((1,), (0,)), ((), ())), preferred_element_type=F32)


def dot_cols(a, b):
    return lax.dot_general(a, b, (((1,), (1,)), ((), ())), preferred_element_type=F32)


def dot_rows(a, b):
    return lax.dot_general(a, b, (((0,), (0,)), ((), ())), preferred_element_type=F32)


def params(limit=56):
    return pltpu.CompilerParams(vmem_limit_bytes=limit << 20)


def head_mean(v):
    row = lax.broadcasted_iota(jnp.int32, (LANES, LANES), 0) // HEAD_SIZE
    col = lax.broadcasted_iota(jnp.int32, (LANES, LANES), 1) // HEAD_SIZE
    ones = jnp.where(row == col, 1.0 / HEAD_SIZE, 0.0).astype(BF16)
    high = v.astype(BF16)
    low = (v - high.astype(F32)).astype(BF16)
    return dot(high, ones) + dot(low, ones)


def swap_halves(v):
    lane = lax.broadcasted_iota(jnp.int32, v.shape, 1) % HEAD_SIZE
    return jnp.where(
        lane < HEAD_SIZE // 2,
        pltpu.roll(v, LANES - HEAD_SIZE // 2, 1),
        pltpu.roll(v, HEAD_SIZE // 2, 1),
    )


def prep_kernel(raw_ref, gain_ref, cos_ref, sin_ref, q_ref, *kv_refs):
    cosine, sine = cos_ref[...], sin_ref[...]
    for group in range(12):
        part = slice(group * LANES, (group + 1) * LANES)
        u = raw_ref[:, part]
        gain = gain_ref[0:1] if group < 8 else gain_ref[1:2]
        n = u * lax.rsqrt(head_mean(u * u) + NORM_EPS) * gain
        out = n * cosine + swap_halves(n) * sine
        if group < 8:
            q_ref[:, part] = (out * HEAD_SIZE**-0.5).astype(BF16)
        else:
            kv_ref = kv_refs[group - 8]
            kv_ref[:, :LANES] = out.astype(BF16)
            value = raw_ref[:, slice((group + 4) * LANES, (group + 5) * LANES)]
            kv_ref[:, LANES:] = value.astype(BF16)


def prep(raw, gains, cosine, sine):
    rows = raw.shape[0]
    block = min(rows, 256)
    whole = lambda width: pl.BlockSpec((block, width), lambda i: (i, 0))
    return pl.pallas_call(
        prep_kernel,
        name="prep",
        grid=(rows // block,),
        in_specs=[whole(2048), pl.BlockSpec((8, LANES), lambda i: (0, 0)), whole(LANES), whole(LANES)],
        out_specs=[whole(QUERY_FEATURES)] + [whole(2 * LANES)] * PIECES,
        out_shape=[jax.ShapeDtypeStruct((rows, QUERY_FEATURES), BF16)]
        + [jax.ShapeDtypeStruct((rows, 2 * LANES), BF16)] * PIECES,
        compiler_params=params(),
        cost_estimate=pl.CostEstimate(
            flops=rows * 2048 * 40, transcendentals=rows * 24, bytes_accessed=rows * 2048 * 6
        ),
    )(raw, gains, cosine, sine)


def stack_heads(rows):
    first, second = rows[:, :LANES].astype(F32), rows[:, LANES:].astype(F32)
    lane = lax.broadcasted_iota(jnp.int32, first.shape, 1)
    low = lane < HEAD_SIZE
    turn = lambda v: pltpu.roll(v, HEAD_SIZE, 1)
    heads = [
        jnp.where(low, first, 0.0),
        jnp.where(low, turn(first), 0.0),
        jnp.where(low, 0.0, turn(second)),
        jnp.where(low, 0.0, second),
    ]
    return jnp.concatenate(heads, axis=0).astype(BF16)


def unstack_heads(tall):
    n = tall.shape[0] // 4
    a, b, c, d = (tall[i * n : (i + 1) * n] for i in range(4))
    low = lax.broadcasted_iota(jnp.int32, a.shape, 1) < HEAD_SIZE
    turn = lambda v: pltpu.roll(v, HEAD_SIZE, 1)
    return jnp.concatenate([jnp.where(low, a, turn(b)), jnp.where(low, turn(c), d)], axis=1)


def key_range(low_ref, turn, block, start, rows):
    begin = low_ref[1 + turn] // KEY_BLOCK
    end = (low_ref[0] + turn * block + block - 1) // KEY_BLOCK + 1
    first, last = start // KEY_BLOCK, (start + rows) // KEY_BLOCK
    return jnp.clip(begin, first, last), jnp.clip(end, first, last)


def attend_kernel(low_ref, first_ref, q_ref, *rest):
    sources = (rest[:PIECES], rest[PIECES : 2 * PIECES])
    out_ref, lse_ref, queries, totals = rest[2 * PIECES :]
    turn = pl.program_id(0)
    block = q_ref.shape[0]
    for p in range(PIECES):
        queries[p] = stack_heads(q_ref[:, p * 2 * LANES : (p + 1) * 2 * LANES])
    totals[...] = jnp.zeros_like(totals)
    place = low_ref[0] + turn * block + lax.broadcasted_iota(jnp.int32, (block, KEY_BLOCK), 0)
    first = jnp.concatenate([first_ref[...]] * (KEY_BLOCK // LANES), axis=1)
    column = lax.broadcasted_iota(jnp.int32, (block, KEY_BLOCK), 1)
    ones = jnp.ones((KEY_BLOCK, LANES), BF16)
    start = 0
    for refs in sources:
        rows = refs[0].shape[0]

        def step(at, _):
            span = pl.ds(pl.multiple_of(at * KEY_BLOCK - start, KEY_BLOCK), KEY_BLOCK)
            key_place = at * KEY_BLOCK + column
            allowed = (key_place >= first) & (key_place <= place)
            for p in range(PIECES):
                scores = dot_cols(queries[p], refs[p][span, :LANES])
                scores = scores.reshape(4, block, KEY_BLOCK)
                powers = jnp.where(allowed[None], jnp.exp(scores), 0.0).astype(BF16)
                values = jnp.concatenate([refs[p][span, LANES:], ones], axis=1)
                totals[p] += dot(powers.reshape(4 * block, KEY_BLOCK), values)
            return 0

        begin, end = key_range(low_ref, turn, block, start, rows)
        lax.fori_loop(begin, end, step, 0)
        start += rows
    for p in range(PIECES):
        mass = totals[p, :, LANES:]
        mixed = totals[p, :, :LANES] / mass
        out_ref[:, p * 2 * LANES : (p + 1) * 2 * LANES] = unstack_heads(mixed).astype(BF16)
        lse_ref[:, p * 4 * block : (p + 1) * 4 * block] = jnp.transpose(jnp.log(mass))[0:8, :]


def attend(q, others, own, low, first):
    rows = q.shape[0]
    block = QUERY_BLOCK
    turns = rows // block
    whole = lambda size: pl.BlockSpec((size, 2 * LANES), lambda t, low: (0, 0))
    wide = pl.BlockSpec((block, QUERY_FEATURES), lambda t, low: (t, 0))
    return pl.pallas_call(
        attend_kernel,
        name="attend",
        grid_spec=pltpu.PrefetchScalarGridSpec(
            num_scalar_prefetch=1,
            grid=(turns,),
            in_specs=[pl.BlockSpec((block, LANES), lambda t, low: (t, 0)), wide]
            + [whole(others[0].shape[0])] * PIECES
            + [whole(rows)] * PIECES,
            out_specs=[wide, pl.BlockSpec((8, HQ * block), lambda t, low: (t, 0))],
            scratch_shapes=[
                pltpu.VMEM((PIECES, 4 * block, LANES), BF16),
                pltpu.VMEM((PIECES, 4 * block, 2 * LANES), F32),
            ],
        ),
        out_shape=[
            jax.ShapeDtypeStruct((rows, QUERY_FEATURES), BF16),
            jax.ShapeDtypeStruct((8 * turns, HQ * block), F32),
        ],
        compiler_params=params(),
        cost_estimate=pl.CostEstimate(
            flops=rows * 1024 * 1024 * 24, transcendentals=rows * 1024 * 16, bytes_accessed=16 << 20
        ),
    )(low, first, q, *others, *own)


def attend_back_kernel(start, low_ref, first_ref, q_ref, do_ref, mixed_ref, lse_ref, before_ref, *rest):
    refs = rest[:PIECES]
    d_ref, dq_ref, queries, rising, deltas, dqs, dkvs = rest[PIECES:]
    turn = pl.program_id(0)
    block = q_ref.shape[0]
    rows = refs[0].shape[0]
    tall = 4 * block

    @pl.when(turn == 0)
    def _():
        dkvs[...] = jnp.zeros_like(dkvs)

    begin, end = key_range(low_ref, turn, block, start, rows)

    @pl.when(end <= begin)
    def _():
        dq_ref[...] = before_ref[...]

    @pl.when(end > begin)
    def _():
        for p in range(PIECES):
            part = slice(p * 2 * LANES, (p + 1) * 2 * LANES)
            queries[p] = stack_heads(q_ref[:, part])
            rising[p] = stack_heads(do_ref[:, part])
            across = jnp.transpose(do_ref[:, part].astype(F32) * mixed_ref[:, part].astype(F32))
            deltas[p] = jnp.concatenate(
                [
                    jnp.broadcast_to(
                        jnp.sum(across[i * HEAD_SIZE : (i + 1) * HEAD_SIZE], axis=0, keepdims=True),
                        (8, block),
                    )
                    for i in range(4)
                ],
                axis=1,
            )
        dqs[...] = jnp.zeros_like(dqs)
        shape = (KEY_BLOCK, block)
        place = low_ref[0] + turn * block + lax.broadcasted_iota(jnp.int32, shape, 1)
        row = lax.broadcasted_iota(jnp.int32, shape, 0)
        first = first_ref[0:1]

        def step(at, _):
            span = pl.ds(pl.multiple_of(at * KEY_BLOCK - start, KEY_BLOCK), KEY_BLOCK)
            key_place = at * KEY_BLOCK + row
            allowed = (key_place >= first) & (key_place <= place)
            allowed = jnp.concatenate([allowed] * 4, axis=1)
            for p in range(PIECES):
                key, value = refs[p][span, :LANES], refs[p][span, LANES:]
                logs = lse_ref[0:1, p * tall : (p + 1) * tall]
                probs = jnp.where(allowed, jnp.exp(dot_cols(key, queries[p]) - logs), 0.0)
                dprobs = dot_cols(value, rising[p])
                dscores = (probs * (dprobs - deltas[p, 0:1])).astype(BF16)
                dkvs[p, span, :LANES] += dot(dscores, queries[p])
                dkvs[p, span, LANES:] += dot(probs.astype(BF16), rising[p])
                dqs[p] += dot_rows(dscores, key)
            return 0

        lax.fori_loop(begin, end, step, 0)
        for p in range(PIECES):
            part = slice(p * 2 * LANES, (p + 1) * 2 * LANES)
            dq_ref[:, part] = before_ref[:, part] + unstack_heads(dqs[p])

    @pl.when(turn == pl.num_programs(0) - 1)
    def _():
        for p in range(PIECES):
            for half in range(2):
                part = slice(half * KEY_FEATURES + p * LANES, half * KEY_FEATURES + (p + 1) * LANES)
                d_ref[:, part] = dkvs[p, :, half * LANES : (half + 1) * LANES].astype(d_ref.dtype)


def attend_back(start, q, d_mixed, mixed, lse, before, source, low, first_lane, kind):
    rows = q.shape[0]
    block = QUERY_BLOCK
    turns = rows // block
    count = source[0].shape[0]
    whole = pl.BlockSpec((count, 2 * KEY_FEATURES), lambda t, low: (0, 0))
    wide = pl.BlockSpec((block, QUERY_FEATURES), lambda t, low: (t, 0))
    d_keys, dq = pl.pallas_call(
        functools.partial(attend_back_kernel, start),
        name="attend_back",
        grid_spec=pltpu.PrefetchScalarGridSpec(
            num_scalar_prefetch=1,
            grid=(turns,),
            in_specs=[
                pl.BlockSpec((8, block), lambda t, low: (0, t)),
                wide,
                wide,
                wide,
                pl.BlockSpec((8, HQ * block), lambda t, low: (t, 0)),
                wide,
            ]
            + [pl.BlockSpec((count, 2 * LANES), lambda t, low: (0, 0))] * PIECES,
            out_specs=[whole, wide],
            scratch_shapes=[
                pltpu.VMEM((PIECES, 4 * block, LANES), BF16),
                pltpu.VMEM((PIECES, 4 * block, LANES), BF16),
                pltpu.VMEM((PIECES, 8, 4 * block), F32),
                pltpu.VMEM((PIECES, 4 * block, LANES), F32),
                pltpu.VMEM((PIECES, count, 2 * LANES), F32),
            ],
        ),
        out_shape=[
            jax.ShapeDtypeStruct((count, 2 * KEY_FEATURES), kind),
            jax.ShapeDtypeStruct((rows, QUERY_FEATURES), F32),
        ],
        compiler_params=params(),
        cost_estimate=pl.CostEstimate(
            flops=rows << 18, transcendentals=0, bytes_accessed=rows << 8
        ),
    )(low, first_lane, q, d_mixed, mixed, lse, before, *source)
    return dq, d_keys


def rms_scale(v):
    return lax.rsqrt(jnp.mean(v * v, axis=-1, keepdims=True) + NORM_EPS)


def rms_back(v, scale, gain_row, d_out):
    w = d_out * gain_row
    n = v * scale
    d_v = scale * (w - n * jnp.mean(w * n, axis=-1, keepdims=True))
    return d_v, jnp.sum(d_out * n, axis=0)


def adam_update(master, first_moment, second_moment, gradient, rate, decay):
    first_moment = BETA_ONE * first_moment + (1.0 - BETA_ONE) * gradient
    second_moment = BETA_TWO * second_moment + (1.0 - BETA_TWO) * gradient * gradient
    corrected = (
        first_moment
        / (1.0 - BETA_ONE**STEP)
        / (jnp.sqrt(second_moment / (1.0 - BETA_TWO**STEP)) + ADAM_EPS)
    )
    return (master - rate * (corrected + decay * master), first_moment, second_moment)


def rotation_tables(position):
    half = HEAD_SIZE // 2
    index_row = jnp.arange(half, dtype=F32)
    frequency = jnp.exp(index_row * (-2.0 * math.log(ROPE_BASE) / HEAD_SIZE))
    angles = position.astype(F32)[:, None] * frequency[None, :]
    cosine, sine = jnp.cos(angles), jnp.sin(angles)
    return (
        jnp.concatenate([cosine] * 4, axis=1),
        jnp.concatenate([-sine, sine, -sine, sine], axis=1),
    )


ALL = ("fsdp", "seq")


def gather(shard):
    return lax.all_gather(shard, ALL, axis=0, tiled=True)


def dims():
    rest = lax.axis_size("fsdp") // 8
    return {
        "z": ("fsdp", 2 * rest, 4),
        "y": ("fsdp", 2, rest),
        "c": ("fsdp", 1, 2),
        "x": ("seq", 1, lax.axis_size("seq")),
    }


def place_along(direction):
    axis, stride, size = dims()[direction]
    return lax.rem(lax.div(lax.axis_index(axis), stride), size)


def swap(value, direction, distance):
    axis, stride, _ = dims()[direction]
    pairs = [(i, i ^ (distance * stride)) for i in range(lax.axis_size(axis))]
    return lax.ppermute(value, axis, pairs)


def relative_rows(order, count):
    sizes = {k: v[2] for k, v in dims().items()}
    width = count
    for size in sizes.values():
        width //= size
    index = jnp.arange(count, dtype=jnp.int32)
    left = index // width
    place = {}
    for k in reversed(order):
        place[k] = jnp.bitwise_xor(left % sizes[k], place_along(k))
        left = left // sizes[k]
    block = jnp.zeros_like(index)
    for k in "zycx":
        block = block * sizes[k] + place[k]
    row = block * width + index % width
    return (row[:, None] == index[None, :]).astype(BF16)


def transpose_in_order(hot, value):
    return dot_cols(hot, value).astype(BF16)


MESH = pl.DeviceIdType.MESH
NAMES = "zycx"


def neighbour(direction, distance):
    axis, stride, _ = dims()[direction]
    here = place_along(direction)
    return {axis: lax.axis_index(axis) + (jnp.bitwise_xor(here, distance) - here) * stride}


def greet():
    barrier = pltpu.get_barrier_semaphore()
    count = 0
    for k in NAMES:
        for d in range(1, dims()[k][2]):
            pl.semaphore_signal(barrier, 1, device_id=neighbour(k, d), device_id_type=MESH)
            count += 1
    pl.semaphore_wait(barrier, count)


def part_view(full, at, columns):
    index = tuple(at[k] if k in at else slice(None) for k in NAMES)
    return full.at[index + (slice(None), columns)]


def gather_kernel(plan, *refs):
    count = 1 + max(p[0] for p in plan)
    shards, fulls = refs[:count], refs[count : 2 * count]
    local, send, recv = refs[2 * count :]
    here = {k: place_along(k) for k in NAMES}
    own = []
    for t in range(count):
        copy = pltpu.make_async_copy(shards[t], part_view(fulls[t], here, slice(None)), local.at[t])
        copy.start()
        own.append(copy)
    greet()
    posted = []

    def post(source, target, k, d):
        n = len(posted)
        copy = pltpu.make_async_remote_copy(
            source, target, send.at[n], recv.at[n], device_id=neighbour(k, d), device_id_type=MESH
        )
        copy.start()
        posted.append(copy)
        return copy

    coming = {}
    for when in range(len(plan) + 3):
        for step in range(4):
            p = when - step
            if not 0 <= p < len(plan):
                continue
            t, column, width, order = plan[p]
            columns = pl.ds(column, width)
            full = fulls[t]
            if step == 0:
                k = order[0]
                target = part_view(full, here, columns)
                coming[p, 0] = [
                    post(shards[t].at[:, columns], target, k, d) for d in range(1, dims()[k][2])
                ]
                continue
            if own[t] is not None:
                own[t].wait()
                own[t] = None
            for copy in coming[p, step - 1]:
                copy.wait_recv()
            at = {k: v for k, v in here.items() if k not in order[:step]}
            if step < 3:
                k = order[step]
                view = part_view(full, at, columns)
                coming[p, step] = [post(view, view, k, d) for d in range(1, dims()[k][2])]
                if step == 2:
                    coming[p, 3] = [post(view, view, "c", 1)]
            else:
                k = order[2]
                for d in range(1, dims()[k][2]):
                    view = part_view(full, {**at, k: jnp.bitwise_xor(here[k], d)}, columns)
                    coming[p, 3].append(post(view, view, "c", 1))
    for p in range(len(plan)):
        for copy in coming[p, 3]:
            copy.wait_recv()
    for copy in posted:
        copy.wait_send()


def plan_parts(arrays, cut):
    plan = []
    for t, shard in enumerate(arrays):
        pieces = max(1, shard.shape[1] // cut)
        width = shard.shape[1] // pieces
        for i in range(pieces):
            plan.append((t, i * width, width, "zxy" if len(plan) % 2 else "zyx"))
    return plan


def gather_all(shards, cut, number):
    plan = plan_parts(shards, cut)
    size = {k: dims()[k][2] for k in NAMES}
    total = sum(sum(size[k] - 1 for k in order) + size[order[2]] for _, _, _, order in plan)
    fulls = pl.pallas_call(
        functools.partial(gather_kernel, plan),
        name="gather_all",
        in_specs=[pl.BlockSpec(memory_space=pl.ANY)] * len(shards),
        out_specs=[pl.BlockSpec(memory_space=pl.ANY)] * len(shards),
        out_shape=[
            jax.ShapeDtypeStruct((*(size[k] for k in NAMES), *shard.shape), shard.dtype)
            for shard in shards
        ],
        scratch_shapes=[
            pltpu.SemaphoreType.DMA((len(shards),)),
            pltpu.SemaphoreType.DMA((total,)),
            pltpu.SemaphoreType.DMA((total,)),
        ],
        compiler_params=pltpu.CompilerParams(collective_id=number, has_side_effects=True),
    )(*shards)
    return [full.reshape(-1, full.shape[-1]) for full in fulls]


def after(values, earlier):
    return lax.optimization_barrier((values, earlier))[0]


FIRST_PARTS = 3
FEED_LEAD = 4


def feed_kernel(
    shard_ref,
    a_ref,
    at_ref,
    g_ref,
    start_ref,
    wd_ref,
    full_ref,
    y_ref,
    b_ref,
    gd_ref,
    sum_ref,
    weights,
    terms,
    total_1,
    total_2,
    total_3,
    got_c,
    got_1,
    got_2,
    got_z,
    load_sem,
    start_sem,
    own_sem,
    out_send,
    out_recv,
    in_send,
    in_recv,
):
    step = pl.program_id(0)
    width = weights.shape[-1]
    parts = shard_ref.shape[2] // width
    size = {k: v[2] for k, v in dims().items()}
    here = {k: place_along(k) for k in NAMES}
    shard_rows = shard_ref.shape[1]
    orders = ("xy", "yx")

    def columns(p):
        return pl.ds(pl.multiple_of(p * width, width), width)

    def view(which, at, p):
        index = tuple(at[k] if k in at else slice(None) for k in NAMES)
        return full_ref.at[(which,) + index + (slice(None), columns(p))]

    def remote(source, target, sems, p, n, k, d):
        send, recv = sems
        return pltpu.make_async_remote_copy(
            source,
            target,
            send.at[p, n],
            recv.at[p, n],
            device_id=neighbour(k, d),
            device_id_type=MESH,
        )

    def gather_copies(p, stage):
        sems = (out_send, out_recv)
        copies = []
        if stage == 0:
            for d in range(1, size["z"]):
                copies.append(
                    remote(shard_ref.at[:, :, columns(p)], view(slice(None), here, p), sems, p, d - 1, "z", d)
                )
            return copies
        slot = size["z"] - 1
        if stage == 3:
            slot += 2 * (size["x"] + size["y"] - 2)
            at = view(slice(None), {"c": here["c"]}, p)
            return [remote(at, at, sems, p, slot, "c", 1)]
        for which, order in enumerate(orders):
            for s in (1, 2):
                k = order[s - 1]
                gone = "z" + order[: s - 1]
                at = view(which, {q: v for q, v in here.items() if q not in gone}, p)
                for d in range(1, size[k]):
                    if s == stage:
                        copies.append(remote(at, at, sems, p, slot, k, d))
                    slot += 1
        return copies

    def scatter_copies(p, stage):
        sems = (in_send, in_recv)
        if stage == 0:
            return [remote(terms.at[lax.rem(p, 2), :, 1], got_c.at[p], sems, p, 0, "c", 1)]
        copies = []
        slot = 1
        for which, order in enumerate(orders):
            for s in (1, 2):
                k = order[s - 1]
                for d in range(1, size[k]):
                    if s == 1:
                        source = total_1.at[0, d] if k == "x" else total_1.at[1, :, d]
                    else:
                        source = total_2[which].at[d]
                    target = (got_1, got_2)[s - 1][which].at[p, d - 1]
                    if s == stage:
                        copies.append(remote(source, target, sems, p, slot, k, d))
                    slot += 1
        if stage == 3:
            for d in range(1, size["z"]):
                copies.append(remote(total_3.at[:, d], got_z.at[p, d - 1], sems, p, slot + d - 1, "z", d))
        return copies

    def own_copy():
        return pltpu.make_async_copy(shard_ref, full_ref.at[(slice(None),) + tuple(here[k] for k in NAMES)], own_sem)

    def load_copy(p):
        return pltpu.make_async_copy(
            full_ref.at[:, :, :, :, :, :, columns(p)], weights.at[lax.rem(p, 2)], load_sem.at[lax.rem(p, 2)]
        )

    def on(offset, run):
        p = step - offset

        @pl.when((p >= 0) & (p < parts))
        def _():
            run(p)

    def begin(p):
        for copy in gather_copies(p, 0):
            copy.start()

    @pl.when(step == 0)
    def _():
        own_copy().start()
        pltpu.make_async_copy(start_ref, y_ref, start_sem).start()
        greet()

        for p in range(FIRST_PARTS):
            begin(jnp.int32(p))
        own_copy().wait()
        pltpu.make_async_copy(start_ref, y_ref, start_sem).wait()
        b_ref[...] = jnp.zeros_like(b_ref)

    def pass_on(stage):
        def run(p):
            for copy in gather_copies(p, stage - 1):
                copy.wait_recv()
            for copy in gather_copies(p, stage):
                copy.start()

        return run

    def arrived(p):
        for copy in gather_copies(p, 3):
            copy.wait_recv()
        load_copy(p).start()

    @pl.when((step > 0) & (step + FIRST_PARTS - 1 < parts))
    def _():
        begin(step + FIRST_PARTS - 1)

    on(3, arrived)
    on(2, pass_on(3))
    on(1, pass_on(2))
    on(0, pass_on(1))

    def finish(p):
        for copy in scatter_copies(p, 3):
            copy.wait()
        total = total_3[:, 0].astype(F32)
        for d in range(1, size["z"]):
            total = total + got_z[p, d - 1].astype(F32)
        for which in range(2):
            sum_ref[:, pl.ds(pl.multiple_of(which * parts * width + p * width, width), width)] = total[which]

    def third(p):
        for copy in scatter_copies(p, 2):
            copy.wait()
        for which, order in enumerate(orders):
            total = total_2[which][0].astype(F32)
            for d in range(1, size[order[1]]):
                total = total + got_2[which][p, d - 1].astype(F32)
            total_3[which] = total.astype(BF16)
        for copy in scatter_copies(p, 3):
            copy.start()

    def second(p):
        for copy in scatter_copies(p, 1):
            copy.wait()
        for which, order in enumerate(orders):
            kept = total_1[0, 0] if order[0] == "x" else total_1[1, :, 0]
            total = kept.astype(F32)
            for d in range(1, size[order[0]]):
                total = total + got_1[which][p, d - 1].astype(F32)
            total_2[which][...] = total.astype(BF16)
        for copy in scatter_copies(p, 2):
            copy.start()

    def first(p):
        for copy in scatter_copies(p, 0):
            copy.wait()
        total = terms[lax.rem(p, 2), :, 0].astype(F32) + got_c[p].astype(F32)
        total_1[...] = total.astype(BF16)
        for copy in scatter_copies(p, 1):
            copy.start()

    on(FEED_LEAD + 4, finish)
    on(FEED_LEAD + 3, third)
    on(FEED_LEAD + 2, second)
    on(FEED_LEAD + 1, first)

    def compute(p):
        load_copy(p).wait()
        slot = lax.rem(p, 2)
        rows = D
        a, g, wd = a_ref[...], g_ref[...], wd_ref[...]
        wg = weights[slot, 0].reshape(rows, width)
        wu = weights[slot, 1].reshape(rows, width)
        gate = dot(a, wg)
        up = dot(a, wu)
        d_hidden = dot_cols(g, wd)
        sigma = 1.0 / (1.0 + jnp.exp(-gate))
        swish = gate * sigma
        hidden = (swish * up).astype(BF16)
        d_gate = (d_hidden * up * sigma * (1.0 + gate * (1.0 - sigma))).astype(BF16)
        d_up = (d_hidden * swish).astype(BF16)
        y_ref[...] += dot(hidden, wd)
        b_ref[...] += dot_cols(d_gate, wg) + dot_cols(d_up, wu)
        at = at_ref[...]
        shape = (2,) + total_1.shape[1:]
        terms[slot, 0] = dot(at, d_gate).astype(BF16).reshape(shape)
        terms[slot, 1] = dot(at, d_up).astype(BF16).reshape(shape)
        gd_ref[...] = dot_rows(hidden, g).astype(BF16)
        for copy in scatter_copies(p, 0):
            copy.start()

    on(FEED_LEAD, compute)

    @pl.when(step == pl.num_programs(0) - 1)
    def _():
        def end(p, _):
            for stage in range(4):
                for copy in gather_copies(p, stage):
                    copy.wait_send()
            return 0

        lax.fori_loop(0, parts, end, 0)


def feed(shards, a, at, g, w_down, start, number):
    rows = a.shape[0]
    size = {k: v[2] for k, v in dims().items()}
    _, shard_rows, width = shards.shape
    parts = width // FF_BLOCK
    x, y, z = size["x"], size["y"], size["z"]
    last = (z, shard_rows, FF_BLOCK)
    whole = pl.BlockSpec(memory_space=pltpu.VMEM)
    anywhere = pl.BlockSpec(memory_space=pl.ANY)
    row = pl.BlockSpec((FF_BLOCK, D), lambda t: (jnp.clip(t - FEED_LEAD, 0, parts - 1), 0))
    out_count = z - 1 + 2 * (x + y - 2) + 1
    in_count = 1 + 2 * (x + y - 2) + z - 1
    sems = pltpu.SemaphoreType.DMA
    _, y_sum, b_sum, grad_down, sums = pl.pallas_call(
        feed_kernel,
        name="feed",
        grid=(parts + FEED_LEAD + 4,),
        in_specs=[anywhere, whole, whole, whole, anywhere, row],
        out_specs=[anywhere, whole, whole, row, whole],
        out_shape=[
            jax.ShapeDtypeStruct((2, *(size[k] for k in NAMES), shard_rows, width), BF16),
            jax.ShapeDtypeStruct((rows, D), F32),
            jax.ShapeDtypeStruct((rows, D), F32),
            jax.ShapeDtypeStruct((width, D), BF16),
            jax.ShapeDtypeStruct((shard_rows, 2 * width), F32),
        ],
        scratch_shapes=[
            pltpu.VMEM((2, 2, *(size[k] for k in NAMES), shard_rows, FF_BLOCK), BF16),
            pltpu.VMEM((2, 2, 2, x, y, *last), BF16),
            pltpu.VMEM((2, x, y, *last), BF16),
            [pltpu.VMEM((y, *last), BF16), pltpu.VMEM((x, *last), BF16)],
            pltpu.VMEM((2, *last), BF16),
            pltpu.VMEM((parts, 2, x, y, *last), BF16),
            [pltpu.VMEM((parts, x - 1, y, *last), BF16), pltpu.VMEM((parts, y - 1, x, *last), BF16)],
            [pltpu.VMEM((parts, y - 1, *last), BF16), pltpu.VMEM((parts, x - 1, *last), BF16)],
            pltpu.VMEM((parts, z - 1, 2, shard_rows, FF_BLOCK), BF16),
            sems((2,)),
            sems,
            sems,
            sems((parts, out_count)),
            sems((parts, out_count)),
            sems((parts, in_count)),
            sems((parts, in_count)),
        ],
        compiler_params=pltpu.CompilerParams(
            collective_id=number, has_side_effects=True, vmem_limit_bytes=60 << 20
        ),
        cost_estimate=pl.CostEstimate(
            flops=18 * rows * D * width, transcendentals=rows * width, bytes_accessed=12 * D * width
        ),
    )(shards, a, at, g, start, w_down)
    return y_sum, b_sum, grad_down, sums


OUT_PARTS = 2
EXIT_PARTS = OUT_PARTS + 4


def exit_kernel(
    raw_ref,
    dq_ref,
    near_ref,
    back_ref,
    w_ref,
    attn_ref,
    mixed_ref,
    at_ref,
    gain_ref,
    cos_ref,
    sin_ref,
    x_ref,
    norm_ref,
    second_ref,
    grad_ref,
    sum_ref,
    gains_ref,
    part_ref,
    first_ref,
    head_ref,
    terms,
    total_1,
    total_2,
    total_3,
    got_c,
    got_1,
    got_2,
    got_z,
    gains_got,
    in_send,
    in_recv,
    gain_send,
    gain_recv,
):
    step = pl.program_id(0)
    width = terms.shape[-1]
    parts = EXIT_PARTS
    size = {k: v[2] for k, v in dims().items()}
    here = {k: place_along(k) for k in NAMES}
    orders = ("xy", "yx")
    rows = x_ref.shape[0]

    def columns(p):
        return pl.ds(pl.multiple_of(p * width, width), width)

    def remote(source, target, p, n, k, d):
        return pltpu.make_async_remote_copy(
            source,
            target,
            in_send.at[p, n],
            in_recv.at[p, n],
            device_id=neighbour(k, d),
            device_id_type=MESH,
        )

    def scatter_copies(p, stage):
        if stage == 0:
            return [remote(terms.at[lax.rem(p, 2), :, 1], got_c.at[p], p, 0, "c", 1)]
        copies = []
        slot = 1
        for which, order in enumerate(orders):
            for s in (1, 2):
                k = order[s - 1]
                for d in range(1, size[k]):
                    if s == 1:
                        source = total_1.at[0, d] if k == "x" else total_1.at[1, :, d]
                    else:
                        source = total_2[which].at[d]
                    if s == stage:
                        target = (got_1, got_2)[s - 1][which].at[p, d - 1]
                        copies.append(remote(source, target, p, slot, k, d))
                    slot += 1
        if stage == 3:
            for d in range(1, size["z"]):
                copies.append(remote(total_3.at[:, d], got_z.at[p, d - 1], p, slot + d - 1, "z", d))
        return copies

    def on(offset, run):
        p = step - offset

        @pl.when((p >= 0) & (p < parts))
        def _():
            run(p)

    def finish(p):
        for copy in scatter_copies(p, 3):
            copy.wait()
        total = total_3[:, 0].astype(F32)
        for d in range(1, size["z"]):
            total = total + got_z[p, d - 1].astype(F32)
        for which in range(2):
            sum_ref[:, pl.ds(pl.multiple_of((2 * p + which) * width, width), width)] = total[which]

    def third(p):
        for copy in scatter_copies(p, 2):
            copy.wait()
        for which, order in enumerate(orders):
            total = total_2[which][0].astype(F32)
            for d in range(1, size[order[1]]):
                total = total + got_2[which][p, d - 1].astype(F32)
            total_3[which] = total.astype(BF16)
        for copy in scatter_copies(p, 3):
            copy.start()

    def second(p):
        for copy in scatter_copies(p, 1):
            copy.wait()
        for which, order in enumerate(orders):
            kept = total_1[0, 0] if order[0] == "x" else total_1[1, :, 0]
            total = kept.astype(F32)
            for d in range(1, size[order[0]]):
                total = total + got_1[which][p, d - 1].astype(F32)
            total_2[which][...] = total.astype(BF16)
        for copy in scatter_copies(p, 2):
            copy.start()

    def first(p):
        for copy in scatter_copies(p, 0):
            copy.wait()
        total = terms[lax.rem(p, 2), :, 0].astype(F32) + got_c[p].astype(F32)
        total_1[...] = total.astype(BF16)
        for copy in scatter_copies(p, 1):
            copy.start()

    @pl.when(step == 0)
    def _():
        greet()
        first_ref[...] = jnp.zeros_like(first_ref)
        head_ref[...] = jnp.zeros_like(head_ref)

    on(4, finish)
    on(3, third)
    on(2, second)
    on(1, first)

    block = 256

    def turn_back(which, scale):
        def some(i, sums):
            at = pl.ds(pl.multiple_of(i * block, block), block)
            cosine, sine = cos_ref[at, :], sin_ref[at, :]
            for j in range(4):
                part = slice(j * LANES, (j + 1) * LANES)
                u = raw_ref[at, part]
                if which == 0:
                    d = dq_ref[at, part]
                else:
                    d = near_ref[at, part] + back_ref[at, part].astype(F32)
                d = (d * cosine - swap_halves(d) * sine) * scale
                r = lax.rsqrt(head_mean(u * u) + NORM_EPS)
                w = d * gain_ref[which : which + 1]
                n = u * r
                part_ref[at, part] = (r * (w - n * head_mean(w * n))).astype(BF16)
                sums = sums + jnp.sum(d * n, axis=0, keepdims=True)
            return sums

        sums = lax.fori_loop(0, rows // block, some, jnp.zeros((1, LANES), F32))
        head_ref[which : which + 1] += sums

    @pl.when((step >= OUT_PARTS) & (step < OUT_PARTS + 2))
    def _():
        turn_back(0, HEAD_SIZE**-0.5)

    @pl.when(step == OUT_PARTS + 2)
    def _():
        turn_back(1, 1.0)

    @pl.when(step == OUT_PARTS + 3)
    def _():
        part_ref[...] = (near_ref[...] + back_ref[...].astype(F32)).astype(BF16)

    def compute(p):
        shape = (2,) + total_1.shape[1:]
        slot = lax.rem(p, 2)

        @pl.when(p < OUT_PARTS)
        def _():
            for half in range(2):
                some = attn_ref[:, half * width : (half + 1) * width]
                terms[slot, half] = dot(mixed_ref[...], some).astype(BF16).reshape(shape)

        @pl.when(p >= OUT_PARTS)
        def _():
            first_ref[...] += dot_cols(part_ref[...], w_ref[...])
            for half in range(2):
                some = part_ref[:, half * width : (half + 1) * width]
                terms[slot, half] = dot(at_ref[...], some).astype(BF16).reshape(shape)

        for copy in scatter_copies(p, 0):
            copy.start()

    on(0, compute)

    @pl.when(step == parts - 1)
    def _():
        gain = norm_ref[0:1]

        def some(i, sums):
            at = pl.ds(pl.multiple_of(i * block, block), block)
            v = x_ref[at, :].astype(F32)
            scale = lax.rsqrt(jnp.mean(v * v, axis=-1, keepdims=True) + NORM_EPS)
            d = first_ref[at, :]
            n = v * scale
            w = d * gain
            mean = jnp.mean(w * n, axis=-1, keepdims=True)
            grad_ref[at, :] = (scale * (w - n * mean)).astype(BF16)
            return sums + jnp.sum(d * n, axis=0, keepdims=True)

        sums = lax.fori_loop(0, rows // block, some, jnp.zeros((1, D), F32))
        gains_ref[...] = jnp.zeros_like(gains_ref)
        gains_ref[0:1] = sums
        gains_ref[1:2] = second_ref[0:1]
        gains_ref[2:4, :LANES] = head_ref[0:2]

    stage = 0
    for k in NAMES:
        d = 1
        while d < size[k]:

            @pl.when(step == parts + stage // 2)
            def _(k=k, d=d, stage=stage):
                copy = pltpu.make_async_remote_copy(
                    gains_ref,
                    gains_got.at[stage],
                    gain_send.at[stage],
                    gain_recv.at[stage],
                    device_id=neighbour(k, d),
                    device_id_type=MESH,
                )
                copy.start()
                copy.wait()
                gains_ref[...] += gains_got[stage]

            d *= 2
            stage += 1


def leave(raw, dq, near, back, w, d_attn, mixed_rows, at, gains, cosine, sine, x, norm_gains, second, number):
    rows = x.shape[0]
    size = {k: v[2] for k, v in dims().items()}
    xs, ys, zs = size["x"], size["y"], size["z"]
    width = 256
    shard_rows = D // math.prod(size.values())
    last = (zs, shard_rows, width)
    parts = EXIT_PARTS
    whole = pl.BlockSpec(memory_space=pltpu.VMEM)
    block = lambda size, start, count: pl.BlockSpec(
        (size, 2 * width), lambda t: (0, jnp.clip(t - start, 0, count - 1))
    )
    in_count = 1 + 2 * (xs + ys - 2) + zs - 1
    stages = sum(v.bit_length() - 1 for v in size.values())
    sems = pltpu.SemaphoreType.DMA
    return pl.pallas_call(
        exit_kernel,
        name="leave",
        grid=(parts + 4,),
        in_specs=[
            block(rows, OUT_PARTS, 4),
            block(rows, OUT_PARTS, 2),
            block(rows, OUT_PARTS + 2, 2),
            block(rows, OUT_PARTS + 2, 2),
            block(D, OUT_PARTS, 4),
            block(rows, 0, 2),
        ]
        + [whole] * 8,
        out_specs=[whole] * 3,
        out_shape=[
            jax.ShapeDtypeStruct((rows, D), BF16),
            jax.ShapeDtypeStruct((shard_rows, 2 * parts * width), F32),
            jax.ShapeDtypeStruct((8, D), F32),
        ],
        scratch_shapes=[
            pltpu.VMEM((rows, 2 * width), BF16),
            pltpu.VMEM((rows, D), F32),
            pltpu.VMEM((8, LANES), F32),
            pltpu.VMEM((2, 2, 2, xs, ys, *last), BF16),
            pltpu.VMEM((2, xs, ys, *last), BF16),
            [pltpu.VMEM((ys, *last), BF16), pltpu.VMEM((xs, *last), BF16)],
            pltpu.VMEM((2, *last), BF16),
            pltpu.VMEM((parts, 2, xs, ys, *last), BF16),
            [pltpu.VMEM((parts, xs - 1, ys, *last), BF16), pltpu.VMEM((parts, ys - 1, xs, *last), BF16)],
            [pltpu.VMEM((parts, ys - 1, *last), BF16), pltpu.VMEM((parts, xs - 1, *last), BF16)],
            pltpu.VMEM((parts, zs - 1, 2, shard_rows, width), BF16),
            pltpu.VMEM((stages, 8, D), F32),
            sems((parts, in_count)),
            sems((parts, in_count)),
            sems((stages,)),
            sems((stages,)),
        ],
        compiler_params=pltpu.CompilerParams(
            collective_id=number, has_side_effects=True, vmem_limit_bytes=56 << 20
        ),
        cost_estimate=pl.CostEstimate(flops=rows << 20, transcendentals=0, bytes_accessed=rows << 10),
    )(raw, dq, near, back, w, d_attn, mixed_rows, at, gains, cosine, sine, x, norm_gains, second)


def add_swapped(keep, send, direction):
    return (keep.astype(F32) + swap(send, direction, 1).astype(F32)).astype(BF16)


def add_along(terms, direction, last=False):
    size = dims()[direction][2]
    step = terms.shape[0] // size
    total = terms[:step].astype(F32)
    for d in range(1, size):
        total = total + swap(terms[d * step : (d + 1) * step], direction, d).astype(F32)
    return total if last else total.astype(BF16)


def own_part(terms, direction, last=False):
    at, here, size = NAMES.index(direction), place_along(direction), dims()[direction][2]
    total = lax.dynamic_slice_in_dim(terms, here, 1, at).astype(F32)
    for d in range(1, size):
        sent = lax.dynamic_slice_in_dim(terms, jnp.bitwise_xor(here, d), 1, at)
        total = total + swap(sent, direction, d).astype(F32)
    return total if last else total.astype(BF16)


def per_device(
    inputs,
    cotangent,
    lengths,
    norm_gains,
    norm_first,
    norm_second,
    qk_gains,
    qk_first,
    qk_second,
    qkv_master,
    qkv_first,
    qkv_second,
    out_master,
    out_first,
    out_second,
    gate_up_master,
    gate_up_first,
    gate_up_second,
    down_master,
    down_first,
    down_second,
):
    seq_width = lax.axis_size("seq")
    turn_here = lax.axis_index("seq")
    rows = inputs.shape[1]
    block = QUERY_BLOCK
    w_qkv, w_out = gather_all([qkv_master.astype(BF16), out_master.astype(BF16)], 512, 1)

    places = turn_here * rows + jnp.arange(rows, dtype=jnp.int32)
    row_lengths = lengths[0]
    doc_ends = jnp.cumsum(row_lengths)
    passed = doc_ends[None, :] <= places[:, None]
    begins = jnp.sum(jnp.where(passed, row_lengths[None, :], 0), axis=1)
    cosine, sine = rotation_tables(places - begins)
    if seq_width == 2:
        base = (turn_here - 1) * rows
    else:
        base = turn_here * 0
    first = (begins - base).astype(jnp.int32)
    low = jnp.concatenate([(turn_here * rows - base)[None], first[::block]]).astype(jnp.int32)
    first_wide = jnp.broadcast_to(first[:, None], (rows, LANES))
    first_lane = jnp.broadcast_to(first[None, :], (8, rows))

    x = inputs[0].astype(F32)
    scale_first = rms_scale(x)
    normed_first = (x * scale_first * norm_gains[0]).astype(BF16)
    raw = jnp.dot(normed_first, w_qkv, preferred_element_type=F32)
    gain_rows = jnp.pad(jnp.tile(qk_gains, (1, 2)), ((0, 6), (0, 0)))
    q, *own = prep(raw, gain_rows, cosine, sine)
    if seq_width == 2:
        others = [lax.ppermute(p, "seq", [(0, 1)]) for p in own]
    else:
        others = [lax.all_gather(p, "seq", axis=0, tiled=True) for p in own]
    w_down = gather(after(down_master.astype(BF16), others[3]))
    mixed, lse = attend(q, others, own, low, first_wide)
    x_mid = x + jnp.dot(mixed, w_out, preferred_element_type=F32)
    scale_second = rms_scale(x_mid)
    normed_second = (x_mid * scale_second * norm_gains[1]).astype(BF16)
    g = cotangent[0]
    hot_x = relative_rows("cxyz", D)
    shards = jnp.stack([gate_up_master[:, :FF], gate_up_master[:, FF:]]).astype(BF16)
    out_sum, d_b, grad_down, gate_up_sums = feed(
        after(shards, normed_second),
        normed_second,
        transpose_in_order(hot_x, normed_second),
        g,
        w_down,
        x_mid,
        2,
    )
    outputs = out_sum.astype(BF16)
    down_grad = lax.psum_scatter(grad_down, ALL, scatter_dimension=0, tiled=True).astype(F32)
    d_norm, d_gain_second = rms_back(x_mid, scale_second, norm_gains[1], d_b)
    d_mid = g.astype(F32) + d_norm
    d_attn = d_mid.astype(BF16)
    d_mixed = dot_cols(d_attn, w_out).astype(BF16)
    zero = jnp.zeros((rows, QUERY_FEATURES), F32)
    dq, far = attend_back(0, q, d_mixed, mixed, lse, zero, others, low, first_lane, BF16)
    if seq_width == 2:
        back = lax.ppermute(far, "seq", [(1, 0)])
    else:
        back = lax.psum_scatter(far, "seq", scatter_dimension=0, tiled=True)
    dq, near = attend_back(
        others[0].shape[0], q, d_mixed, mixed, lse, dq, own, low, first_lane, F32
    )
    d_x, sums, gain_sums = leave(
        raw,
        dq,
        near,
        back,
        w_qkv,
        d_attn,
        transpose_in_order(hot_x, mixed),
        transpose_in_order(hot_x, normed_first),
        gain_rows,
        cosine,
        sine,
        inputs[0],
        jnp.pad(norm_gains, ((0, 6), (0, 0))),
        jnp.broadcast_to(d_gain_second[None], (8, D)),
        3,
    )
    input_grad = (d_mid + d_x.astype(F32))[None]
    out_grad, qkv_grad = sums[:, :D], sums[:, D:]
    norm_grad = gain_sums[:2]
    qk_grad = gain_sums[2:4, :HEAD_SIZE] + gain_sums[2:4, HEAD_SIZE:LANES]

    norm_new = adam_update(norm_gains, norm_first, norm_second, norm_grad, GAIN_RATE, 0.0)
    qk_new = adam_update(qk_gains, qk_first, qk_second, qk_grad, GAIN_RATE, 0.0)
    qkv_new = adam_update(qkv_master, qkv_first, qkv_second, qkv_grad, D**-0.5, DECAY_RATE)
    out_new = adam_update(
        out_master, out_first, out_second, out_grad, (QUERY_FEATURES // 16) ** -0.5, DECAY_RATE
    )
    gate_new = adam_update(
        gate_up_master, gate_up_first, gate_up_second, gate_up_sums, D**-0.5, DECAY_RATE
    )
    down_new = adam_update(down_master, down_first, down_second, down_grad, FF**-0.5, DECAY_RATE)
    return (
        outputs[None],
        input_grad,
        *norm_new,
        *qk_new,
        *qkv_new,
        *out_new,
        *gate_new,
        *down_new,
    )


def solution(mesh):
    token = P("fsdp", "seq", None)
    weight = P(ALL, None)
    return jax.shard_map(
        per_device,
        mesh=mesh,
        in_specs=(token, token, P("fsdp", None)) + (P(),) * 6 + (weight,) * 12,
        out_specs=(token, token) + (P(),) * 6 + (weight,) * 12,
        check_vma=False,
    )
```

```python
import functools
import math

import jax
import jax.numpy as jnp
from jax import lax
from jax.experimental import pallas as pl
from jax.experimental.pallas import tpu as pltpu
from jax.sharding import PartitionSpec as P

D = 1024
HQ = 16
KEY_VALUE_HEADS = 8
HEAD_SIZE = 64
FF = 4608
QUERY_FEATURES = 1024
KEY_FEATURES = 512
STEP = 10
LANES = 128

NORM_EPS = 1e-05
ROPE_BASE = 1000000.0
BETA_ONE = 0.9
BETA_TWO = 0.95
ADAM_EPS = 1e-08
DECAY_RATE = 0.1
GAIN_RATE = 0.3

F32 = jnp.float32
BF16 = jnp.bfloat16
QUERY_BLOCK = 128
KEY_BLOCK = 256
FF_BLOCK = 256
PIECES = 4


def dot(a, b):
    return lax.dot_general(a, b, (((1,), (0,)), ((), ())), preferred_element_type=F32)


def dot_cols(a, b):
    return lax.dot_general(a, b, (((1,), (1,)), ((), ())), preferred_element_type=F32)


def dot_rows(a, b):
    return lax.dot_general(a, b, (((0,), (0,)), ((), ())), preferred_element_type=F32)


def params(limit=56):
    return pltpu.CompilerParams(vmem_limit_bytes=limit << 20)


def head_mean(v):
    row = lax.broadcasted_iota(jnp.int32, (LANES, LANES), 0) // HEAD_SIZE
    col = lax.broadcasted_iota(jnp.int32, (LANES, LANES), 1) // HEAD_SIZE
    ones = jnp.where(row == col, 1.0 / HEAD_SIZE, 0.0).astype(BF16)
    high = v.astype(BF16)
    low = (v - high.astype(F32)).astype(BF16)
    return dot(high, ones) + dot(low, ones)


def swap_halves(v):
    lane = lax.broadcasted_iota(jnp.int32, v.shape, 1) % HEAD_SIZE
    return jnp.where(
        lane < HEAD_SIZE // 2,
        pltpu.roll(v, LANES - HEAD_SIZE // 2, 1),
        pltpu.roll(v, HEAD_SIZE // 2, 1),
    )


def prep_kernel(raw_ref, gain_ref, cos_ref, sin_ref, q_ref, *kv_refs):
    cosine, sine = cos_ref[...], sin_ref[...]
    for group in range(12):
        part = slice(group * LANES, (group + 1) * LANES)
        u = raw_ref[:, part]
        gain = gain_ref[0:1] if group < 8 else gain_ref[1:2]
        n = u * lax.rsqrt(head_mean(u * u) + NORM_EPS) * gain
        out = n * cosine + swap_halves(n) * sine
        if group < 8:
            q_ref[:, part] = (out * HEAD_SIZE**-0.5).astype(BF16)
        else:
            kv_ref = kv_refs[group - 8]
            kv_ref[:, :LANES] = out.astype(BF16)
            value = raw_ref[:, slice((group + 4) * LANES, (group + 5) * LANES)]
            kv_ref[:, LANES:] = value.astype(BF16)


def prep(raw, gains, cosine, sine):
    rows = raw.shape[0]
    block = min(rows, 256)
    whole = lambda width: pl.BlockSpec((block, width), lambda i: (i, 0))
    return pl.pallas_call(
        prep_kernel,
        name="prep",
        grid=(rows // block,),
        in_specs=[whole(2048), pl.BlockSpec((8, LANES), lambda i: (0, 0)), whole(LANES), whole(LANES)],
        out_specs=[whole(QUERY_FEATURES)] + [whole(2 * LANES)] * PIECES,
        out_shape=[jax.ShapeDtypeStruct((rows, QUERY_FEATURES), BF16)]
        + [jax.ShapeDtypeStruct((rows, 2 * LANES), BF16)] * PIECES,
        compiler_params=params(),
        cost_estimate=pl.CostEstimate(
            flops=rows * 2048 * 40, transcendentals=rows * 24, bytes_accessed=rows * 2048 * 6
        ),
    )(raw, gains, cosine, sine)


def stack_heads(rows):
    first, second = rows[:, :LANES].astype(F32), rows[:, LANES:].astype(F32)
    lane = lax.broadcasted_iota(jnp.int32, first.shape, 1)
    low = lane < HEAD_SIZE
    turn = lambda v: pltpu.roll(v, HEAD_SIZE, 1)
    heads = [
        jnp.where(low, first, 0.0),
        jnp.where(low, turn(first), 0.0),
        jnp.where(low, 0.0, turn(second)),
        jnp.where(low, 0.0, second),
    ]
    return jnp.concatenate(heads, axis=0).astype(BF16)


def unstack_heads(tall):
    n = tall.shape[0] // 4
    a, b, c, d = (tall[i * n : (i + 1) * n] for i in range(4))
    low = lax.broadcasted_iota(jnp.int32, a.shape, 1) < HEAD_SIZE
    turn = lambda v: pltpu.roll(v, HEAD_SIZE, 1)
    return jnp.concatenate([jnp.where(low, a, turn(b)), jnp.where(low, turn(c), d)], axis=1)


def key_range(low_ref, turn, block, start, rows):
    begin = low_ref[1 + turn] // KEY_BLOCK
    end = (low_ref[0] + turn * block + block - 1) // KEY_BLOCK + 1
    first, last = start // KEY_BLOCK, (start + rows) // KEY_BLOCK
    return jnp.clip(begin, first, last), jnp.clip(end, first, last)


def attend_kernel(low_ref, first_ref, q_ref, *rest):
    sources = (rest[:PIECES], rest[PIECES : 2 * PIECES])
    out_ref, lse_ref, queries, totals = rest[2 * PIECES :]
    turn = pl.program_id(0)
    block = q_ref.shape[0]
    for p in range(PIECES):
        queries[p] = stack_heads(q_ref[:, p * 2 * LANES : (p + 1) * 2 * LANES])
    totals[...] = jnp.zeros_like(totals)
    place = low_ref[0] + turn * block + lax.broadcasted_iota(jnp.int32, (block, KEY_BLOCK), 0)
    first = jnp.concatenate([first_ref[...]] * (KEY_BLOCK // LANES), axis=1)
    column = lax.broadcasted_iota(jnp.int32, (block, KEY_BLOCK), 1)
    ones = jnp.ones((KEY_BLOCK, LANES), BF16)
    start = 0
    for refs in sources:
        rows = refs[0].shape[0]

        def step(at, _):
            span = pl.ds(pl.multiple_of(at * KEY_BLOCK - start, KEY_BLOCK), KEY_BLOCK)
            key_place = at * KEY_BLOCK + column
            allowed = (key_place >= first) & (key_place <= place)
            for p in range(PIECES):
                scores = dot_cols(queries[p], refs[p][span, :LANES])
                scores = scores.reshape(4, block, KEY_BLOCK)
                powers = jnp.where(allowed[None], jnp.exp(scores), 0.0).astype(BF16)
                values = jnp.concatenate([refs[p][span, LANES:], ones], axis=1)
                totals[p] += dot(powers.reshape(4 * block, KEY_BLOCK), values)
            return 0

        begin, end = key_range(low_ref, turn, block, start, rows)
        lax.fori_loop(begin, end, step, 0)
        start += rows
    for p in range(PIECES):
        mass = totals[p, :, LANES:]
        mixed = totals[p, :, :LANES] / mass
        out_ref[:, p * 2 * LANES : (p + 1) * 2 * LANES] = unstack_heads(mixed).astype(BF16)
        lse_ref[:, p * 4 * block : (p + 1) * 4 * block] = jnp.transpose(jnp.log(mass))[0:8, :]


def attend(q, others, own, low, first):
    rows = q.shape[0]
    block = QUERY_BLOCK
    turns = rows // block
    whole = lambda size: pl.BlockSpec((size, 2 * LANES), lambda t, low: (0, 0))
    wide = pl.BlockSpec((block, QUERY_FEATURES), lambda t, low: (t, 0))
    return pl.pallas_call(
        attend_kernel,
        name="attend",
        grid_spec=pltpu.PrefetchScalarGridSpec(
            num_scalar_prefetch=1,
            grid=(turns,),
            in_specs=[pl.BlockSpec((block, LANES), lambda t, low: (t, 0)), wide]
            + [whole(others[0].shape[0])] * PIECES
            + [whole(rows)] * PIECES,
            out_specs=[wide, pl.BlockSpec((8, HQ * block), lambda t, low: (t, 0))],
            scratch_shapes=[
                pltpu.VMEM((PIECES, 4 * block, LANES), BF16),
                pltpu.VMEM((PIECES, 4 * block, 2 * LANES), F32),
            ],
        ),
        out_shape=[
            jax.ShapeDtypeStruct((rows, QUERY_FEATURES), BF16),
            jax.ShapeDtypeStruct((8 * turns, HQ * block), F32),
        ],
        compiler_params=params(),
        cost_estimate=pl.CostEstimate(
            flops=rows * 1024 * 1024 * 24, transcendentals=rows * 1024 * 16, bytes_accessed=16 << 20
        ),
    )(low, first, q, *others, *own)


def attend_back_kernel(
    start, pieces, count, low_ref, first_ref, q_ref, do_ref, mixed_ref, lse_ref, *rest
):
    befores, refs = rest[:count], rest[count : count + len(pieces)]
    d_ref, dq_ref, queries, rising, deltas, dqs, dkvs = rest[count + len(pieces) :]
    turn = pl.program_id(0)
    block = q_ref.shape[0]
    rows = refs[0].shape[0]
    tall = 4 * block

    @pl.when(turn == 0)
    def _():
        dkvs[...] = jnp.zeros_like(dkvs)

    begin, end = key_range(low_ref, turn, block, start, rows)

    @pl.when(end <= begin)
    def _():
        if befores:
            dq_ref[...] = jnp.concatenate([ref[...] for ref in befores], axis=1)
        else:
            dq_ref[...] = jnp.zeros_like(dq_ref)

    @pl.when(end > begin)
    def _():
        for p, piece in enumerate(pieces):
            part = slice(piece * 2 * LANES, (piece + 1) * 2 * LANES)
            queries[p] = stack_heads(q_ref[:, part])
            rising[p] = stack_heads(do_ref[:, part])
            across = jnp.transpose(do_ref[:, part].astype(F32) * mixed_ref[:, part].astype(F32))
            deltas[p] = jnp.concatenate(
                [
                    jnp.broadcast_to(
                        jnp.sum(across[i * HEAD_SIZE : (i + 1) * HEAD_SIZE], axis=0, keepdims=True),
                        (8, block),
                    )
                    for i in range(4)
                ],
                axis=1,
            )
        dqs[...] = jnp.zeros_like(dqs)
        shape = (KEY_BLOCK, block)
        place = low_ref[0] + turn * block + lax.broadcasted_iota(jnp.int32, shape, 1)
        row = lax.broadcasted_iota(jnp.int32, shape, 0)
        first = first_ref[0:1]

        def step(at, _):
            span = pl.ds(pl.multiple_of(at * KEY_BLOCK - start, KEY_BLOCK), KEY_BLOCK)
            key_place = at * KEY_BLOCK + row
            allowed = (key_place >= first) & (key_place <= place)
            allowed = jnp.concatenate([allowed] * 4, axis=1)
            for p, piece in enumerate(pieces):
                key, value = refs[p][span, :LANES], refs[p][span, LANES:]
                logs = lse_ref[0:1, piece * tall : (piece + 1) * tall]
                probs = jnp.where(allowed, jnp.exp(dot_cols(key, queries[p]) - logs), 0.0)
                dprobs = dot_cols(value, rising[p])
                dscores = (probs * (dprobs - deltas[p, 0:1])).astype(BF16)
                dkvs[p, span, :LANES] += dot(dscores, queries[p])
                dkvs[p, span, LANES:] += dot(probs.astype(BF16), rising[p])
                dqs[p] += dot_rows(dscores, key)
            return 0

        lax.fori_loop(begin, end, step, 0)
        for p in range(len(pieces)):
            part = slice(p * 2 * LANES, (p + 1) * 2 * LANES)
            total = unstack_heads(dqs[p])
            if befores:
                each = len(pieces) // count
                at = p % each * 2 * LANES
                total = total + befores[p // each][:, at : at + 2 * LANES]
            dq_ref[:, part] = total

    @pl.when(turn == pl.num_programs(0) - 1)
    def _():
        for p in range(len(pieces)):
            for half in range(2):
                at = (half * len(pieces) + p) * LANES
                part = slice(at, at + LANES)
                d_ref[:, part] = dkvs[p, :, half * LANES : (half + 1) * LANES].astype(d_ref.dtype)


def attend_back(start, pieces, q, d_mixed, mixed, lse, befores, source, low, first_lane, kind):
    rows = q.shape[0]
    block = QUERY_BLOCK
    turns = rows // block
    count = source[0].shape[0]
    some = len(pieces)
    whole = pl.BlockSpec((count, some * 2 * LANES), lambda t, low: (0, 0))
    part = lambda width: pl.BlockSpec((block, width), lambda t, low: (t, 0))
    wide = pl.BlockSpec((block, QUERY_FEATURES), lambda t, low: (t, 0))
    d_keys, dq = pl.pallas_call(
        functools.partial(attend_back_kernel, start, pieces, len(befores)),
        name="attend_back",
        grid_spec=pltpu.PrefetchScalarGridSpec(
            num_scalar_prefetch=1,
            grid=(turns,),
            in_specs=[
                pl.BlockSpec((8, block), lambda t, low: (0, t)),
                wide,
                wide,
                wide,
                pl.BlockSpec((8, HQ * block), lambda t, low: (t, 0)),
            ]
            + [part(v.shape[1]) for v in befores]
            + [pl.BlockSpec((count, 2 * LANES), lambda t, low: (0, 0))] * some,
            out_specs=[whole, part(some * 2 * LANES)],
            scratch_shapes=[
                pltpu.VMEM((some, 4 * block, LANES), BF16),
                pltpu.VMEM((some, 4 * block, LANES), BF16),
                pltpu.VMEM((some, 8, 4 * block), F32),
                pltpu.VMEM((some, 4 * block, LANES), F32),
                pltpu.VMEM((some, count, 2 * LANES), F32),
            ],
        ),
        out_shape=[
            jax.ShapeDtypeStruct((count, some * 2 * LANES), kind),
            jax.ShapeDtypeStruct((rows, some * 2 * LANES), F32),
        ],
        compiler_params=params(),
        cost_estimate=pl.CostEstimate(
            flops=rows << 18, transcendentals=0, bytes_accessed=rows << 8
        ),
    )(low, first_lane, q, d_mixed, mixed, lse, *befores, *[source[p] for p in pieces])
    return dq, d_keys


def rms_scale(v):
    return lax.rsqrt(jnp.mean(v * v, axis=-1, keepdims=True) + NORM_EPS)


def rms_back(v, scale, gain_row, d_out):
    w = d_out * gain_row
    n = v * scale
    d_v = scale * (w - n * jnp.mean(w * n, axis=-1, keepdims=True))
    return d_v, jnp.sum(d_out * n, axis=0)


def adam_update(master, first_moment, second_moment, gradient, rate, decay):
    first_moment = BETA_ONE * first_moment + (1.0 - BETA_ONE) * gradient
    second_moment = BETA_TWO * second_moment + (1.0 - BETA_TWO) * gradient * gradient
    corrected = (
        first_moment
        / (1.0 - BETA_ONE**STEP)
        / (jnp.sqrt(second_moment / (1.0 - BETA_TWO**STEP)) + ADAM_EPS)
    )
    return (master - rate * (corrected + decay * master), first_moment, second_moment)


def rotation_tables(position):
    half = HEAD_SIZE // 2
    index_row = jnp.arange(half, dtype=F32)
    frequency = jnp.exp(index_row * (-2.0 * math.log(ROPE_BASE) / HEAD_SIZE))
    angles = position.astype(F32)[:, None] * frequency[None, :]
    cosine, sine = jnp.cos(angles), jnp.sin(angles)
    return (
        jnp.concatenate([cosine] * 4, axis=1),
        jnp.concatenate([-sine, sine, -sine, sine], axis=1),
    )


ALL = ("fsdp", "seq")


def gather(shard):
    return lax.all_gather(shard, ALL, axis=0, tiled=True)


def dims():
    rest = lax.axis_size("fsdp") // 8
    return {
        "z": ("fsdp", 2 * rest, 4),
        "y": ("fsdp", 2, rest),
        "c": ("fsdp", 1, 2),
        "x": ("seq", 1, lax.axis_size("seq")),
    }


def place_along(direction):
    axis, stride, size = dims()[direction]
    return lax.rem(lax.div(lax.axis_index(axis), stride), size)


def swap(value, direction, distance):
    axis, stride, _ = dims()[direction]
    pairs = [(i, i ^ (distance * stride)) for i in range(lax.axis_size(axis))]
    return lax.ppermute(value, axis, pairs)


def relative_rows(order, count):
    sizes = {k: v[2] for k, v in dims().items()}
    width = count
    for size in sizes.values():
        width //= size
    index = jnp.arange(count, dtype=jnp.int32)
    left = index // width
    place = {}
    for k in reversed(order):
        place[k] = jnp.bitwise_xor(left % sizes[k], place_along(k))
        left = left // sizes[k]
    block = jnp.zeros_like(index)
    for k in "zycx":
        block = block * sizes[k] + place[k]
    row = block * width + index % width
    return (row[:, None] == index[None, :]).astype(BF16)


def transpose_in_order(hot, value):
    return dot_cols(hot, value).astype(BF16)


MESH = pl.DeviceIdType.MESH
NAMES = "zycx"


def neighbour(direction, distance):
    axis, stride, _ = dims()[direction]
    here = place_along(direction)
    return {axis: lax.axis_index(axis) + (jnp.bitwise_xor(here, distance) - here) * stride}


def greet():
    barrier = pltpu.get_barrier_semaphore()
    count = 0
    for k in NAMES:
        for d in range(1, dims()[k][2]):
            pl.semaphore_signal(barrier, 1, device_id=neighbour(k, d), device_id_type=MESH)
            count += 1
    pl.semaphore_wait(barrier, count)


def part_view(full, at, columns):
    index = tuple(at[k] if k in at else slice(None) for k in NAMES)
    return full.at[index + (slice(None), columns)]


def gather_kernel(plan, *refs):
    count = 1 + max(p[0] for p in plan)
    shards, fulls = refs[:count], refs[count : 2 * count]
    local, send, recv = refs[2 * count :]
    here = {k: place_along(k) for k in NAMES}
    own = []
    for t in range(count):
        copy = pltpu.make_async_copy(shards[t], part_view(fulls[t], here, slice(None)), local.at[t])
        copy.start()
        own.append(copy)
    greet()
    posted = []

    def post(source, target, k, d):
        n = len(posted)
        copy = pltpu.make_async_remote_copy(
            source, target, send.at[n], recv.at[n], device_id=neighbour(k, d), device_id_type=MESH
        )
        copy.start()
        posted.append(copy)
        return copy

    coming = {}
    for when in range(len(plan) + 3):
        for step in range(4):
            p = when - step
            if not 0 <= p < len(plan):
                continue
            t, column, width, order = plan[p]
            columns = pl.ds(column, width)
            full = fulls[t]
            if step == 0:
                k = order[0]
                target = part_view(full, here, columns)
                coming[p, 0] = [
                    post(shards[t].at[:, columns], target, k, d) for d in range(1, dims()[k][2])
                ]
                continue
            if own[t] is not None:
                own[t].wait()
                own[t] = None
            for copy in coming[p, step - 1]:
                copy.wait_recv()
            at = {k: v for k, v in here.items() if k not in order[:step]}
            if step < 3:
                k = order[step]
                view = part_view(full, at, columns)
                coming[p, step] = [post(view, view, k, d) for d in range(1, dims()[k][2])]
                if step == 2:
                    coming[p, 3] = [post(view, view, "c", 1)]
            else:
                k = order[2]
                for d in range(1, dims()[k][2]):
                    view = part_view(full, {**at, k: jnp.bitwise_xor(here[k], d)}, columns)
                    coming[p, 3].append(post(view, view, "c", 1))
    for p in range(len(plan)):
        for copy in coming[p, 3]:
            copy.wait_recv()
    for copy in posted:
        copy.wait_send()


def plan_parts(arrays, cut):
    plan = []
    for t, shard in enumerate(arrays):
        pieces = max(1, shard.shape[1] // cut)
        width = shard.shape[1] // pieces
        for i in range(pieces):
            plan.append((t, i * width, width, "zxy" if len(plan) % 2 else "zyx"))
    return plan


def gather_all(shards, cut, number):
    plan = plan_parts(shards, cut)
    size = {k: dims()[k][2] for k in NAMES}
    total = sum(sum(size[k] - 1 for k in order) + size[order[2]] for _, _, _, order in plan)
    fulls = pl.pallas_call(
        functools.partial(gather_kernel, plan),
        name="gather_all",
        in_specs=[pl.BlockSpec(memory_space=pl.ANY)] * len(shards),
        out_specs=[pl.BlockSpec(memory_space=pl.ANY)] * len(shards),
        out_shape=[
            jax.ShapeDtypeStruct((*(size[k] for k in NAMES), *shard.shape), shard.dtype)
            for shard in shards
        ],
        scratch_shapes=[
            pltpu.SemaphoreType.DMA((len(shards),)),
            pltpu.SemaphoreType.DMA((total,)),
            pltpu.SemaphoreType.DMA((total,)),
        ],
        compiler_params=pltpu.CompilerParams(collective_id=number, has_side_effects=True),
    )(*shards)
    return [full.reshape(-1, full.shape[-1]) for full in fulls]


def after(values, earlier):
    return lax.optimization_barrier((values, earlier))[0]


FIRST_PARTS = 6
SLACK = 2
TERM_SLOTS = SLACK + 1
FEED_LEAD = 3 * SLACK + 1


def feed_kernel(
    shard_ref,
    a_ref,
    at_ref,
    g_ref,
    start_ref,
    wd_ref,
    full_ref,
    y_ref,
    b_ref,
    gd_ref,
    sum_ref,
    weights,
    terms,
    total_1,
    total_2,
    total_3,
    got_c,
    got_1,
    got_2,
    got_z,
    load_sem,
    start_sem,
    own_sem,
    out_send,
    out_recv,
    in_send,
    in_recv,
):
    step = pl.program_id(0)
    width = weights.shape[-1]
    parts = shard_ref.shape[2] // width
    size = {k: v[2] for k, v in dims().items()}
    here = {k: place_along(k) for k in NAMES}
    shard_rows = shard_ref.shape[1]
    orders = ("xy", "yx")

    def columns(p):
        return pl.ds(pl.multiple_of(p * width, width), width)

    def view(which, at, p):
        index = tuple(at[k] if k in at else slice(None) for k in NAMES)
        return full_ref.at[(which,) + index + (slice(None), columns(p))]

    def remote(source, target, sems, p, n, k, d):
        send, recv = sems
        return pltpu.make_async_remote_copy(
            source,
            target,
            send.at[p, n],
            recv.at[p, n],
            device_id=neighbour(k, d),
            device_id_type=MESH,
        )

    def gather_copies(p, stage):
        sems = (out_send, out_recv)
        copies = []
        if stage == 0:
            for d in range(1, size["z"]):
                copies.append(
                    remote(shard_ref.at[:, :, columns(p)], view(slice(None), here, p), sems, p, d - 1, "z", d)
                )
            return copies
        slot = size["z"] - 1
        if stage == 3:
            slot += 2 * (size["x"] + size["y"] - 2)
            at = view(slice(None), {"c": here["c"]}, p)
            return [remote(at, at, sems, p, slot, "c", 1)]
        for which, order in enumerate(orders):
            for s in (1, 2):
                k = order[s - 1]
                gone = "z" + order[: s - 1]
                at = view(which, {q: v for q, v in here.items() if q not in gone}, p)
                for d in range(1, size[k]):
                    if s == stage:
                        copies.append(remote(at, at, sems, p, slot, k, d))
                    slot += 1
        return copies

    def scatter_copies(p, stage):
        sems = (in_send, in_recv)
        if stage == 0:
            return [remote(terms.at[lax.rem(p, TERM_SLOTS), :, 1], got_c.at[p], sems, p, 0, "c", 1)]
        copies = []
        slot, slot_now = 1, lax.rem(p, 2)
        for which, order in enumerate(orders):
            for s in (1, 2):
                k = order[s - 1]
                for d in range(1, size[k]):
                    if s == 1:
                        source = total_1.at[slot_now, 0, d] if k == "x" else total_1.at[slot_now, 1, :, d]
                    else:
                        source = total_2[which].at[slot_now, d]
                    target = (got_1, got_2)[s - 1][which].at[p, d - 1]
                    if s == stage:
                        copies.append(remote(source, target, sems, p, slot, k, d))
                    slot += 1
        if stage == 3:
            for d in range(1, size["z"]):
                copies.append(remote(total_3.at[slot_now, :, d], got_z.at[p, d - 1], sems, p, slot + d - 1, "z", d))
        return copies

    def own_copy():
        return pltpu.make_async_copy(shard_ref, full_ref.at[(slice(None),) + tuple(here[k] for k in NAMES)], own_sem)

    def load_copy(p):
        return pltpu.make_async_copy(
            full_ref.at[:, :, :, :, :, :, columns(p)], weights.at[lax.rem(p, 2)], load_sem.at[lax.rem(p, 2)]
        )

    def on(offset, run):
        p = step - offset

        @pl.when((p >= 0) & (p < parts))
        def _():
            run(p)

    def begin(p):
        for copy in gather_copies(p, 0):
            copy.start()

    @pl.when(step == 0)
    def _():
        own_copy().start()
        pltpu.make_async_copy(start_ref, y_ref, start_sem).start()
        greet()

        for p in range(FIRST_PARTS):
            begin(jnp.int32(p))
        own_copy().wait()
        pltpu.make_async_copy(start_ref, y_ref, start_sem).wait()
        b_ref[...] = jnp.zeros_like(b_ref)

    def pass_on(stage):
        def run(p):
            for copy in gather_copies(p, stage - 1):
                copy.wait_recv()
            for copy in gather_copies(p, stage):
                copy.start()

        return run

    def arrived(p):
        for copy in gather_copies(p, 3):
            copy.wait_recv()
        load_copy(p).start()

    @pl.when((step > 0) & (step + FIRST_PARTS - 1 < parts))
    def _():
        begin(step + FIRST_PARTS - 1)

    on(3 * SLACK, arrived)
    on(2 * SLACK, pass_on(3))
    on(SLACK, pass_on(2))
    on(0, pass_on(1))

    def finish(p):
        for copy in scatter_copies(p, 3):
            copy.wait()
        total = total_3[lax.rem(p, 2), :, 0].astype(F32)
        for d in range(1, size["z"]):
            total = total + got_z[p, d - 1].astype(F32)
        for which in range(2):
            sum_ref[:, pl.ds(pl.multiple_of(which * parts * width + p * width, width), width)] = total[which]

    def third(p):
        for copy in scatter_copies(p, 2):
            copy.wait()
        for which, order in enumerate(orders):
            total = total_2[which][lax.rem(p, 2), 0].astype(F32)
            for d in range(1, size[order[1]]):
                total = total + got_2[which][p, d - 1].astype(F32)
            total_3[lax.rem(p, 2), which] = total.astype(BF16)
        for copy in scatter_copies(p, 3):
            copy.start()

    def second(p):
        for copy in scatter_copies(p, 1):
            copy.wait()
        for which, order in enumerate(orders):
            kept = total_1[lax.rem(p, 2), 0, 0] if order[0] == "x" else total_1[lax.rem(p, 2), 1, :, 0]
            total = kept.astype(F32)
            for d in range(1, size[order[0]]):
                total = total + got_1[which][p, d - 1].astype(F32)
            total_2[which][lax.rem(p, 2)] = total.astype(BF16)
        for copy in scatter_copies(p, 2):
            copy.start()

    def first(p):
        for copy in scatter_copies(p, 0):
            copy.wait()
        total = terms[lax.rem(p, TERM_SLOTS), :, 0].astype(F32) + got_c[p].astype(F32)
        total_1[lax.rem(p, 2)] = total.astype(BF16)
        for copy in scatter_copies(p, 1):
            copy.start()

    on(FEED_LEAD + 4 * SLACK, finish)
    on(FEED_LEAD + 3 * SLACK, third)
    on(FEED_LEAD + 2 * SLACK, second)
    on(FEED_LEAD + SLACK, first)

    def compute(p):
        load_copy(p).wait()
        slot = lax.rem(p, 2)
        rows = D
        a, g, wd = a_ref[...], g_ref[...], wd_ref[...]
        wg = weights[slot, 0].reshape(rows, width)
        wu = weights[slot, 1].reshape(rows, width)
        gate = dot(a, wg)
        up = dot(a, wu)
        d_hidden = dot_cols(g, wd)
        sigma = 1.0 / (1.0 + jnp.exp(-gate))
        swish = gate * sigma
        hidden = (swish * up).astype(BF16)
        d_gate = (d_hidden * up * sigma * (1.0 + gate * (1.0 - sigma))).astype(BF16)
        d_up = (d_hidden * swish).astype(BF16)
        y_ref[...] += dot(hidden, wd)
        b_ref[...] += dot_cols(d_gate, wg) + dot_cols(d_up, wu)
        at = at_ref[...]
        shape = (2,) + total_1.shape[2:]
        slot = lax.rem(p, TERM_SLOTS)
        terms[slot, 0] = dot(at, d_gate).astype(BF16).reshape(shape)
        terms[slot, 1] = dot(at, d_up).astype(BF16).reshape(shape)
        gd_ref[...] = dot_rows(hidden, g).astype(BF16)
        for copy in scatter_copies(p, 0):
            copy.start()

    on(FEED_LEAD, compute)

    @pl.when(step == pl.num_programs(0) - 1)
    def _():
        def end(p, _):
            for stage in range(4):
                for copy in gather_copies(p, stage):
                    copy.wait_send()
            return 0

        lax.fori_loop(0, parts, end, 0)


def feed(shards, a, at, g, w_down, start, number):
    rows = a.shape[0]
    size = {k: v[2] for k, v in dims().items()}
    _, shard_rows, width = shards.shape
    parts = width // FF_BLOCK
    x, y, z = size["x"], size["y"], size["z"]
    last = (z, shard_rows, FF_BLOCK)
    whole = pl.BlockSpec(memory_space=pltpu.VMEM)
    anywhere = pl.BlockSpec(memory_space=pl.ANY)
    row = pl.BlockSpec((FF_BLOCK, D), lambda t: (jnp.clip(t - FEED_LEAD, 0, parts - 1), 0))
    out_count = z - 1 + 2 * (x + y - 2) + 1
    in_count = 1 + 2 * (x + y - 2) + z - 1
    sems = pltpu.SemaphoreType.DMA
    _, y_sum, b_sum, grad_down, sums = pl.pallas_call(
        feed_kernel,
        name="feed",
        grid=(parts + FEED_LEAD + 4 * SLACK,),
        in_specs=[anywhere, whole, whole, whole, anywhere, row],
        out_specs=[anywhere, whole, whole, row, whole],
        out_shape=[
            jax.ShapeDtypeStruct((2, *(size[k] for k in NAMES), shard_rows, width), BF16),
            jax.ShapeDtypeStruct((rows, D), F32),
            jax.ShapeDtypeStruct((rows, D), F32),
            jax.ShapeDtypeStruct((width, D), BF16),
            jax.ShapeDtypeStruct((shard_rows, 2 * width), F32),
        ],
        scratch_shapes=[
            pltpu.VMEM((2, 2, *(size[k] for k in NAMES), shard_rows, FF_BLOCK), BF16),
            pltpu.VMEM((TERM_SLOTS, 2, 2, x, y, *last), BF16),
            pltpu.VMEM((2, 2, x, y, *last), BF16),
            [pltpu.VMEM((2, y, *last), BF16), pltpu.VMEM((2, x, *last), BF16)],
            pltpu.VMEM((2, 2, *last), BF16),
            pltpu.VMEM((parts, 2, x, y, *last), BF16),
            [pltpu.VMEM((parts, x - 1, y, *last), BF16), pltpu.VMEM((parts, y - 1, x, *last), BF16)],
            [pltpu.VMEM((parts, y - 1, *last), BF16), pltpu.VMEM((parts, x - 1, *last), BF16)],
            pltpu.VMEM((parts, z - 1, 2, shard_rows, FF_BLOCK), BF16),
            sems((2,)),
            sems,
            sems,
            sems((parts, out_count)),
            sems((parts, out_count)),
            sems((parts, in_count)),
            sems((parts, in_count)),
        ],
        compiler_params=pltpu.CompilerParams(
            collective_id=number, has_side_effects=True, vmem_limit_bytes=60 << 20
        ),
        cost_estimate=pl.CostEstimate(
            flops=18 * rows * D * width, transcendentals=rows * width, bytes_accessed=12 * D * width
        ),
    )(shards, a, at, g, start, w_down)
    return y_sum, b_sum, grad_down, sums


OUT_PARTS = 2
EXIT_PARTS = OUT_PARTS + 4


def exit_kernel(
    raw_ref,
    dq_ref,
    near_ref,
    w_ref,
    attn_ref,
    *rest,
):
    back_refs, rest = rest[:2], rest[2:]
    run_leave(back_refs, raw_ref, dq_ref, near_ref, w_ref, attn_ref, *rest)


def run_leave(
    back_refs,
    raw_ref,
    dq_ref,
    near_ref,
    w_ref,
    attn_ref,
    mixed_ref,
    at_ref,
    gain_ref,
    cos_ref,
    sin_ref,
    x_ref,
    norm_ref,
    second_ref,
    grad_ref,
    sum_ref,
    gains_ref,
    part_ref,
    first_ref,
    head_ref,
    terms,
    total_1,
    total_2,
    total_3,
    got_c,
    got_1,
    got_2,
    got_z,
    gains_got,
    in_send,
    in_recv,
    gain_send,
    gain_recv,
):
    step = pl.program_id(0)
    width = terms.shape[-1]
    parts = EXIT_PARTS
    size = {k: v[2] for k, v in dims().items()}
    here = {k: place_along(k) for k in NAMES}
    orders = ("xy", "yx")
    rows = x_ref.shape[0]

    def columns(p):
        return pl.ds(pl.multiple_of(p * width, width), width)

    def remote(source, target, p, n, k, d):
        return pltpu.make_async_remote_copy(
            source,
            target,
            in_send.at[p, n],
            in_recv.at[p, n],
            device_id=neighbour(k, d),
            device_id_type=MESH,
        )

    def scatter_copies(p, stage):
        if stage == 0:
            return [remote(terms.at[lax.rem(p, 3), :, 1], got_c.at[p], p, 0, "c", 1)]
        copies = []
        slot = 1
        for which, order in enumerate(orders):
            for s in (1, 2):
                k = order[s - 1]
                for d in range(1, size[k]):
                    if s == 1:
                        source = total_1.at[0, d] if k == "x" else total_1.at[1, :, d]
                    else:
                        source = total_2[which].at[d]
                    if s == stage:
                        target = (got_1, got_2)[s - 1][which].at[p, d - 1]
                        copies.append(remote(source, target, p, slot, k, d))
                    slot += 1
        if stage == 3:
            for d in range(1, size["z"]):
                copies.append(remote(total_3.at[:, d], got_z.at[p, d - 1], p, slot + d - 1, "z", d))
        return copies

    def on(offset, run):
        p = step - offset

        @pl.when((p >= 0) & (p < parts))
        def _():
            run(p)

    def finish(p):
        for copy in scatter_copies(p, 3):
            copy.wait()
        total = total_3[:, 0].astype(F32)
        for d in range(1, size["z"]):
            total = total + got_z[p, d - 1].astype(F32)
        for which in range(2):
            sum_ref[:, pl.ds(pl.multiple_of((2 * p + which) * width, width), width)] = total[which]

    def third(p):
        for copy in scatter_copies(p, 2):
            copy.wait()
        for which, order in enumerate(orders):
            total = total_2[which][0].astype(F32)
            for d in range(1, size[order[1]]):
                total = total + got_2[which][p, d - 1].astype(F32)
            total_3[which] = total.astype(BF16)
        for copy in scatter_copies(p, 3):
            copy.start()

    def second(p):
        for copy in scatter_copies(p, 1):
            copy.wait()
        for which, order in enumerate(orders):
            kept = total_1[0, 0] if order[0] == "x" else total_1[1, :, 0]
            total = kept.astype(F32)
            for d in range(1, size[order[0]]):
                total = total + got_1[which][p, d - 1].astype(F32)
            total_2[which][...] = total.astype(BF16)
        for copy in scatter_copies(p, 2):
            copy.start()

    def first(p):
        for copy in scatter_copies(p, 0):
            copy.wait()
        total = terms[lax.rem(p, 3), :, 0].astype(F32) + got_c[p].astype(F32)
        total_1[...] = total.astype(BF16)
        for copy in scatter_copies(p, 1):
            copy.start()

    @pl.when(step == 0)
    def _():
        greet()
        first_ref[...] = jnp.zeros_like(first_ref)
        head_ref[...] = jnp.zeros_like(head_ref)

    on(5, finish)
    on(4, third)
    on(3, second)
    on(2, first)

    block = 256

    def back(half, j, rows_at):
        at = (2 * half + j % 2) * LANES
        return back_refs[j // 2][rows_at, at : at + LANES].astype(F32)

    def turn_back(which, scale):
        def some(i, sums):
            at = pl.ds(pl.multiple_of(i * block, block), block)
            cosine, sine = cos_ref[at, :], sin_ref[at, :]
            for j in range(4):
                part = slice(j * LANES, (j + 1) * LANES)
                u = raw_ref[at, part]
                if which == 0:
                    d = dq_ref[at, part]
                else:
                    d = near_ref[at, part] + back(0, j, at)
                d = (d * cosine - swap_halves(d) * sine) * scale
                r = lax.rsqrt(head_mean(u * u) + NORM_EPS)
                w = d * gain_ref[which : which + 1]
                n = u * r
                part_ref[at, part] = (r * (w - n * head_mean(w * n))).astype(BF16)
                sums = sums + jnp.sum(d * n, axis=0, keepdims=True)
            return sums

        sums = lax.fori_loop(0, rows // block, some, jnp.zeros((1, LANES), F32))
        head_ref[which : which + 1] += sums

    @pl.when((step >= OUT_PARTS) & (step < OUT_PARTS + 2))
    def _():
        turn_back(0, HEAD_SIZE**-0.5)

    @pl.when(step == OUT_PARTS + 2)
    def _():
        turn_back(1, 1.0)

    @pl.when(step == OUT_PARTS + 3)
    def _():
        for j in range(4):
            part = slice(j * LANES, (j + 1) * LANES)
            part_ref[:, part] = (near_ref[:, part] + back(1, j, slice(None))).astype(BF16)

    def compute(p):
        shape = (2,) + total_1.shape[1:]
        slot = lax.rem(p, 3)

        @pl.when(p < OUT_PARTS)
        def _():
            for half in range(2):
                some = attn_ref[:, half * width : (half + 1) * width]
                terms[slot, half] = dot(mixed_ref[...], some).astype(BF16).reshape(shape)

        @pl.when(p >= OUT_PARTS)
        def _():
            first_ref[...] += dot_cols(part_ref[...], w_ref[...])
            for half in range(2):
                some = part_ref[:, half * width : (half + 1) * width]
                terms[slot, half] = dot(at_ref[...], some).astype(BF16).reshape(shape)

        for copy in scatter_copies(p, 0):
            copy.start()

    on(0, compute)

    @pl.when(step == parts - 1)
    def _():
        gain = norm_ref[0:1]

        def some(i, sums):
            at = pl.ds(pl.multiple_of(i * block, block), block)
            v = x_ref[at, :].astype(F32)
            scale = lax.rsqrt(jnp.mean(v * v, axis=-1, keepdims=True) + NORM_EPS)
            d = first_ref[at, :]
            n = v * scale
            w = d * gain
            mean = jnp.mean(w * n, axis=-1, keepdims=True)
            grad_ref[at, :] = (scale * (w - n * mean)).astype(BF16)
            return sums + jnp.sum(d * n, axis=0, keepdims=True)

        sums = lax.fori_loop(0, rows // block, some, jnp.zeros((1, D), F32))
        gains_ref[...] = jnp.zeros_like(gains_ref)
        gains_ref[0:1] = sums
        gains_ref[1:2] = second_ref[0:1]
        gains_ref[2:4, :LANES] = head_ref[0:2]

    stage = 0
    for k in NAMES:
        d = 1
        while d < size[k]:

            @pl.when(step == parts + stage // 2)
            def _(k=k, d=d, stage=stage):
                copy = pltpu.make_async_remote_copy(
                    gains_ref,
                    gains_got.at[stage],
                    gain_send.at[stage],
                    gain_recv.at[stage],
                    device_id=neighbour(k, d),
                    device_id_type=MESH,
                )
                copy.start()
                copy.wait()
                gains_ref[...] += gains_got[stage]

            d *= 2
            stage += 1


def leave(raw, dq, near, back, w, d_attn, mixed_rows, at, gains, cosine, sine, x, norm_gains, second, number):
    rows = x.shape[0]
    size = {k: v[2] for k, v in dims().items()}
    xs, ys, zs = size["x"], size["y"], size["z"]
    width = 256
    shard_rows = D // math.prod(size.values())
    last = (zs, shard_rows, width)
    parts = EXIT_PARTS
    whole = pl.BlockSpec(memory_space=pltpu.VMEM)
    block = lambda size, start, count: pl.BlockSpec(
        (size, 2 * width), lambda t: (0, jnp.clip(t - start, 0, count - 1))
    )
    in_count = 1 + 2 * (xs + ys - 2) + zs - 1
    stages = sum(v.bit_length() - 1 for v in size.values())
    sems = pltpu.SemaphoreType.DMA
    return pl.pallas_call(
        exit_kernel,
        name="leave",
        grid=(parts + 5,),
        in_specs=[
            block(rows, OUT_PARTS, 4),
            block(rows, OUT_PARTS, 2),
            block(rows, OUT_PARTS + 2, 2),
            block(D, OUT_PARTS, 4),
            block(rows, 0, 2),
        ]
        + [whole] * 10,
        out_specs=[whole] * 3,
        out_shape=[
            jax.ShapeDtypeStruct((rows, D), BF16),
            jax.ShapeDtypeStruct((shard_rows, 2 * parts * width), F32),
            jax.ShapeDtypeStruct((8, D), F32),
        ],
        scratch_shapes=[
            pltpu.VMEM((rows, 2 * width), BF16),
            pltpu.VMEM((rows, D), F32),
            pltpu.VMEM((8, LANES), F32),
            pltpu.VMEM((3, 2, 2, xs, ys, *last), BF16),
            pltpu.VMEM((2, xs, ys, *last), BF16),
            [pltpu.VMEM((ys, *last), BF16), pltpu.VMEM((xs, *last), BF16)],
            pltpu.VMEM((2, *last), BF16),
            pltpu.VMEM((parts, 2, xs, ys, *last), BF16),
            [pltpu.VMEM((parts, xs - 1, ys, *last), BF16), pltpu.VMEM((parts, ys - 1, xs, *last), BF16)],
            [pltpu.VMEM((parts, ys - 1, *last), BF16), pltpu.VMEM((parts, xs - 1, *last), BF16)],
            pltpu.VMEM((parts, zs - 1, 2, shard_rows, width), BF16),
            pltpu.VMEM((stages, 8, D), F32),
            sems((parts, in_count)),
            sems((parts, in_count)),
            sems((stages,)),
            sems((stages,)),
        ],
        compiler_params=pltpu.CompilerParams(
            collective_id=number, has_side_effects=True, vmem_limit_bytes=56 << 20
        ),
        cost_estimate=pl.CostEstimate(flops=rows << 20, transcendentals=0, bytes_accessed=rows << 10),
    )(raw, dq, near, w, d_attn, *back, mixed_rows, at, gains, cosine, sine, x, norm_gains, second)


def add_swapped(keep, send, direction):
    return (keep.astype(F32) + swap(send, direction, 1).astype(F32)).astype(BF16)


def add_along(terms, direction, last=False):
    size = dims()[direction][2]
    step = terms.shape[0] // size
    total = terms[:step].astype(F32)
    for d in range(1, size):
        total = total + swap(terms[d * step : (d + 1) * step], direction, d).astype(F32)
    return total if last else total.astype(BF16)


def own_part(terms, direction, last=False):
    at, here, size = NAMES.index(direction), place_along(direction), dims()[direction][2]
    total = lax.dynamic_slice_in_dim(terms, here, 1, at).astype(F32)
    for d in range(1, size):
        sent = lax.dynamic_slice_in_dim(terms, jnp.bitwise_xor(here, d), 1, at)
        total = total + swap(sent, direction, d).astype(F32)
    return total if last else total.astype(BF16)


def per_device(
    inputs,
    cotangent,
    lengths,
    norm_gains,
    norm_first,
    norm_second,
    qk_gains,
    qk_first,
    qk_second,
    qkv_master,
    qkv_first,
    qkv_second,
    out_master,
    out_first,
    out_second,
    gate_up_master,
    gate_up_first,
    gate_up_second,
    down_master,
    down_first,
    down_second,
):
    seq_width = lax.axis_size("seq")
    turn_here = lax.axis_index("seq")
    rows = inputs.shape[1]
    block = QUERY_BLOCK
    w_qkv, w_out = gather_all([qkv_master.astype(BF16), out_master.astype(BF16)], 512, 1)

    places = turn_here * rows + jnp.arange(rows, dtype=jnp.int32)
    row_lengths = lengths[0]
    doc_ends = jnp.cumsum(row_lengths)
    passed = doc_ends[None, :] <= places[:, None]
    begins = jnp.sum(jnp.where(passed, row_lengths[None, :], 0), axis=1)
    cosine, sine = rotation_tables(places - begins)
    if seq_width == 2:
        base = (turn_here - 1) * rows
    else:
        base = turn_here * 0
    first = (begins - base).astype(jnp.int32)
    low = jnp.concatenate([(turn_here * rows - base)[None], first[::block]]).astype(jnp.int32)
    first_wide = jnp.broadcast_to(first[:, None], (rows, LANES))
    first_lane = jnp.broadcast_to(first[None, :], (8, rows))

    x = inputs[0].astype(F32)
    scale_first = rms_scale(x)
    normed_first = (x * scale_first * norm_gains[0]).astype(BF16)
    raw = jnp.dot(normed_first, w_qkv, preferred_element_type=F32)
    gain_rows = jnp.pad(jnp.tile(qk_gains, (1, 2)), ((0, 6), (0, 0)))
    q, *own = prep(raw, gain_rows, cosine, sine)
    if seq_width == 2:
        others = [lax.ppermute(p, "seq", [(0, 1)]) for p in own]
    else:
        others = [lax.all_gather(p, "seq", axis=0, tiled=True) for p in own]
    w_down = gather(after(down_master.astype(BF16), others[3]))
    hot_x = relative_rows("cxyz", D)
    first_rows = transpose_in_order(hot_x, normed_first)
    q = after(q, first_rows)
    mixed, lse = attend(q, others, own, low, first_wide)
    x_mid = x + jnp.dot(mixed, w_out, preferred_element_type=F32)
    scale_second = rms_scale(x_mid)
    normed_second = (x_mid * scale_second * norm_gains[1]).astype(BF16)
    g = cotangent[0]
    shards = jnp.stack([gate_up_master[:, :FF], gate_up_master[:, FF:]]).astype(BF16)
    out_sum, d_b, grad_down, gate_up_sums = feed(
        after(shards, normed_second),
        normed_second,
        transpose_in_order(hot_x, normed_second),
        g,
        w_down,
        x_mid,
        2,
    )
    outputs = out_sum.astype(BF16)
    down_grad = lax.psum_scatter(grad_down, ALL, scatter_dimension=0, tiled=True).astype(F32)
    d_norm, d_gain_second = rms_back(x_mid, scale_second, norm_gains[1], d_b)
    d_mid = g.astype(F32) + d_norm
    d_attn = d_mid.astype(BF16)
    d_mixed = dot_cols(d_attn, w_out).astype(BF16)
    far, back = [], []
    for pieces in ((0, 1), (2, 3)):
        far.append(attend_back(0, pieces, q, d_mixed, mixed, lse, [], others, low, first_lane, BF16))
        d_keys = far[-1][1]
        if seq_width == 2:
            back.append(lax.ppermute(d_keys, "seq", [(1, 0)]))
        else:
            back.append(lax.psum_scatter(d_keys, "seq", scatter_dimension=0, tiled=True))
    befores = [dq for dq, _ in far]
    dq, near = attend_back(
        others[0].shape[0], range(4), q, d_mixed, mixed, lse, befores, own, low, first_lane, F32
    )
    d_x, sums, gain_sums = leave(
        raw,
        dq,
        near,
        back,
        w_qkv,
        d_attn,
        transpose_in_order(hot_x, after(mixed, befores)),
        first_rows,
        gain_rows,
        cosine,
        sine,
        inputs[0],
        jnp.pad(norm_gains, ((0, 6), (0, 0))),
        jnp.broadcast_to(d_gain_second[None], (8, D)),
        3,
    )
    input_grad = (d_mid + d_x.astype(F32))[None]
    out_grad, qkv_grad = sums[:, :D], sums[:, D:]
    norm_grad = gain_sums[:2]
    qk_grad = gain_sums[2:4, :HEAD_SIZE] + gain_sums[2:4, HEAD_SIZE:LANES]

    norm_new = adam_update(norm_gains, norm_first, norm_second, norm_grad, GAIN_RATE, 0.0)
    qk_new = adam_update(qk_gains, qk_first, qk_second, qk_grad, GAIN_RATE, 0.0)
    qkv_new = adam_update(qkv_master, qkv_first, qkv_second, qkv_grad, D**-0.5, DECAY_RATE)
    out_new = adam_update(
        out_master, out_first, out_second, out_grad, (QUERY_FEATURES // 16) ** -0.5, DECAY_RATE
    )
    gate_new = adam_update(
        gate_up_master, gate_up_first, gate_up_second, gate_up_sums, D**-0.5, DECAY_RATE
    )
    down_new = adam_update(down_master, down_first, down_second, down_grad, FF**-0.5, DECAY_RATE)
    return (
        outputs[None],
        input_grad,
        *norm_new,
        *qk_new,
        *qkv_new,
        *out_new,
        *gate_new,
        *down_new,
    )


def solution(mesh):
    token = P("fsdp", "seq", None)
    weight = P(ALL, None)
    return jax.shard_map(
        per_device,
        mesh=mesh,
        in_specs=(token, token, P("fsdp", None)) + (P(),) * 6 + (weight,) * 12,
        out_specs=(token, token) + (P(),) * 6 + (weight,) * 12,
        check_vma=False,
    )
```

```python
import functools
import math

import jax
import jax.numpy as jnp
from jax import lax
from jax.experimental import pallas as pl
from jax.experimental.pallas import tpu as pltpu
from jax.sharding import PartitionSpec as P

D = 1024
HQ = 16
KEY_VALUE_HEADS = 8
HEAD_SIZE = 64
FF = 4608
QUERY_FEATURES = 1024
KEY_FEATURES = 512
STEP = 10
LANES = 128

NORM_EPS = 1e-05
ROPE_BASE = 1000000.0
BETA_ONE = 0.9
BETA_TWO = 0.95
ADAM_EPS = 1e-08
DECAY_RATE = 0.1
GAIN_RATE = 0.3

F32 = jnp.float32
BF16 = jnp.bfloat16
QUERY_BLOCK = 128
KEY_BLOCK = 256
FF_BLOCK = 256
PIECES = 4


def dot(a, b):
    return lax.dot_general(a, b, (((1,), (0,)), ((), ())), preferred_element_type=F32)


def dot_cols(a, b):
    return lax.dot_general(a, b, (((1,), (1,)), ((), ())), preferred_element_type=F32)


def dot_rows(a, b):
    return lax.dot_general(a, b, (((0,), (0,)), ((), ())), preferred_element_type=F32)


def params(limit=56):
    return pltpu.CompilerParams(vmem_limit_bytes=limit << 20)


def head_mean(v):
    row = lax.broadcasted_iota(jnp.int32, (LANES, LANES), 0) // HEAD_SIZE
    col = lax.broadcasted_iota(jnp.int32, (LANES, LANES), 1) // HEAD_SIZE
    ones = jnp.where(row == col, 1.0 / HEAD_SIZE, 0.0).astype(BF16)
    high = v.astype(BF16)
    low = (v - high.astype(F32)).astype(BF16)
    return dot(high, ones) + dot(low, ones)


def swap_halves(v):
    lane = lax.broadcasted_iota(jnp.int32, v.shape, 1) % HEAD_SIZE
    return jnp.where(
        lane < HEAD_SIZE // 2,
        pltpu.roll(v, LANES - HEAD_SIZE // 2, 1),
        pltpu.roll(v, HEAD_SIZE // 2, 1),
    )


def prep_kernel(raw_ref, gain_ref, cos_ref, sin_ref, q_ref, *kv_refs):
    cosine, sine = cos_ref[...], sin_ref[...]
    for group in range(12):
        part = slice(group * LANES, (group + 1) * LANES)
        u = raw_ref[:, part]
        gain = gain_ref[0:1] if group < 8 else gain_ref[1:2]
        n = u * lax.rsqrt(head_mean(u * u) + NORM_EPS) * gain
        out = n * cosine + swap_halves(n) * sine
        if group < 8:
            q_ref[:, part] = (out * HEAD_SIZE**-0.5).astype(BF16)
        else:
            kv_ref = kv_refs[group - 8]
            kv_ref[:, :LANES] = out.astype(BF16)
            value = raw_ref[:, slice((group + 4) * LANES, (group + 5) * LANES)]
            kv_ref[:, LANES:] = value.astype(BF16)


def prep(raw, gains, cosine, sine):
    rows = raw.shape[0]
    block = min(rows, 256)
    whole = lambda width: pl.BlockSpec((block, width), lambda i: (i, 0))
    return pl.pallas_call(
        prep_kernel,
        name="prep",
        grid=(rows // block,),
        in_specs=[whole(2048), pl.BlockSpec((8, LANES), lambda i: (0, 0)), whole(LANES), whole(LANES)],
        out_specs=[whole(QUERY_FEATURES)] + [whole(2 * LANES)] * PIECES,
        out_shape=[jax.ShapeDtypeStruct((rows, QUERY_FEATURES), BF16)]
        + [jax.ShapeDtypeStruct((rows, 2 * LANES), BF16)] * PIECES,
        compiler_params=params(),
        cost_estimate=pl.CostEstimate(
            flops=rows * 2048 * 40, transcendentals=rows * 24, bytes_accessed=rows * 2048 * 6
        ),
    )(raw, gains, cosine, sine)


def stack_heads(rows):
    first, second = rows[:, :LANES].astype(F32), rows[:, LANES:].astype(F32)
    lane = lax.broadcasted_iota(jnp.int32, first.shape, 1)
    low = lane < HEAD_SIZE
    turn = lambda v: pltpu.roll(v, HEAD_SIZE, 1)
    heads = [
        jnp.where(low, first, 0.0),
        jnp.where(low, turn(first), 0.0),
        jnp.where(low, 0.0, turn(second)),
        jnp.where(low, 0.0, second),
    ]
    return jnp.concatenate(heads, axis=0).astype(BF16)


def unstack_heads(tall):
    n = tall.shape[0] // 4
    a, b, c, d = (tall[i * n : (i + 1) * n] for i in range(4))
    low = lax.broadcasted_iota(jnp.int32, a.shape, 1) < HEAD_SIZE
    turn = lambda v: pltpu.roll(v, HEAD_SIZE, 1)
    return jnp.concatenate([jnp.where(low, a, turn(b)), jnp.where(low, turn(c), d)], axis=1)


def key_range(low_ref, turn, block, start, rows):
    begin = low_ref[1 + turn] // KEY_BLOCK
    end = (low_ref[0] + turn * block + block - 1) // KEY_BLOCK + 1
    first, last = start // KEY_BLOCK, (start + rows) // KEY_BLOCK
    return jnp.clip(begin, first, last), jnp.clip(end, first, last)


def attend_kernel(start, last, low_ref, first_ref, q_ref, *rest):
    befores, rest = (rest[:2], rest[2:]) if last else ((), rest)
    refs = rest[:PIECES]
    first_out, second_out, queries, totals = rest[PIECES:]
    turn = pl.program_id(0)
    block = q_ref.shape[0]
    rows = refs[0].shape[0]
    begin, end = key_range(low_ref, turn, block, start, rows)
    totals[...] = jnp.zeros_like(totals)

    @pl.when(end > begin)
    def _():
        for p in range(PIECES):
            queries[p] = stack_heads(q_ref[:, p * 2 * LANES : (p + 1) * 2 * LANES])
        place = low_ref[0] + turn * block + lax.broadcasted_iota(jnp.int32, (block, KEY_BLOCK), 0)
        first = jnp.concatenate([first_ref[...]] * (KEY_BLOCK // LANES), axis=1)
        column = lax.broadcasted_iota(jnp.int32, (block, KEY_BLOCK), 1)
        ones = jnp.ones((KEY_BLOCK, LANES), BF16)

        def step(at, _):
            span = pl.ds(pl.multiple_of(at * KEY_BLOCK - start, KEY_BLOCK), KEY_BLOCK)
            key_place = at * KEY_BLOCK + column
            allowed = (key_place >= first) & (key_place <= place)
            for p in range(PIECES):
                scores = dot_cols(queries[p], refs[p][span, :LANES])
                scores = scores.reshape(4, block, KEY_BLOCK)
                powers = jnp.where(allowed[None], jnp.exp(scores), 0.0).astype(BF16)
                values = jnp.concatenate([refs[p][span, LANES:], ones], axis=1)
                totals[p] += dot(powers.reshape(4 * block, KEY_BLOCK), values)
            return 0

        lax.fori_loop(begin, end, step, 0)

    for p in range(PIECES):
        part = slice(p * 2 * LANES, (p + 1) * 2 * LANES)
        mixed = unstack_heads(totals[p, :, :LANES])
        mass = unstack_heads(totals[p, :, LANES:])
        if not last:
            first_out[:, part] = mixed
            second_out[:, part] = mass
            continue
        mixed = mixed + befores[0][:, part]
        mass = mass + befores[1][:, part]
        first_out[:, part] = (mixed / mass).astype(BF16)
        logs = jnp.transpose(jnp.log(mass))
        heads = [logs[i * HEAD_SIZE : i * HEAD_SIZE + 8] for i in range(4)]
        second_out[:, p * 4 * block : (p + 1) * 4 * block] = jnp.concatenate(heads, axis=1)


def attend(start, q, befores, source, low, first):
    rows = q.shape[0]
    block = QUERY_BLOCK
    turns = rows // block
    last = len(befores) > 0
    wide = pl.BlockSpec((block, QUERY_FEATURES), lambda t, low: (t, 0))
    if last:
        second = pl.BlockSpec((8, HQ * block), lambda t, low: (t, 0))
        shapes = [
            jax.ShapeDtypeStruct((rows, QUERY_FEATURES), BF16),
            jax.ShapeDtypeStruct((8 * turns, HQ * block), F32),
        ]
    else:
        second = wide
        shapes = [jax.ShapeDtypeStruct((rows, QUERY_FEATURES), F32)] * 2
    return pl.pallas_call(
        functools.partial(attend_kernel, start, last),
        name="attend",
        grid_spec=pltpu.PrefetchScalarGridSpec(
            num_scalar_prefetch=1,
            grid=(turns,),
            in_specs=[pl.BlockSpec((block, LANES), lambda t, low: (t, 0)), wide]
            + [wide] * len(befores)
            + [pl.BlockSpec((source[0].shape[0], 2 * LANES), lambda t, low: (0, 0))] * PIECES,
            out_specs=[wide, second],
            scratch_shapes=[
                pltpu.VMEM((PIECES, 4 * block, LANES), BF16),
                pltpu.VMEM((PIECES, 4 * block, 2 * LANES), F32),
            ],
        ),
        out_shape=shapes,
        compiler_params=params(),
        cost_estimate=pl.CostEstimate(
            flops=rows * 1024 * 1024 * 12, transcendentals=rows * 1024 * 8, bytes_accessed=16 << 20
        ),
    )(low, first, q, *befores, *source)


def attend_back_kernel(
    start, pieces, count, low_ref, first_ref, q_ref, do_ref, mixed_ref, lse_ref, *rest
):
    befores, refs = rest[:count], rest[count : count + len(pieces)]
    d_ref, dq_ref, queries, rising, deltas, dqs, dkvs = rest[count + len(pieces) :]
    turn = pl.program_id(0)
    block = q_ref.shape[0]
    rows = refs[0].shape[0]
    tall = 4 * block

    @pl.when(turn == 0)
    def _():
        dkvs[...] = jnp.zeros_like(dkvs)

    begin, end = key_range(low_ref, turn, block, start, rows)

    @pl.when(end <= begin)
    def _():
        if befores:
            dq_ref[...] = jnp.concatenate([ref[...] for ref in befores], axis=1)
        else:
            dq_ref[...] = jnp.zeros_like(dq_ref)

    @pl.when(end > begin)
    def _():
        for p, piece in enumerate(pieces):
            part = slice(piece * 2 * LANES, (piece + 1) * 2 * LANES)
            queries[p] = stack_heads(q_ref[:, part])
            rising[p] = stack_heads(do_ref[:, part])
            across = jnp.transpose(do_ref[:, part].astype(F32) * mixed_ref[:, part].astype(F32))
            deltas[p] = jnp.concatenate(
                [
                    jnp.broadcast_to(
                        jnp.sum(across[i * HEAD_SIZE : (i + 1) * HEAD_SIZE], axis=0, keepdims=True),
                        (8, block),
                    )
                    for i in range(4)
                ],
                axis=1,
            )
        dqs[...] = jnp.zeros_like(dqs)
        shape = (KEY_BLOCK, block)
        place = low_ref[0] + turn * block + lax.broadcasted_iota(jnp.int32, shape, 1)
        row = lax.broadcasted_iota(jnp.int32, shape, 0)
        first = first_ref[0:1]

        def step(at, _):
            span = pl.ds(pl.multiple_of(at * KEY_BLOCK - start, KEY_BLOCK), KEY_BLOCK)
            key_place = at * KEY_BLOCK + row
            allowed = (key_place >= first) & (key_place <= place)
            allowed = jnp.concatenate([allowed] * 4, axis=1)
            for p, piece in enumerate(pieces):
                key, value = refs[p][span, :LANES], refs[p][span, LANES:]
                logs = lse_ref[0:1, piece * tall : (piece + 1) * tall]
                probs = jnp.where(allowed, jnp.exp(dot_cols(key, queries[p]) - logs), 0.0)
                dprobs = dot_cols(value, rising[p])
                dscores = (probs * (dprobs - deltas[p, 0:1])).astype(BF16)
                dkvs[p, span, :LANES] += dot(dscores, queries[p])
                dkvs[p, span, LANES:] += dot(probs.astype(BF16), rising[p])
                dqs[p] += dot_rows(dscores, key)
            return 0

        lax.fori_loop(begin, end, step, 0)
        for p in range(len(pieces)):
            part = slice(p * 2 * LANES, (p + 1) * 2 * LANES)
            total = unstack_heads(dqs[p])
            if befores:
                each = len(pieces) // count
                at = p % each * 2 * LANES
                total = total + befores[p // each][:, at : at + 2 * LANES]
            dq_ref[:, part] = total

    @pl.when(turn == pl.num_programs(0) - 1)
    def _():
        for p in range(len(pieces)):
            for half in range(2):
                at = (half * len(pieces) + p) * LANES
                part = slice(at, at + LANES)
                d_ref[:, part] = dkvs[p, :, half * LANES : (half + 1) * LANES].astype(d_ref.dtype)


def attend_back(start, pieces, q, d_mixed, mixed, lse, befores, source, low, first_lane, kind):
    rows = q.shape[0]
    block = QUERY_BLOCK
    turns = rows // block
    count = source[0].shape[0]
    some = len(pieces)
    whole = pl.BlockSpec((count, some * 2 * LANES), lambda t, low: (0, 0))
    part = lambda width: pl.BlockSpec((block, width), lambda t, low: (t, 0))
    wide = pl.BlockSpec((block, QUERY_FEATURES), lambda t, low: (t, 0))
    d_keys, dq = pl.pallas_call(
        functools.partial(attend_back_kernel, start, pieces, len(befores)),
        name="attend_back",
        grid_spec=pltpu.PrefetchScalarGridSpec(
            num_scalar_prefetch=1,
            grid=(turns,),
            in_specs=[
                pl.BlockSpec((8, block), lambda t, low: (0, t)),
                wide,
                wide,
                wide,
                pl.BlockSpec((8, HQ * block), lambda t, low: (t, 0)),
            ]
            + [part(v.shape[1]) for v in befores]
            + [pl.BlockSpec((count, 2 * LANES), lambda t, low: (0, 0))] * some,
            out_specs=[whole, part(some * 2 * LANES)],
            scratch_shapes=[
                pltpu.VMEM((some, 4 * block, LANES), BF16),
                pltpu.VMEM((some, 4 * block, LANES), BF16),
                pltpu.VMEM((some, 8, 4 * block), F32),
                pltpu.VMEM((some, 4 * block, LANES), F32),
                pltpu.VMEM((some, count, 2 * LANES), F32),
            ],
        ),
        out_shape=[
            jax.ShapeDtypeStruct((count, some * 2 * LANES), kind),
            jax.ShapeDtypeStruct((rows, some * 2 * LANES), F32),
        ],
        compiler_params=params(),
        cost_estimate=pl.CostEstimate(
            flops=rows << 18, transcendentals=0, bytes_accessed=rows << 8
        ),
    )(low, first_lane, q, d_mixed, mixed, lse, *befores, *[source[p] for p in pieces])
    return dq, d_keys


def rms_scale(v):
    return lax.rsqrt(jnp.mean(v * v, axis=-1, keepdims=True) + NORM_EPS)


def rms_back(v, scale, gain_row, d_out):
    w = d_out * gain_row
    n = v * scale
    d_v = scale * (w - n * jnp.mean(w * n, axis=-1, keepdims=True))
    return d_v, jnp.sum(d_out * n, axis=0)


def adam_update(master, first_moment, second_moment, gradient, rate, decay):
    first_moment = BETA_ONE * first_moment + (1.0 - BETA_ONE) * gradient
    second_moment = BETA_TWO * second_moment + (1.0 - BETA_TWO) * gradient * gradient
    corrected = (
        first_moment
        / (1.0 - BETA_ONE**STEP)
        / (jnp.sqrt(second_moment / (1.0 - BETA_TWO**STEP)) + ADAM_EPS)
    )
    return (master - rate * (corrected + decay * master), first_moment, second_moment)


def rotation_tables(position):
    half = HEAD_SIZE // 2
    index_row = jnp.arange(half, dtype=F32)
    frequency = jnp.exp(index_row * (-2.0 * math.log(ROPE_BASE) / HEAD_SIZE))
    angles = position.astype(F32)[:, None] * frequency[None, :]
    cosine, sine = jnp.cos(angles), jnp.sin(angles)
    return (
        jnp.concatenate([cosine] * 4, axis=1),
        jnp.concatenate([-sine, sine, -sine, sine], axis=1),
    )


ALL = ("fsdp", "seq")


def gather(shard):
    return lax.all_gather(shard, ALL, axis=0, tiled=True)


def dims():
    rest = lax.axis_size("fsdp") // 8
    return {
        "z": ("fsdp", 2 * rest, 4),
        "y": ("fsdp", 2, rest),
        "c": ("fsdp", 1, 2),
        "x": ("seq", 1, lax.axis_size("seq")),
    }


def place_along(direction):
    axis, stride, size = dims()[direction]
    return lax.rem(lax.div(lax.axis_index(axis), stride), size)


def swap(value, direction, distance):
    axis, stride, _ = dims()[direction]
    pairs = [(i, i ^ (distance * stride)) for i in range(lax.axis_size(axis))]
    return lax.ppermute(value, axis, pairs)


def relative_rows(order, count):
    sizes = {k: v[2] for k, v in dims().items()}
    width = count
    for size in sizes.values():
        width //= size
    index = jnp.arange(count, dtype=jnp.int32)
    left = index // width
    place = {}
    for k in reversed(order):
        place[k] = jnp.bitwise_xor(left % sizes[k], place_along(k))
        left = left // sizes[k]
    block = jnp.zeros_like(index)
    for k in "zycx":
        block = block * sizes[k] + place[k]
    row = block * width + index % width
    return (row[:, None] == index[None, :]).astype(BF16)


def transpose_in_order(hot, value):
    return dot_cols(hot, value).astype(BF16)


MESH = pl.DeviceIdType.MESH
NAMES = "zycx"


def neighbour(direction, distance):
    axis, stride, _ = dims()[direction]
    here = place_along(direction)
    return {axis: lax.axis_index(axis) + (jnp.bitwise_xor(here, distance) - here) * stride}


def greet():
    barrier = pltpu.get_barrier_semaphore()
    count = 0
    for k in NAMES:
        for d in range(1, dims()[k][2]):
            pl.semaphore_signal(barrier, 1, device_id=neighbour(k, d), device_id_type=MESH)
            count += 1
    pl.semaphore_wait(barrier, count)


def part_view(full, at, columns):
    index = tuple(at[k] if k in at else slice(None) for k in NAMES)
    return full.at[index + (slice(None), columns)]


def gather_kernel(plan, *refs):
    count = 1 + max(p[0] for p in plan)
    shards, fulls = refs[:count], refs[count : 2 * count]
    local, send, recv = refs[2 * count :]
    here = {k: place_along(k) for k in NAMES}
    own = []
    for t in range(count):
        copy = pltpu.make_async_copy(shards[t], part_view(fulls[t], here, slice(None)), local.at[t])
        copy.start()
        own.append(copy)
    greet()
    posted = []

    def post(source, target, k, d):
        n = len(posted)
        copy = pltpu.make_async_remote_copy(
            source, target, send.at[n], recv.at[n], device_id=neighbour(k, d), device_id_type=MESH
        )
        copy.start()
        posted.append(copy)
        return copy

    coming = {}
    for when in range(len(plan) + 3):
        for step in range(4):
            p = when - step
            if not 0 <= p < len(plan):
                continue
            t, column, width, order = plan[p]
            columns = pl.ds(column, width)
            full = fulls[t]
            if step == 0:
                k = order[0]
                target = part_view(full, here, columns)
                coming[p, 0] = [
                    post(shards[t].at[:, columns], target, k, d) for d in range(1, dims()[k][2])
                ]
                continue
            if own[t] is not None:
                own[t].wait()
                own[t] = None
            for copy in coming[p, step - 1]:
                copy.wait_recv()
            at = {k: v for k, v in here.items() if k not in order[:step]}
            if step < 3:
                k = order[step]
                view = part_view(full, at, columns)
                coming[p, step] = [post(view, view, k, d) for d in range(1, dims()[k][2])]
                if step == 2:
                    coming[p, 3] = [post(view, view, "c", 1)]
            else:
                k = order[2]
                for d in range(1, dims()[k][2]):
                    view = part_view(full, {**at, k: jnp.bitwise_xor(here[k], d)}, columns)
                    coming[p, 3].append(post(view, view, "c", 1))
    for p in range(len(plan)):
        for copy in coming[p, 3]:
            copy.wait_recv()
    for copy in posted:
        copy.wait_send()


def plan_parts(arrays, cut):
    plan = []
    for t, shard in enumerate(arrays):
        pieces = max(1, shard.shape[1] // cut)
        width = shard.shape[1] // pieces
        for i in range(pieces):
            plan.append((t, i * width, width, "zxy" if len(plan) % 2 else "zyx"))
    return plan


def gather_all(shards, cut, number):
    plan = plan_parts(shards, cut)
    size = {k: dims()[k][2] for k in NAMES}
    total = sum(sum(size[k] - 1 for k in order) + size[order[2]] for _, _, _, order in plan)
    fulls = pl.pallas_call(
        functools.partial(gather_kernel, plan),
        name="gather_all",
        in_specs=[pl.BlockSpec(memory_space=pl.ANY)] * len(shards),
        out_specs=[pl.BlockSpec(memory_space=pl.ANY)] * len(shards),
        out_shape=[
            jax.ShapeDtypeStruct((*(size[k] for k in NAMES), *shard.shape), shard.dtype)
            for shard in shards
        ],
        scratch_shapes=[
            pltpu.SemaphoreType.DMA((len(shards),)),
            pltpu.SemaphoreType.DMA((total,)),
            pltpu.SemaphoreType.DMA((total,)),
        ],
        compiler_params=pltpu.CompilerParams(collective_id=number, has_side_effects=True),
    )(*shards)
    return [full.reshape(-1, full.shape[-1]) for full in fulls]


def after(values, earlier):
    return lax.optimization_barrier((values, earlier))[0]


FIRST_PARTS = 6
SLACK = 2
TERM_SLOTS = SLACK + 1
FEED_LEAD = 3 * SLACK + 1


def feed_kernel(
    shard_ref,
    a_ref,
    at_ref,
    g_ref,
    start_ref,
    wd_ref,
    full_ref,
    y_ref,
    b_ref,
    gd_ref,
    sum_ref,
    weights,
    terms,
    total_1,
    total_2,
    total_3,
    got_c,
    got_1,
    got_2,
    got_z,
    load_sem,
    start_sem,
    own_sem,
    out_send,
    out_recv,
    in_send,
    in_recv,
):
    step = pl.program_id(0)
    width = weights.shape[-1]
    parts = shard_ref.shape[2] // width
    size = {k: v[2] for k, v in dims().items()}
    here = {k: place_along(k) for k in NAMES}
    shard_rows = shard_ref.shape[1]
    orders = ("xy", "yx")

    def columns(p):
        return pl.ds(pl.multiple_of(p * width, width), width)

    def view(which, at, p):
        index = tuple(at[k] if k in at else slice(None) for k in NAMES)
        return full_ref.at[(which,) + index + (slice(None), columns(p))]

    def remote(source, target, sems, p, n, k, d):
        send, recv = sems
        return pltpu.make_async_remote_copy(
            source,
            target,
            send.at[p, n],
            recv.at[p, n],
            device_id=neighbour(k, d),
            device_id_type=MESH,
        )

    def gather_copies(p, stage):
        sems = (out_send, out_recv)
        copies = []
        if stage == 0:
            for d in range(1, size["z"]):
                copies.append(
                    remote(shard_ref.at[:, :, columns(p)], view(slice(None), here, p), sems, p, d - 1, "z", d)
                )
            return copies
        slot = size["z"] - 1
        if stage == 3:
            slot += 2 * (size["x"] + size["y"] - 2)
            at = view(slice(None), {"c": here["c"]}, p)
            return [remote(at, at, sems, p, slot, "c", 1)]
        for which, order in enumerate(orders):
            for s in (1, 2):
                k = order[s - 1]
                gone = "z" + order[: s - 1]
                at = view(which, {q: v for q, v in here.items() if q not in gone}, p)
                for d in range(1, size[k]):
                    if s == stage:
                        copies.append(remote(at, at, sems, p, slot, k, d))
                    slot += 1
        return copies

    def scatter_copies(p, stage):
        sems = (in_send, in_recv)
        if stage == 0:
            return [remote(terms.at[lax.rem(p, TERM_SLOTS), :, 1], got_c.at[p], sems, p, 0, "c", 1)]
        copies = []
        slot, slot_now = 1, lax.rem(p, 2)
        for which, order in enumerate(orders):
            for s in (1, 2):
                k = order[s - 1]
                for d in range(1, size[k]):
                    if s == 1:
                        source = total_1.at[slot_now, 0, d] if k == "x" else total_1.at[slot_now, 1, :, d]
                    else:
                        source = total_2[which].at[slot_now, d]
                    target = (got_1, got_2)[s - 1][which].at[p, d - 1]
                    if s == stage:
                        copies.append(remote(source, target, sems, p, slot, k, d))
                    slot += 1
        if stage == 3:
            for d in range(1, size["z"]):
                copies.append(remote(total_3.at[slot_now, :, d], got_z.at[p, d - 1], sems, p, slot + d - 1, "z", d))
        return copies

    def own_copy():
        return pltpu.make_async_copy(shard_ref, full_ref.at[(slice(None),) + tuple(here[k] for k in NAMES)], own_sem)

    def load_copy(p):
        return pltpu.make_async_copy(
            full_ref.at[:, :, :, :, :, :, columns(p)], weights.at[lax.rem(p, 2)], load_sem.at[lax.rem(p, 2)]
        )

    def on(offset, run):
        p = step - offset

        @pl.when((p >= 0) & (p < parts))
        def _():
            run(p)

    def begin(p):
        for copy in gather_copies(p, 0):
            copy.start()

    @pl.when(step == 0)
    def _():
        own_copy().start()
        pltpu.make_async_copy(start_ref, y_ref, start_sem).start()
        greet()

        for p in range(FIRST_PARTS):
            begin(jnp.int32(p))
        own_copy().wait()
        pltpu.make_async_copy(start_ref, y_ref, start_sem).wait()
        b_ref[...] = jnp.zeros_like(b_ref)

    def pass_on(stage):
        def run(p):
            for copy in gather_copies(p, stage - 1):
                copy.wait_recv()
            for copy in gather_copies(p, stage):
                copy.start()

        return run

    def arrived(p):
        for copy in gather_copies(p, 3):
            copy.wait_recv()
        load_copy(p).start()

    @pl.when((step > 0) & (step + FIRST_PARTS - 1 < parts))
    def _():
        begin(step + FIRST_PARTS - 1)

    on(3 * SLACK, arrived)
    on(2 * SLACK, pass_on(3))
    on(SLACK, pass_on(2))
    on(0, pass_on(1))

    def finish(p):
        for copy in scatter_copies(p, 3):
            copy.wait()
        total = total_3[lax.rem(p, 2), :, 0].astype(F32)
        for d in range(1, size["z"]):
            total = total + got_z[p, d - 1].astype(F32)
        for which in range(2):
            sum_ref[:, pl.ds(pl.multiple_of(which * parts * width + p * width, width), width)] = total[which]

    def third(p):
        for copy in scatter_copies(p, 2):
            copy.wait()
        for which, order in enumerate(orders):
            total = total_2[which][lax.rem(p, 2), 0].astype(F32)
            for d in range(1, size[order[1]]):
                total = total + got_2[which][p, d - 1].astype(F32)
            total_3[lax.rem(p, 2), which] = total.astype(BF16)
        for copy in scatter_copies(p, 3):
            copy.start()

    def second(p):
        for copy in scatter_copies(p, 1):
            copy.wait()
        for which, order in enumerate(orders):
            kept = total_1[lax.rem(p, 2), 0, 0] if order[0] == "x" else total_1[lax.rem(p, 2), 1, :, 0]
            total = kept.astype(F32)
            for d in range(1, size[order[0]]):
                total = total + got_1[which][p, d - 1].astype(F32)
            total_2[which][lax.rem(p, 2)] = total.astype(BF16)
        for copy in scatter_copies(p, 2):
            copy.start()

    def first(p):
        for copy in scatter_copies(p, 0):
            copy.wait()
        total = terms[lax.rem(p, TERM_SLOTS), :, 0].astype(F32) + got_c[p].astype(F32)
        total_1[lax.rem(p, 2)] = total.astype(BF16)
        for copy in scatter_copies(p, 1):
            copy.start()

    on(FEED_LEAD + 4 * SLACK, finish)
    on(FEED_LEAD + 3 * SLACK, third)
    on(FEED_LEAD + 2 * SLACK, second)
    on(FEED_LEAD + SLACK, first)

    def compute(p):
        load_copy(p).wait()
        slot = lax.rem(p, 2)
        rows = D
        a, g, wd = a_ref[...], g_ref[...], wd_ref[...]
        wg = weights[slot, 0].reshape(rows, width)
        wu = weights[slot, 1].reshape(rows, width)
        gate = dot(a, wg)
        up = dot(a, wu)
        d_hidden = dot_cols(g, wd)
        sigma = 1.0 / (1.0 + jnp.exp(-gate))
        swish = gate * sigma
        hidden = (swish * up).astype(BF16)
        d_gate = (d_hidden * up * sigma * (1.0 + gate * (1.0 - sigma))).astype(BF16)
        d_up = (d_hidden * swish).astype(BF16)
        y_ref[...] += dot(hidden, wd)
        b_ref[...] += dot_cols(d_gate, wg) + dot_cols(d_up, wu)
        at = at_ref[...]
        shape = (2,) + total_1.shape[2:]
        slot = lax.rem(p, TERM_SLOTS)
        terms[slot, 0] = dot(at, d_gate).astype(BF16).reshape(shape)
        terms[slot, 1] = dot(at, d_up).astype(BF16).reshape(shape)
        gd_ref[...] = dot_rows(hidden, g).astype(BF16)
        for copy in scatter_copies(p, 0):
            copy.start()

    on(FEED_LEAD, compute)

    @pl.when(step == pl.num_programs(0) - 1)
    def _():
        def end(p, _):
            for stage in range(4):
                for copy in gather_copies(p, stage):
                    copy.wait_send()
            return 0

        lax.fori_loop(0, parts, end, 0)


def feed(shards, a, at, g, w_down, start, number):
    rows = a.shape[0]
    size = {k: v[2] for k, v in dims().items()}
    _, shard_rows, width = shards.shape
    parts = width // FF_BLOCK
    x, y, z = size["x"], size["y"], size["z"]
    last = (z, shard_rows, FF_BLOCK)
    whole = pl.BlockSpec(memory_space=pltpu.VMEM)
    anywhere = pl.BlockSpec(memory_space=pl.ANY)
    row = pl.BlockSpec((FF_BLOCK, D), lambda t: (jnp.clip(t - FEED_LEAD, 0, parts - 1), 0))
    out_count = z - 1 + 2 * (x + y - 2) + 1
    in_count = 1 + 2 * (x + y - 2) + z - 1
    sems = pltpu.SemaphoreType.DMA
    _, y_sum, b_sum, grad_down, sums = pl.pallas_call(
        feed_kernel,
        name="feed",
        grid=(parts + FEED_LEAD + 4 * SLACK,),
        in_specs=[anywhere, whole, whole, whole, anywhere, row],
        out_specs=[anywhere, whole, whole, row, whole],
        out_shape=[
            jax.ShapeDtypeStruct((2, *(size[k] for k in NAMES), shard_rows, width), BF16),
            jax.ShapeDtypeStruct((rows, D), F32),
            jax.ShapeDtypeStruct((rows, D), F32),
            jax.ShapeDtypeStruct((width, D), BF16),
            jax.ShapeDtypeStruct((shard_rows, 2 * width), F32),
        ],
        scratch_shapes=[
            pltpu.VMEM((2, 2, *(size[k] for k in NAMES), shard_rows, FF_BLOCK), BF16),
            pltpu.VMEM((TERM_SLOTS, 2, 2, x, y, *last), BF16),
            pltpu.VMEM((2, 2, x, y, *last), BF16),
            [pltpu.VMEM((2, y, *last), BF16), pltpu.VMEM((2, x, *last), BF16)],
            pltpu.VMEM((2, 2, *last), BF16),
            pltpu.VMEM((parts, 2, x, y, *last), BF16),
            [pltpu.VMEM((parts, x - 1, y, *last), BF16), pltpu.VMEM((parts, y - 1, x, *last), BF16)],
            [pltpu.VMEM((parts, y - 1, *last), BF16), pltpu.VMEM((parts, x - 1, *last), BF16)],
            pltpu.VMEM((parts, z - 1, 2, shard_rows, FF_BLOCK), BF16),
            sems((2,)),
            sems,
            sems,
            sems((parts, out_count)),
            sems((parts, out_count)),
            sems((parts, in_count)),
            sems((parts, in_count)),
        ],
        compiler_params=pltpu.CompilerParams(
            collective_id=number, has_side_effects=True, vmem_limit_bytes=60 << 20
        ),
        cost_estimate=pl.CostEstimate(
            flops=18 * rows * D * width, transcendentals=rows * width, bytes_accessed=12 * D * width
        ),
    )(shards, a, at, g, start, w_down)
    return y_sum, b_sum, grad_down, sums


OUT_PARTS = 2
EXIT_PARTS = OUT_PARTS + 4


def exit_kernel(
    raw_ref,
    dq_ref,
    near_ref,
    w_ref,
    attn_ref,
    *rest,
):
    back_refs, rest = rest[:2], rest[2:]
    run_leave(back_refs, raw_ref, dq_ref, near_ref, w_ref, attn_ref, *rest)


def run_leave(
    back_refs,
    raw_ref,
    dq_ref,
    near_ref,
    w_ref,
    attn_ref,
    mixed_ref,
    at_ref,
    gain_ref,
    cos_ref,
    sin_ref,
    x_ref,
    norm_ref,
    second_ref,
    grad_ref,
    sum_ref,
    gains_ref,
    part_ref,
    first_ref,
    head_ref,
    terms,
    total_1,
    total_2,
    total_3,
    got_c,
    got_1,
    got_2,
    got_z,
    gains_got,
    in_send,
    in_recv,
    gain_send,
    gain_recv,
):
    step = pl.program_id(0)
    width = terms.shape[-1]
    parts = EXIT_PARTS
    size = {k: v[2] for k, v in dims().items()}
    here = {k: place_along(k) for k in NAMES}
    orders = ("xy", "yx")
    rows = x_ref.shape[0]

    def columns(p):
        return pl.ds(pl.multiple_of(p * width, width), width)

    def remote(source, target, p, n, k, d):
        return pltpu.make_async_remote_copy(
            source,
            target,
            in_send.at[p, n],
            in_recv.at[p, n],
            device_id=neighbour(k, d),
            device_id_type=MESH,
        )

    def scatter_copies(p, stage):
        if stage == 0:
            return [remote(terms.at[lax.rem(p, 3), :, 1], got_c.at[p], p, 0, "c", 1)]
        copies = []
        slot = 1
        for which, order in enumerate(orders):
            for s in (1, 2):
                k = order[s - 1]
                for d in range(1, size[k]):
                    if s == 1:
                        source = total_1.at[0, d] if k == "x" else total_1.at[1, :, d]
                    else:
                        source = total_2[which].at[d]
                    if s == stage:
                        target = (got_1, got_2)[s - 1][which].at[p, d - 1]
                        copies.append(remote(source, target, p, slot, k, d))
                    slot += 1
        if stage == 3:
            for d in range(1, size["z"]):
                copies.append(remote(total_3.at[:, d], got_z.at[p, d - 1], p, slot + d - 1, "z", d))
        return copies

    def on(offset, run):
        p = step - offset

        @pl.when((p >= 0) & (p < parts))
        def _():
            run(p)

    def finish(p):
        for copy in scatter_copies(p, 3):
            copy.wait()
        total = total_3[:, 0].astype(F32)
        for d in range(1, size["z"]):
            total = total + got_z[p, d - 1].astype(F32)
        for which in range(2):
            sum_ref[:, pl.ds(pl.multiple_of((2 * p + which) * width, width), width)] = total[which]

    def third(p):
        for copy in scatter_copies(p, 2):
            copy.wait()
        for which, order in enumerate(orders):
            total = total_2[which][0].astype(F32)
            for d in range(1, size[order[1]]):
                total = total + got_2[which][p, d - 1].astype(F32)
            total_3[which] = total.astype(BF16)
        for copy in scatter_copies(p, 3):
            copy.start()

    def second(p):
        for copy in scatter_copies(p, 1):
            copy.wait()
        for which, order in enumerate(orders):
            kept = total_1[0, 0] if order[0] == "x" else total_1[1, :, 0]
            total = kept.astype(F32)
            for d in range(1, size[order[0]]):
                total = total + got_1[which][p, d - 1].astype(F32)
            total_2[which][...] = total.astype(BF16)
        for copy in scatter_copies(p, 2):
            copy.start()

    def first(p):
        for copy in scatter_copies(p, 0):
            copy.wait()
        total = terms[lax.rem(p, 3), :, 0].astype(F32) + got_c[p].astype(F32)
        total_1[...] = total.astype(BF16)
        for copy in scatter_copies(p, 1):
            copy.start()

    @pl.when(step == 0)
    def _():
        greet()
        first_ref[...] = jnp.zeros_like(first_ref)
        head_ref[...] = jnp.zeros_like(head_ref)

    on(5, finish)
    on(4, third)
    on(3, second)
    on(2, first)

    block = 256

    def back(half, j, rows_at):
        at = (2 * half + j % 2) * LANES
        return back_refs[j // 2][rows_at, at : at + LANES].astype(F32)

    def turn_back(which, scale):
        def some(i, sums):
            at = pl.ds(pl.multiple_of(i * block, block), block)
            cosine, sine = cos_ref[at, :], sin_ref[at, :]
            for j in range(4):
                part = slice(j * LANES, (j + 1) * LANES)
                u = raw_ref[at, part]
                if which == 0:
                    d = dq_ref[at, part]
                else:
                    d = near_ref[at, part] + back(0, j, at)
                d = (d * cosine - swap_halves(d) * sine) * scale
                r = lax.rsqrt(head_mean(u * u) + NORM_EPS)
                w = d * gain_ref[which : which + 1]
                n = u * r
                part_ref[at, part] = (r * (w - n * head_mean(w * n))).astype(BF16)
                sums = sums + jnp.sum(d * n, axis=0, keepdims=True)
            return sums

        sums = lax.fori_loop(0, rows // block, some, jnp.zeros((1, LANES), F32))
        head_ref[which : which + 1] += sums

    @pl.when((step >= OUT_PARTS) & (step < OUT_PARTS + 2))
    def _():
        turn_back(0, HEAD_SIZE**-0.5)

    @pl.when(step == OUT_PARTS + 2)
    def _():
        turn_back(1, 1.0)

    @pl.when(step == OUT_PARTS + 3)
    def _():
        for j in range(4):
            part = slice(j * LANES, (j + 1) * LANES)
            part_ref[:, part] = (near_ref[:, part] + back(1, j, slice(None))).astype(BF16)

    def compute(p):
        shape = (2,) + total_1.shape[1:]
        slot = lax.rem(p, 3)

        @pl.when(p < OUT_PARTS)
        def _():
            for half in range(2):
                some = attn_ref[:, half * width : (half + 1) * width]
                terms[slot, half] = dot(mixed_ref[...], some).astype(BF16).reshape(shape)

        @pl.when(p >= OUT_PARTS)
        def _():
            first_ref[...] += dot_cols(part_ref[...], w_ref[...])
            for half in range(2):
                some = part_ref[:, half * width : (half + 1) * width]
                terms[slot, half] = dot(at_ref[...], some).astype(BF16).reshape(shape)

        for copy in scatter_copies(p, 0):
            copy.start()

    on(0, compute)

    @pl.when(step == parts - 1)
    def _():
        gain = norm_ref[0:1]

        def some(i, sums):
            at = pl.ds(pl.multiple_of(i * block, block), block)
            v = x_ref[at, :].astype(F32)
            scale = lax.rsqrt(jnp.mean(v * v, axis=-1, keepdims=True) + NORM_EPS)
            d = first_ref[at, :]
            n = v * scale
            w = d * gain
            mean = jnp.mean(w * n, axis=-1, keepdims=True)
            grad_ref[at, :] = (scale * (w - n * mean)).astype(BF16)
            return sums + jnp.sum(d * n, axis=0, keepdims=True)

        sums = lax.fori_loop(0, rows // block, some, jnp.zeros((1, D), F32))
        gains_ref[...] = jnp.zeros_like(gains_ref)
        gains_ref[0:1] = sums
        gains_ref[1:2] = second_ref[0:1]
        gains_ref[2:4, :LANES] = head_ref[0:2]

    stage = 0
    for k in NAMES:
        d = 1
        while d < size[k]:

            @pl.when(step == parts + stage // 2)
            def _(k=k, d=d, stage=stage):
                copy = pltpu.make_async_remote_copy(
                    gains_ref,
                    gains_got.at[stage],
                    gain_send.at[stage],
                    gain_recv.at[stage],
                    device_id=neighbour(k, d),
                    device_id_type=MESH,
                )
                copy.start()
                copy.wait()
                gains_ref[...] += gains_got[stage]

            d *= 2
            stage += 1


def leave(raw, dq, near, back, w, d_attn, mixed_rows, at, gains, cosine, sine, x, norm_gains, second, number):
    rows = x.shape[0]
    size = {k: v[2] for k, v in dims().items()}
    xs, ys, zs = size["x"], size["y"], size["z"]
    width = 256
    shard_rows = D // math.prod(size.values())
    last = (zs, shard_rows, width)
    parts = EXIT_PARTS
    whole = pl.BlockSpec(memory_space=pltpu.VMEM)
    block = lambda size, start, count: pl.BlockSpec(
        (size, 2 * width), lambda t: (0, jnp.clip(t - start, 0, count - 1))
    )
    in_count = 1 + 2 * (xs + ys - 2) + zs - 1
    stages = sum(v.bit_length() - 1 for v in size.values())
    sems = pltpu.SemaphoreType.DMA
    return pl.pallas_call(
        exit_kernel,
        name="leave",
        grid=(parts + 5,),
        in_specs=[
            block(rows, OUT_PARTS, 4),
            block(rows, OUT_PARTS, 2),
            block(rows, OUT_PARTS + 2, 2),
            block(D, OUT_PARTS, 4),
            block(rows, 0, 2),
        ]
        + [whole] * 10,
        out_specs=[whole] * 3,
        out_shape=[
            jax.ShapeDtypeStruct((rows, D), BF16),
            jax.ShapeDtypeStruct((shard_rows, 2 * parts * width), F32),
            jax.ShapeDtypeStruct((8, D), F32),
        ],
        scratch_shapes=[
            pltpu.VMEM((rows, 2 * width), BF16),
            pltpu.VMEM((rows, D), F32),
            pltpu.VMEM((8, LANES), F32),
            pltpu.VMEM((3, 2, 2, xs, ys, *last), BF16),
            pltpu.VMEM((2, xs, ys, *last), BF16),
            [pltpu.VMEM((ys, *last), BF16), pltpu.VMEM((xs, *last), BF16)],
            pltpu.VMEM((2, *last), BF16),
            pltpu.VMEM((parts, 2, xs, ys, *last), BF16),
            [pltpu.VMEM((parts, xs - 1, ys, *last), BF16), pltpu.VMEM((parts, ys - 1, xs, *last), BF16)],
            [pltpu.VMEM((parts, ys - 1, *last), BF16), pltpu.VMEM((parts, xs - 1, *last), BF16)],
            pltpu.VMEM((parts, zs - 1, 2, shard_rows, width), BF16),
            pltpu.VMEM((stages, 8, D), F32),
            sems((parts, in_count)),
            sems((parts, in_count)),
            sems((stages,)),
            sems((stages,)),
        ],
        compiler_params=pltpu.CompilerParams(
            collective_id=number, has_side_effects=True, vmem_limit_bytes=56 << 20
        ),
        cost_estimate=pl.CostEstimate(flops=rows << 20, transcendentals=0, bytes_accessed=rows << 10),
    )(raw, dq, near, w, d_attn, *back, mixed_rows, at, gains, cosine, sine, x, norm_gains, second)


def add_swapped(keep, send, direction):
    return (keep.astype(F32) + swap(send, direction, 1).astype(F32)).astype(BF16)


def add_along(terms, direction, last=False):
    size = dims()[direction][2]
    step = terms.shape[0] // size
    total = terms[:step].astype(F32)
    for d in range(1, size):
        total = total + swap(terms[d * step : (d + 1) * step], direction, d).astype(F32)
    return total if last else total.astype(BF16)


def own_part(terms, direction, last=False):
    at, here, size = NAMES.index(direction), place_along(direction), dims()[direction][2]
    total = lax.dynamic_slice_in_dim(terms, here, 1, at).astype(F32)
    for d in range(1, size):
        sent = lax.dynamic_slice_in_dim(terms, jnp.bitwise_xor(here, d), 1, at)
        total = total + swap(sent, direction, d).astype(F32)
    return total if last else total.astype(BF16)


def per_device(
    inputs,
    cotangent,
    lengths,
    norm_gains,
    norm_first,
    norm_second,
    qk_gains,
    qk_first,
    qk_second,
    qkv_master,
    qkv_first,
    qkv_second,
    out_master,
    out_first,
    out_second,
    gate_up_master,
    gate_up_first,
    gate_up_second,
    down_master,
    down_first,
    down_second,
):
    seq_width = lax.axis_size("seq")
    turn_here = lax.axis_index("seq")
    rows = inputs.shape[1]
    block = QUERY_BLOCK
    w_qkv, w_out = gather_all([qkv_master.astype(BF16), out_master.astype(BF16)], 512, 1)

    places = turn_here * rows + jnp.arange(rows, dtype=jnp.int32)
    row_lengths = lengths[0]
    doc_ends = jnp.cumsum(row_lengths)
    passed = doc_ends[None, :] <= places[:, None]
    begins = jnp.sum(jnp.where(passed, row_lengths[None, :], 0), axis=1)
    cosine, sine = rotation_tables(places - begins)
    if seq_width == 2:
        base = (turn_here - 1) * rows
    else:
        base = turn_here * 0
    first = (begins - base).astype(jnp.int32)
    low = jnp.concatenate([(turn_here * rows - base)[None], first[::block]]).astype(jnp.int32)
    first_wide = jnp.broadcast_to(first[:, None], (rows, LANES))
    first_lane = jnp.broadcast_to(first[None, :], (8, rows))

    x = inputs[0].astype(F32)
    scale_first = rms_scale(x)
    normed_first = (x * scale_first * norm_gains[0]).astype(BF16)
    raw = jnp.dot(normed_first, w_qkv, preferred_element_type=F32)
    w_down = gather(after(down_master.astype(BF16), raw))
    gain_rows = jnp.pad(jnp.tile(qk_gains, (1, 2)), ((0, 6), (0, 0)))
    q, *own = prep(raw, gain_rows, cosine, sine)
    if seq_width == 2:
        others = [lax.ppermute(p, "seq", [(0, 1)]) for p in own]
    else:
        others = [lax.all_gather(p, "seq", axis=0, tiled=True) for p in own]
    hot_x = relative_rows("cxyz", D)
    first_rows = transpose_in_order(hot_x, normed_first)
    q = after(q, first_rows)
    sums = attend(others[0].shape[0], q, [], own, low, first_wide)
    mixed, lse = attend(0, q, sums, others, low, first_wide)
    x_mid = x + jnp.dot(mixed, w_out, preferred_element_type=F32)
    scale_second = rms_scale(x_mid)
    normed_second = (x_mid * scale_second * norm_gains[1]).astype(BF16)
    g = cotangent[0]
    shards = jnp.stack([gate_up_master[:, :FF], gate_up_master[:, FF:]]).astype(BF16)
    out_sum, d_b, grad_down, gate_up_sums = feed(
        after(shards, normed_second),
        normed_second,
        transpose_in_order(hot_x, normed_second),
        g,
        w_down,
        x_mid,
        2,
    )
    outputs = out_sum.astype(BF16)
    down_grad = lax.psum_scatter(grad_down, ALL, scatter_dimension=0, tiled=True).astype(F32)
    d_norm, d_gain_second = rms_back(x_mid, scale_second, norm_gains[1], d_b)
    d_mid = g.astype(F32) + d_norm
    d_attn = d_mid.astype(BF16)
    d_mixed = dot_cols(d_attn, w_out).astype(BF16)
    far, back = [], []
    for pieces in ((0, 1), (2, 3)):
        far.append(attend_back(0, pieces, q, d_mixed, mixed, lse, [], others, low, first_lane, BF16))
        d_keys = far[-1][1]
        if seq_width == 2:
            back.append(lax.ppermute(d_keys, "seq", [(1, 0)]))
        else:
            back.append(lax.psum_scatter(d_keys, "seq", scatter_dimension=0, tiled=True))
    befores = [dq for dq, _ in far]
    dq, near = attend_back(
        others[0].shape[0], range(4), q, d_mixed, mixed, lse, befores, own, low, first_lane, F32
    )
    d_x, sums, gain_sums = leave(
        raw,
        dq,
        near,
        back,
        w_qkv,
        d_attn,
        transpose_in_order(hot_x, after(mixed, befores)),
        first_rows,
        gain_rows,
        cosine,
        sine,
        inputs[0],
        jnp.pad(norm_gains, ((0, 6), (0, 0))),
        jnp.broadcast_to(d_gain_second[None], (8, D)),
        3,
    )
    input_grad = (d_mid + d_x.astype(F32))[None]
    out_grad, qkv_grad = sums[:, :D], sums[:, D:]
    norm_grad = gain_sums[:2]
    qk_grad = gain_sums[2:4, :HEAD_SIZE] + gain_sums[2:4, HEAD_SIZE:LANES]

    norm_new = adam_update(norm_gains, norm_first, norm_second, norm_grad, GAIN_RATE, 0.0)
    qk_new = adam_update(qk_gains, qk_first, qk_second, qk_grad, GAIN_RATE, 0.0)
    qkv_new = adam_update(qkv_master, qkv_first, qkv_second, qkv_grad, D**-0.5, DECAY_RATE)
    out_new = adam_update(
        out_master, out_first, out_second, out_grad, (QUERY_FEATURES // 16) ** -0.5, DECAY_RATE
    )
    gate_new = adam_update(
        gate_up_master, gate_up_first, gate_up_second, gate_up_sums, D**-0.5, DECAY_RATE
    )
    down_new = adam_update(down_master, down_first, down_second, down_grad, FF**-0.5, DECAY_RATE)
    return (
        outputs[None],
        input_grad,
        *norm_new,
        *qk_new,
        *qkv_new,
        *out_new,
        *gate_new,
        *down_new,
    )


def solution(mesh):
    token = P("fsdp", "seq", None)
    weight = P(ALL, None)
    return jax.shard_map(
        per_device,
        mesh=mesh,
        in_specs=(token, token, P("fsdp", None)) + (P(),) * 6 + (weight,) * 12,
        out_specs=(token, token) + (P(),) * 6 + (weight,) * 12,
        check_vma=False,
    )
```
